32 devices in a mesh: dp: 8 (over y, x, core), tensor: 4 (over z).
Axes of the slice: x: 2, y: 2, z: 4, core: 2. Of those that a mesh axis runs over, the one named last changes fastest.
Arguments:
- inputs: bfloat16 [16384, 768], P('dp'), may hold values from -6 to 6
- cotangent: bfloat16 [16384, 768], P('dp'), may hold values from -6 to 6
- counts: int32 [32], P('dp'), may hold values from 40 to 512, as said below
- keep_mask: int32 [16384], P('dp'), may hold values 0 or 1
- box_x: int32 [16384], P('dp'), may hold values from 0 to 63
- box_y: int32 [16384], P('dp'), may hold values from 0 to 63
- gain_one: float32 [768], replicated, may hold values from 0.5 to 1.5
- shift_one: float32 [768], replicated, may hold values from -4 to 4
- w_qkv: bfloat16 [3, 768, 768], P(None, None, 'tensor'), may hold values from -0.21875 to 0.21875
- b_qv: float32 [2, 768], P(None, 'tensor'), may hold values from -4 to 4
- w_out: bfloat16 [768, 768], P('tensor'), may hold values from -0.875 to 0.875
- b_out: float32 [768], replicated, may hold values from -4 to 4
- gain_two: float32 [768], replicated, may hold values from 0.5 to 1.5
- shift_two: float32 [768], replicated, may hold values from -4 to 4
- w_up: bfloat16 [768, 3072], P(None, 'tensor'), may hold values from -0.21875 to 0.21875
- b_up: float32 [3072], P('tensor'), may hold values from -4 to 4
- w_down: bfloat16 [3072, 768], P('tensor'), may hold values from -0.109375 to 0.109375
- b_down: float32 [768], replicated, may hold values from -4 to 4
- rel_tables: float32 [2, 12, 64], P(None, 'tensor'), may hold values from -4 to 4
Outputs:
- out: bfloat16 [16384, 768], P('dp')
- grad_input: bfloat16 [16384, 768], P('dp')
- grad_w_qkv: float32 [3, 768, 768], P(None, None, 'tensor')
- grad_b_qv: float32 [2, 768], P(None, 'tensor')
- grad_w_out: float32 [768, 768], P('tensor')
- grad_b_out: float32 [768], replicated
- grad_gain_one: float32 [768], replicated
- grad_shift_one: float32 [768], replicated
- grad_gain_two: float32 [768], replicated
- grad_shift_two: float32 [768], replicated
- grad_w_up: float32 [768, 3072], P(None, 'tensor')
- grad_b_up: float32 [3072], P('tensor')
- grad_w_down: float32 [3072, 768], P('tensor')
- grad_b_down: float32 [768], replicated
- grad_tables: float32 [2, 12, 64], P(None, 'tensor')
The draws below stay inside these ranges and needn't reach their ends.
Inputs may be any that keep to these rules, and one draw needn't show every extreme that they name: The first counts[p] slots of page p hold tokens and the rest are padding; in every draw some page has all 512 slots in use.
All inputs are finite; a program needn't handle non-finite values. No bound on the sum of `keep_mask` on one device may be relied on, other than what follows from the above.
Results may differ from the reference program's by a relative error of at most 0.017.
Values may be sent and summed in bfloat16 or wider, within the bound.
A program may use at most 128 MiB of HBM per device.

```python
import jax
import jax.numpy as jnp
from jax import lax

D = 768
HEADS = 12
HEAD_DIM = 64
FF = 3072
BINS = 64
PAGE = 512
MIN_PAGE = 40
PAGES = 32
TOKENS = 16384


def draw_counts(key, part):
    first_key, second_key = jax.random.split(key)
    drawn = jax.random.randint(first_key, (PAGES,), MIN_PAGE, PAGE + 1)
    full_page = jax.random.randint(second_key, (), 0, PAGES)
    return jnp.where(jnp.arange(PAGES) == full_page, PAGE, drawn).astype(jnp.int32)


def plant(values, stream_key, low, high):
    spot = [jax.random.randint(jax.random.fold_in(stream_key, axis), (), 0, length) for axis, length in enumerate(values.shape)]
    longest = values.shape.index(max(values.shape))
    beside = spot[:longest] + [(spot[longest] + 1) % values.shape[longest]] + spot[longest + 1:]
    return values.at[tuple(spot)].set(low).at[tuple(beside)].set(high)


def block_scale(rng, extent, cuts, smallest, high):
    gain = 1.0
    for axis_at, shards_of in cuts:
        heights = jax.random.uniform(jax.random.fold_in(jax.random.fold_in(rng, 6), axis_at), (shards_of,), jnp.float32, smallest / len(cuts), high / len(cuts))
        gain = gain * jnp.repeat(jnp.exp(heights), extent[axis_at] // shards_of).reshape((-1,) + (1,) * (len(extent) - 1 - axis_at))
    return gain


def noise(own_key, extent, width, reach, cuts=(), held_as=jnp.bfloat16):
    values = jax.random.normal(own_key, extent, jnp.float32) * width
    if len(cuts) > 0:
        values = block_scale(own_key, extent, cuts, -0.22, 0.18) * values
    return jnp.clip(values, min=-reach, max=reach).astype(held_as)


def setup_inputs(seed: int = 0) -> dict:
    key_of = jax.random.split(jax.random.key(seed), 20)
    inputs = noise(key_of[0], (TOKENS, D), 1.0, 6.0, ((0, 8),))
    cotangent = noise(key_of[1], (TOKENS, D), 1.0, 6.0, ((0, 8),))
    counts = draw_counts(jax.random.fold_in(key_of[19], 71), 0)
    keep_mask = plant((jax.random.randint(key_of[3], (TOKENS,), 0, 8) < 7).astype(jnp.int32), jax.random.fold_in(key_of[3], 1), 0, 1)
    box_x = plant(jax.random.randint(key_of[4], (TOKENS,), 0, BINS), jax.random.fold_in(key_of[4], 1), 0, BINS - 1).astype(jnp.int32)
    box_y = plant(jax.random.randint(key_of[5], (TOKENS,), 0, BINS), jax.random.fold_in(key_of[5], 1), 0, BINS - 1).astype(jnp.int32)
    gain_one = jnp.clip(1.0 + 0.1 * jax.random.normal(key_of[6], (D,), jnp.float32), 0.5, 1.5)
    shift_one = noise(key_of[7], (D,), 0.3, 4.0, (), jnp.float32)
    w_qkv = noise(key_of[8], (3, D, D), D ** -0.5, 0.21875, ((2, 4),))
    b_qv = noise(key_of[9], (2, D), 0.3, 4.0, ((1, 4),), jnp.float32)
    w_out = noise(key_of[10], (D, D), (D // 16) ** -0.5, 0.875, ((0, 4),))
    b_out = noise(key_of[11], (D,), 0.3, 4.0, (), jnp.float32)
    gain_two = jnp.clip(1.0 + 0.1 * jax.random.normal(key_of[12], (D,), jnp.float32), 0.5, 1.5)
    shift_two = noise(key_of[13], (D,), 0.3, 4.0, (), jnp.float32)
    w_up = noise(key_of[14], (D, FF), D ** -0.5, 0.21875, ((1, 4),))
    b_up = noise(key_of[15], (FF,), 0.3, 4.0, ((0, 4),), jnp.float32)
    w_down = noise(key_of[16], (FF, D), FF ** -0.5, 0.109375, ((0, 4),))
    b_down = noise(key_of[17], (D,), 0.3, 4.0, (), jnp.float32)
    rel_tables = noise(key_of[18], (2, HEADS, BINS), 0.7, 4.0, ((1, 4),), jnp.float32)
    return dict(inputs=inputs, cotangent=cotangent, counts=counts, keep_mask=keep_mask, box_x=box_x, box_y=box_y, gain_one=gain_one, shift_one=shift_one, w_qkv=w_qkv, b_qv=b_qv, w_out=w_out, b_out=b_out, gain_two=gain_two, shift_two=shift_two, w_up=w_up, b_up=b_up, w_down=w_down, b_down=b_down, rel_tables=rel_tables)


@jax.custom_vjp
def low(v):
    return lax.optimization_barrier(v.astype(jnp.bfloat16)).astype(jnp.float32)

@jax.custom_vjp
def low_back(v):
    return v

def low_keep(v):
    return (low(v), None)

def low_pass(kept, grad):
    return (grad,)

def back_keep(v):
    return (v, None)

def back_low(kept, grad):
    return (low(grad),)
low.defvjp(low_keep, low_pass)
low_back.defvjp(back_keep, back_low)
epsilon = 1e-05
exact_precision = lax.Precision.HIGHEST

def normalize(values, scale_vec, shift_vec):
    average = lax.optimization_barrier(jnp.mean(values, axis=-1, keepdims=True))
    centered = values - average
    variance = lax.optimization_barrier(jnp.mean(centered * centered, axis=-1, keepdims=True))
    return centered * lax.rsqrt(variance + epsilon) * scale_vec + shift_vec

def product(remaining_tokens, right):
    return jnp.dot(remaining_tokens, right, precision=exact_precision)

def attend(pieces, tables):
    queries, key_rows, values, page_count, keep_page, page_box_x, page_box_y = pieces
    positions = jnp.arange(PAGE, dtype=jnp.int32)
    half_bins = BINS // 2
    offset_x = jnp.clip(page_box_x[None, :] - page_box_x[:, None], -half_bins, half_bins - 1) + half_bins
    offset_y = jnp.clip(page_box_y[None, :] - page_box_y[:, None], -half_bins, half_bins - 1) + half_bins
    rel_bias = tables[0][:, offset_x] + tables[1][:, offset_y]
    allowed = (positions[None, :] == positions[:, None]) | (positions[None, :] < page_count) & (keep_page[None, :] == 1)
    raw = low_back(jnp.einsum('ihe,jhe->hij', queries, key_rows, precision=exact_precision) * HEAD_DIM ** (-0.5))
    scores = jnp.where(allowed[None], raw + rel_bias, -1e+30)
    probs_low = low(jax.nn.softmax(scores, axis=-1))
    return jnp.einsum('hij,jhe->ihe', probs_low, values, precision=exact_precision)

def reference(inputs, cotangent, counts, keep_mask, box_x, box_y, gain_one, shift_one, w_qkv, b_qv, w_out, b_out, gain_two, shift_two, w_up, b_up, w_down, b_down, rel_tables):
    positions = jnp.arange(PAGE, dtype=jnp.int32)
    validity = (positions[None, :] < counts[:, None]).astype(jnp.float32).reshape(TOKENS, 1)
    retained_page_mask = keep_mask.reshape(PAGES, PAGE)
    box_pages_x = box_x.reshape(PAGES, PAGE)
    box_pages_y = box_y.reshape(PAGES, PAGE)

    def paged(array):
        return array.reshape(PAGES, PAGE, HEADS, HEAD_DIM)

    def forward(tokens, wqkv, bqv, wout, bout, gone, sone, gtwo, stwo, wup, bup, wdown, bdown, tables):
        normed = low(normalize(tokens, gone, sone))
        queries = low_back(low(product(normed, wqkv[0]) + bqv[0]))
        key_rows = low_back(low(product(normed, wqkv[1])))
        values = low_back(low(product(normed, wqkv[2]) + bqv[1]))
        page_fn = jax.checkpoint(lambda pieces: attend(pieces, tables))
        context = lax.map(page_fn, (paged(queries), paged(key_rows), paged(values), counts, retained_page_mask, box_pages_x, box_pages_y))
        context = low_back(low(context.reshape(TOKENS, D)))
        attended = low_back(product(context, wout))
        hidden = tokens + attended + bout
        normed_two = low(normalize(hidden, gtwo, stwo))
        up_proj = low_back(product(normed_two, wup) + bup)
        activated = low(jax.nn.gelu(up_proj, approximate=False))
        down_proj = low_back(product(activated, wdown))
        return validity * (hidden + down_proj + bdown)
    result, pullback = jax.vjp(forward, inputs.astype(jnp.float32), w_qkv.astype(jnp.float32), b_qv, w_out.astype(jnp.float32), b_out, gain_one, shift_one, gain_two, shift_two, w_up.astype(jnp.float32), b_up, w_down.astype(jnp.float32), b_down, rel_tables)
    gradients = pullback(cotangent.astype(jnp.float32))
    return (result.astype(jnp.bfloat16), gradients[0].astype(jnp.bfloat16), gradients[1], gradients[2], gradients[3], gradients[4], gradients[5], gradients[6], gradients[7], gradients[8], gradients[9], gradients[10], gradients[11], gradients[12], gradients[13])
```

```python
import functools
import jax
import jax.numpy as jnp
from jax import lax
from jax.experimental import pallas as pl
from jax.experimental.pallas import tpu as pltpu
from jax.sharding import PartitionSpec as P

HEAD_DIM = 64
PAGE = 512
BLOCK = 128
epsilon = 1e-05
masked_score = -1e30
LOG2E = 1.4426950408889634
LN2 = 0.6931471805599453
bf16 = jnp.bfloat16
f32 = jnp.float32
VMEM_LIMIT = 60 << 20


def dot(left, right, left_dim, right_dim):
    return lax.dot_general(
        left, right, (((left_dim,), (right_dim,)), ((), ())), preferred_element_type=f32
    )


def nn(left, right):
    return dot(left, right, 1, 0)


def nt(left, right):
    return dot(left, right, 1, 1)


def tn(left, right):
    return dot(left, right, 0, 0)


def norm_parts(rows):
    average = jnp.mean(rows, axis=-1, keepdims=True)
    centered = rows - average
    variance = jnp.mean(centered * centered, axis=-1, keepdims=True)
    inverse = lax.rsqrt(variance + epsilon)
    return centered * inverse, inverse


def norm_grad(grad_out, xhat, inverse, gain):
    scaled = grad_out * gain
    mean_one = jnp.mean(scaled, axis=-1, keepdims=True)
    mean_two = jnp.mean(scaled * xhat, axis=-1, keepdims=True)
    return inverse * (scaled - mean_one - xhat * mean_two)


def one_hot_columns(meta_ref, width, bins):
    levels = lax.broadcasted_iota(jnp.int32, (bins, width), 0)
    hot_x = jnp.where(levels == meta_ref[0, 1:2, 0:width], 1.0, 0.0)
    hot_y = jnp.where(levels == meta_ref[0, 2:3, 0:width], 1.0, 0.0)
    return jnp.concatenate([hot_x, hot_y], axis=0).astype(bf16)


def by_blocks(count, most, body):
    blocks = (count + (BLOCK - 1)) // BLOCK
    for used in range(1, most + 1):
        pl.when(blocks == used)(functools.partial(body, used * BLOCK))


def forward_kernel(
    counts_ref,
    x_ref,
    meta_ref,
    rows_ref,
    bias_ref,
    toeplitz_ref,
    gathered_ref,
    qkv_ref,
    probs_ref,
    inverse_ref,
    context_ref,
    hidden_ref,
    weights,
    copy_sem,
    spread,
    scores,
):
    page = pl.program_id(0)
    width_model = x_ref.shape[1]
    heads = toeplitz_ref.shape[0] // 128
    bins = 64

    @pl.when(page == 0)
    def _():
        copies = [
            pltpu.make_async_copy(gathered_ref.at[:, kind], weights.at[kind], copy_sem.at[kind])
            for kind in range(4)
        ]
        for copy in copies:
            copy.start()
        for copy in copies:
            copy.wait()

    count = counts_ref[page]

    def body(width):
        tokens = x_ref[0:width, :].astype(f32)
        xhat, _ = norm_parts(tokens)
        low = (xhat * rows_ref[0:1, :] + rows_ref[1:2, :]).astype(bf16)
        for kind in range(3):
            weight = weights[kind].reshape(width_model, width_model)
            product = nt(weight, low)
            if kind == 0:
                product = (product + bias_ref[:, 0:1]) * (LOG2E * HEAD_DIM**-0.5)
            if kind == 2:
                product = product + bias_ref[:, 1:2]
            qkv_ref[0, kind, :, 0:width] = product.astype(bf16)
        hot = one_hot_columns(meta_ref, width, bins)
        spread[:, 0:width] = nn(toeplitz_ref[...], hot).astype(bf16)
        lane = lax.broadcasted_iota(jnp.int32, (1, width), 1)
        open_key = (lane < count) & (meta_ref[0, 0:1, 0:width] == 1)
        mask_row = jnp.where(open_key, 0.0, masked_score)
        first = lax.broadcasted_iota(jnp.int32, (HEAD_DIM, width), 0) == 0
        key_pad = jnp.where(first, mask_row, 0.0).astype(bf16)
        query_pad = jnp.where(first, 1.0, 0.0).astype(bf16)
        ones = jnp.ones((16, width), bf16)
        eye = lax.broadcasted_iota(jnp.int32, (BLOCK, BLOCK), 0) == lax.broadcasted_iota(
            jnp.int32, (BLOCK, BLOCK), 1
        )

        def head(index, slot):
            rows = pl.ds(pl.multiple_of(index * HEAD_DIM, HEAD_DIM), HEAD_DIM)
            query = qkv_ref[0, 0, rows, 0:width]
            key = qkv_ref[0, 1, rows, 0:width]
            value = qkv_ref[0, 2, rows, 0:width]
            bias = spread[pl.ds(pl.multiple_of(index * 128, 128), 128), 0:width]
            left = jnp.concatenate([key, key_pad, hot], axis=0)
            right = jnp.concatenate([query, query_pad, bias], axis=0)
            own = jnp.sum(query.astype(f32) * key.astype(f32), axis=0, keepdims=True) + jnp.sum(
                bias.astype(f32) * hot.astype(f32), axis=0, keepdims=True
            )
            raw = tn(left, right)
            scores[slot, 0:width, 0:width] = raw
            for at in range(width // BLOCK):
                span = slice(at * BLOCK, (at + 1) * BLOCK)
                scores[slot, span, span] = jnp.where(eye, own[:, span], scores[slot, span, span])
            top = jnp.max(scores[slot, 0:width, 0:width], axis=0, keepdims=True)
            shifted = jnp.exp2(scores[slot, 0:width, 0:width] - top).astype(bf16)
            probs_ref[0, index, 0:width, 0:width] = shifted
            mixed = nn(jnp.concatenate([value, ones], axis=0), shifted)
            inverse = 1.0 / mixed[HEAD_DIM : HEAD_DIM + 1]
            inverse_ref[0, index, :, 0:width] = inverse
            context_ref[0, rows, 0:width] = (mixed[0:HEAD_DIM] * inverse).astype(bf16)

        def pair(step, carry):
            head(step * 2, 0)
            head(step * 2 + 1, 1)
            return carry

        lax.fori_loop(0, heads // 2, pair, 0)
        attended = tn(context_ref[0, :, 0:width], weights[3].reshape(width_model, width_model))
        hidden_ref[0:width, :] = tokens + attended + rows_ref[2:3, :]

    by_blocks(count, PAGE // BLOCK, body)


def mlp_kernel(
    counts_ref,
    place_ref,
    hidden_ref,
    cotangent_ref,
    rows_ref,
    bias_ref,
    up_ref,
    down_ref,
    out_ref,
    grad_hidden_ref,
    grad_up_ref,
    grad_down_ref,
    sums_ref,
    grad_bias_ref,
    up_total,
    down_total,
):
    page = pl.program_id(0)
    shards = up_ref.shape[0]
    place = place_ref[0]

    @pl.when(page == 0)
    def _():
        up_total[...] = jnp.zeros_like(up_total)
        down_total[...] = jnp.zeros_like(down_total)
        sums_ref[...] = jnp.zeros_like(sums_ref)
        grad_bias_ref[...] = jnp.zeros_like(grad_bias_ref)

    count = counts_ref[page]

    def body(width):
        valid = lax.broadcasted_iota(jnp.int32, (width, 1), 0) < count
        hidden = hidden_ref[0:width, :]
        xhat, inverse = norm_parts(hidden)
        low = (xhat * rows_ref[0:1, :] + rows_ref[1:2, :]).astype(bf16)
        grad_result = jnp.where(valid, cotangent_ref[0:width, :].astype(f32), 0.0)
        grad_low = grad_result.astype(bf16)

        def shard(at, carry):
            down_proj, grad_normed = carry
            upper = nn(low, up_ref[at]) + bias_ref[at]
            half = 0.5 * (1.0 + lax.erf(upper * 0.7071067811865476))
            density = jnp.exp(-0.5 * upper * upper) * 0.3989422804014327
            active = (upper * half).astype(bf16)
            slope = half + upper * density
            down_proj = down_proj + nn(active, down_ref[at])
            grad_upper = (nt(grad_low, down_ref[at]) * slope).astype(bf16)
            grad_normed = grad_normed + nt(grad_upper, up_ref[at])

            @pl.when(at == place)
            def _():
                up_total[...] += tn(low, grad_upper)
                down_total[...] += tn(active, grad_low)
                grad_bias_ref[...] += jnp.sum(grad_upper.astype(f32), axis=0, keepdims=True)

            return down_proj, grad_normed

        zero = jnp.zeros((width, hidden.shape[1]), f32)
        down_proj, grad_normed = lax.fori_loop(0, shards, shard, (zero, zero))
        result = jnp.where(valid, hidden + down_proj + rows_ref[2:3, :], 0.0)
        out_ref[0:width, :] = result.astype(bf16)
        grad_hidden = grad_result + norm_grad(grad_normed, xhat, inverse, rows_ref[0:1, :])
        grad_hidden_ref[0:width, :] = grad_hidden
        sums_ref[0:1, :] += jnp.sum(grad_normed * xhat, axis=0, keepdims=True)
        sums_ref[1:2, :] += jnp.sum(grad_normed, axis=0, keepdims=True)
        sums_ref[2:3, :] += jnp.sum(grad_hidden, axis=0, keepdims=True)
        sums_ref[3:4, :] += jnp.sum(grad_result, axis=0, keepdims=True)
        if width < PAGE:
            out_ref[width:PAGE, :] = jnp.zeros((PAGE - width, hidden.shape[1]), bf16)

    by_blocks(count, PAGE // BLOCK, body)

    @pl.when(page == pl.num_programs(0) - 1)
    def _():
        grad_up_ref[...] = up_total[...].astype(bf16)
        grad_down_ref[...] = down_total[...].astype(bf16)


def backward_kernel(
    counts_ref,
    place_ref,
    x_ref,
    meta_ref,
    rows_ref,
    grad_hidden_ref,
    qkv_ref,
    probs_ref,
    inverse_ref,
    context_ref,
    gathered_ref,
    grad_input_ref,
    grad_pack_ref,
    sums_ref,
    grad_bias_ref,
    levels_ref,
    weights,
    copy_sem,
    grad_qkv,
    grad_context,
    small_scores,
    pack_total,
):
    page = pl.program_id(0)
    place = place_ref[0]
    width_model = x_ref.shape[1]
    heads = probs_ref.shape[1]
    own = width_model // 4
    bins = 64

    @pl.when(page == 0)
    def _():
        copies = [
            pltpu.make_async_copy(gathered_ref.at[:, kind], weights.at[kind], copy_sem.at[kind])
            for kind in range(4)
        ]
        for copy in copies:
            copy.start()
        pack_total[...] = jnp.zeros_like(pack_total)
        sums_ref[...] = jnp.zeros_like(sums_ref)
        grad_bias_ref[...] = jnp.zeros_like(grad_bias_ref)
        levels_ref[...] = jnp.zeros_like(levels_ref)
        for copy in copies:
            copy.wait()

    count = counts_ref[page]

    def body(width):
        grad_hidden = grad_hidden_ref[0:width, :]
        grad_low = grad_hidden.astype(bf16)
        grad_context[:, 0:width] = nt(weights[3].reshape(width_model, width_model), grad_low)
        hot = one_hot_columns(meta_ref, width, bins)

        def head(index, slot):
            rows = pl.ds(pl.multiple_of(index * HEAD_DIM, HEAD_DIM), HEAD_DIM)
            query = qkv_ref[0, 0, rows, 0:width]
            key = qkv_ref[0, 1, rows, 0:width]
            value = qkv_ref[0, 2, rows, 0:width]
            probs = probs_ref[0, index, 0:width, 0:width]
            grad_mixed = (grad_context[rows, 0:width] * inverse_ref[0, index, :, 0:width]).astype(bf16)
            delta = jnp.sum(
                grad_mixed.astype(f32) * context_ref[0, rows, 0:width].astype(f32),
                axis=0,
                keepdims=True,
            )
            grad_probs = tn(value, grad_mixed)
            grad_scores = (probs.astype(f32) * (grad_probs - delta)).astype(bf16)
            small_scores[slot, 0:width, 0:width] = grad_scores
            grad_value = nt(grad_mixed, probs)
            grad_key = nt(query, grad_scores) * LN2
            both = nn(jnp.concatenate([key, hot], axis=0), grad_scores)
            grad_qkv[0, rows, 0:width] = (both[0:HEAD_DIM] * HEAD_DIM**-0.5).astype(bf16)
            grad_qkv[1, rows, 0:width] = grad_key.astype(bf16)
            grad_qkv[2, rows, 0:width] = grad_value.astype(bf16)
            levels_ref[index] += nt(both[HEAD_DIM:].astype(bf16), hot)

        def pair(step, carry):
            head(step * 2, 0)
            head(step * 2 + 1, 1)
            return carry

        lax.fori_loop(0, heads // 2, pair, 0)
        tokens = x_ref[0:width, :].astype(f32)
        xhat, inverse = norm_parts(tokens)
        low = (xhat * rows_ref[0:1, :] + rows_ref[1:2, :]).astype(bf16)
        mine = pl.ds(pl.multiple_of(place * own, own), own)
        stacked = jnp.concatenate([grad_qkv[kind, mine, 0:width] for kind in range(3)], axis=0)
        pack_total[0 : 3 * own, :] += nn(stacked, low)
        pack_total[3 * own :, :] += nn(context_ref[0, mine, 0:width], grad_low)
        wide = stacked.astype(f32)
        folded = wide[:, 0:BLOCK]
        for at in range(1, width // BLOCK):
            folded = folded + wide[:, at * BLOCK : (at + 1) * BLOCK]
        grad_bias_ref[...] += folded
        grad_normed = tn(grad_qkv[0, :, 0:width], weights[0].reshape(width_model, width_model))
        for kind in (1, 2):
            grad_normed = grad_normed + tn(
                grad_qkv[kind, :, 0:width], weights[kind].reshape(width_model, width_model)
            )
        grad_total = grad_hidden + norm_grad(grad_normed, xhat, inverse, rows_ref[0:1, :])
        grad_input_ref[0:width, :] = grad_total.astype(bf16)
        sums_ref[0:1, :] += jnp.sum(grad_normed * xhat, axis=0, keepdims=True)
        sums_ref[1:2, :] += jnp.sum(grad_normed, axis=0, keepdims=True)
        if width < PAGE:
            grad_input_ref[width:PAGE, :] = jnp.zeros((PAGE - width, width_model), bf16)

    by_blocks(count, PAGE // BLOCK, body)

    @pl.when(page == pl.num_programs(0) - 1)
    def _():
        grad_pack_ref[...] = pack_total[...].astype(bf16)


def toeplitz(tables):
    bins = tables.shape[-1]
    half = bins // 2
    levels = jnp.arange(bins, dtype=jnp.int32)
    offsets = jnp.clip(levels[:, None] - levels[None, :], -half, half - 1) + half
    pick = (offsets[:, :, None] == levels).astype(f32)
    full = jnp.einsum("khc,bac->khba", tables, pick, precision=lax.Precision.HIGHEST)
    zero = jnp.zeros_like(full[0])
    top = jnp.concatenate([full[0], zero], axis=2)
    bottom = jnp.concatenate([zero, full[1]], axis=2)
    return jnp.concatenate([top, bottom], axis=1)


def fold_levels(levels_grad, bins):
    half = bins // 2
    levels = jnp.arange(bins, dtype=jnp.int32)
    offsets = jnp.clip(levels[:, None] - levels[None, :], -half, half - 1) + half
    pick = (offsets[:, :, None] == levels).astype(f32)
    both = jnp.stack([levels_grad[:, 0:bins, 0:bins], levels_grad[:, bins:, bins:]])
    return jnp.einsum("khba,bac->khc", both, pick, precision=lax.Precision.HIGHEST)


def whole(shape):
    return pl.BlockSpec(shape, lambda *_: (0,) * len(shape), pipeline_mode=pl.Buffered(1))


def on_device(
    inputs,
    cotangent,
    counts,
    keep_mask,
    box_x,
    box_y,
    gain_one,
    shift_one,
    w_qkv,
    b_qv,
    w_out,
    b_out,
    gain_two,
    shift_two,
    w_up,
    b_up,
    w_down,
    b_down,
    rel_tables,
):
    rows_here, model = inputs.shape
    pages = rows_here // PAGE
    own_heads, bins = rel_tables.shape[1:]
    own = own_heads * HEAD_DIM
    shards = model // own
    heads = own_heads * shards
    hidden_units = w_up.shape[1]
    place = lax.axis_index("tensor").astype(jnp.int32).reshape(1)

    pack = jnp.concatenate([w_qkv.transpose(0, 2, 1).reshape(3 * own, model), w_out], axis=0)
    gathered = lax.all_gather(pack, "tensor").reshape(shards, 4, own, model)
    up_all = lax.all_gather(w_up, "tensor")
    down_all = lax.all_gather(w_down, "tensor")
    bias_all = lax.all_gather(b_qv, "tensor", axis=1, tiled=True)
    up_bias = lax.all_gather(b_up, "tensor").reshape(shards, 1, hidden_units)
    tables_all = lax.all_gather(rel_tables, "tensor", axis=1, tiled=True)

    toep = (toeplitz(tables_all) * LOG2E).astype(bf16).reshape(heads * 2 * bins, 2 * bins)
    meta = jnp.stack(
        [keep_mask.reshape(pages, PAGE), box_x.reshape(pages, PAGE), box_y.reshape(pages, PAGE)], axis=1
    )
    meta = jnp.pad(meta, ((0, 0), (0, 5), (0, 0)))
    rows_one = jnp.stack([gain_one, shift_one, b_out])
    rows_two = jnp.stack([gain_two, shift_two, b_down])

    page_rows = lambda: pl.BlockSpec((PAGE, model), lambda p, *_: (p, 0))
    meta_spec = pl.BlockSpec((1, 8, PAGE), lambda p, *_: (p, 0, 0))
    qkv_spec = pl.BlockSpec((1, 3, model, PAGE), lambda p, *_: (p, 0, 0, 0))
    probs_spec = pl.BlockSpec((1, heads, PAGE, PAGE), lambda p, *_: (p, 0, 0, 0))
    inverse_spec = pl.BlockSpec((1, heads, 1, PAGE), lambda p, *_: (p, 0, 0, 0))
    context_spec = pl.BlockSpec((1, model, PAGE), lambda p, *_: (p, 0, 0))
    anywhere = pl.BlockSpec(memory_space=pl.ANY)
    params = pltpu.CompilerParams(
        dimension_semantics=("arbitrary",), vmem_limit_bytes=VMEM_LIMIT
    )
    weight_scratch = [
        pltpu.VMEM((4, shards, own, model), bf16),
        pltpu.SemaphoreType.DMA((4,)),
    ]

    qkv, probs, inverse, context, hidden = pl.pallas_call(
        forward_kernel,
        out_shape=(
            jax.ShapeDtypeStruct((pages, 3, model, PAGE), bf16),
            jax.ShapeDtypeStruct((pages, heads, PAGE, PAGE), bf16),
            jax.ShapeDtypeStruct((pages, heads, 1, PAGE), f32),
            jax.ShapeDtypeStruct((pages, model, PAGE), bf16),
            jax.ShapeDtypeStruct((rows_here, model), f32),
        ),
        grid_spec=pltpu.PrefetchScalarGridSpec(
            num_scalar_prefetch=1,
            grid=(pages,),
            in_specs=[
                page_rows(),
                meta_spec,
                whole((3, model)),
                whole((model, 2)),
                whole((heads * 2 * bins, 2 * bins)),
                anywhere,
            ],
            out_specs=(qkv_spec, probs_spec, inverse_spec, context_spec, page_rows()),
            scratch_shapes=weight_scratch
            + [
                pltpu.VMEM((heads * 2 * bins, PAGE), bf16),
                pltpu.VMEM((2, PAGE, PAGE), f32),
            ],
        ),
        compiler_params=params,
        name="attention_forward",
    )(counts, inputs, meta, rows_one, bias_all.T, toep, gathered)

    out, grad_hidden, grad_up, grad_down, sums_two, grad_b_up = pl.pallas_call(
        mlp_kernel,
        out_shape=(
            jax.ShapeDtypeStruct((rows_here, model), bf16),
            jax.ShapeDtypeStruct((rows_here, model), f32),
            jax.ShapeDtypeStruct((model, hidden_units), bf16),
            jax.ShapeDtypeStruct((hidden_units, model), bf16),
            jax.ShapeDtypeStruct((8, model), f32),
            jax.ShapeDtypeStruct((1, hidden_units), f32),
        ),
        grid_spec=pltpu.PrefetchScalarGridSpec(
            num_scalar_prefetch=2,
            grid=(pages,),
            in_specs=[
                page_rows(),
                page_rows(),
                whole((3, model)),
                whole((shards, 1, hidden_units)),
                whole((shards, model, hidden_units)),
                whole((shards, hidden_units, model)),
            ],
            out_specs=(
                page_rows(),
                page_rows(),
                whole((model, hidden_units)),
                whole((hidden_units, model)),
                whole((8, model)),
                whole((1, hidden_units)),
            ),
            scratch_shapes=[
                pltpu.VMEM((model, hidden_units), f32),
                pltpu.VMEM((hidden_units, model), f32),
            ],
        ),
        compiler_params=params,
        name="feed_forward",
    )(counts, place, hidden, cotangent, rows_two, up_bias, up_all, down_all)

    grad_input, grad_pack, sums_one, grad_bias, levels_grad = pl.pallas_call(
        backward_kernel,
        out_shape=(
            jax.ShapeDtypeStruct((rows_here, model), bf16),
            jax.ShapeDtypeStruct((4 * own, model), bf16),
            jax.ShapeDtypeStruct((8, model), f32),
            jax.ShapeDtypeStruct((3 * own, BLOCK), f32),
            jax.ShapeDtypeStruct((heads, 2 * bins, 2 * bins), f32),
        ),
        grid_spec=pltpu.PrefetchScalarGridSpec(
            num_scalar_prefetch=2,
            grid=(pages,),
            in_specs=[
                page_rows(),
                meta_spec,
                whole((3, model)),
                page_rows(),
                qkv_spec,
                probs_spec,
                inverse_spec,
                context_spec,
                anywhere,
            ],
            out_specs=(
                page_rows(),
                whole((4 * own, model)),
                whole((8, model)),
                whole((3 * own, BLOCK)),
                whole((heads, 2 * bins, 2 * bins)),
            ),
            scratch_shapes=weight_scratch
            + [
                pltpu.VMEM((3, model, PAGE), bf16),
                pltpu.VMEM((model, PAGE), f32),
                pltpu.VMEM((2, PAGE, PAGE), bf16),
                pltpu.VMEM((4 * own, model), f32),
            ],
        ),
        compiler_params=params,
        name="attention_backward",
    )(counts, place, inputs, meta, rows_one, grad_hidden, qkv, probs, inverse, context, gathered)

    levels_own = lax.dynamic_slice_in_dim(levels_grad, place[0] * own_heads, own_heads, 0)
    grad_tables = fold_levels(levels_own, bins)
    bias_sums = jnp.sum(grad_bias, axis=1).reshape(3, own)
    grad_b_qv = jnp.stack([bias_sums[0], bias_sums[2]])

    big = lax.psum((grad_pack, grad_up, grad_down), "dp")
    small = lax.psum((sums_one, sums_two, grad_b_up, grad_b_qv, grad_tables), "dp")
    grad_pack, grad_up, grad_down = (part.astype(f32) for part in big)
    sums_one, sums_two, grad_b_up, grad_b_qv, grad_tables = small
    grad_w_qkv = grad_pack[0 : 3 * own].reshape(3, own, model).transpose(0, 2, 1)
    return (
        out,
        grad_input,
        grad_w_qkv,
        grad_b_qv,
        grad_pack[3 * own :],
        sums_two[2],
        sums_one[0],
        sums_one[1],
        sums_two[0],
        sums_two[1],
        grad_up,
        grad_b_up.reshape(-1),
        grad_down,
        sums_two[3],
        grad_tables,
    )


def solution(mesh):
    placed = (
        P("dp", None),
        P("dp", None),
        P("dp"),
        P("dp"),
        P("dp"),
        P("dp"),
        P(),
        P(),
        P(None, None, "tensor"),
        P(None, "tensor"),
        P("tensor", None),
        P(),
        P(),
        P(),
        P(None, "tensor"),
        P("tensor"),
        P("tensor", None),
        P(),
        P(None, "tensor", None),
    )
    return jax.shard_map(
        on_device,
        mesh=mesh,
        in_specs=placed,
        out_specs=(
            P("dp", None),
            P("dp", None),
            P(None, None, "tensor"),
            P(None, "tensor"),
            P("tensor", None),
            P(),
            P(),
            P(),
            P(),
            P(),
            P(None, "tensor"),
            P("tensor"),
            P("tensor", None),
            P(),
            P(None, "tensor", None),
        ),
        check_vma=False,
    )
```

```python
import functools
import jax
import jax.numpy as jnp
from jax import lax
from jax.experimental import pallas as pl
from jax.experimental.pallas import tpu as pltpu
from jax.sharding import PartitionSpec as P

HEAD_DIM = 64
PAGE = 512
BLOCK = 128
epsilon = 1e-05
masked_score = -1e30
LOG2E = 1.4426950408889634
LN2 = 0.6931471805599453
bf16 = jnp.bfloat16
f32 = jnp.float32
VMEM_LIMIT = 60 << 20


def dot(left, right, left_dim, right_dim):
    return lax.dot_general(
        left, right, (((left_dim,), (right_dim,)), ((), ())), preferred_element_type=f32
    )


def nn(left, right):
    return dot(left, right, 1, 0)


def nt(left, right):
    return dot(left, right, 1, 1)


def tn(left, right):
    return dot(left, right, 0, 0)


def norm_parts(rows):
    average = jnp.mean(rows, axis=-1, keepdims=True)
    centered = rows - average
    variance = jnp.mean(centered * centered, axis=-1, keepdims=True)
    inverse = lax.rsqrt(variance + epsilon)
    return centered * inverse, inverse


def norm_grad(grad_out, xhat, inverse, gain):
    scaled = grad_out * gain
    mean_one = jnp.mean(scaled, axis=-1, keepdims=True)
    mean_two = jnp.mean(scaled * xhat, axis=-1, keepdims=True)
    return inverse * (scaled - mean_one - xhat * mean_two)


def one_hot_columns(meta_ref, width, bins):
    levels = lax.broadcasted_iota(jnp.int32, (bins, width), 0)
    hot_x = jnp.where(levels == meta_ref[0, 1:2, 0:width], 1.0, 0.0)
    hot_y = jnp.where(levels == meta_ref[0, 2:3, 0:width], 1.0, 0.0)
    return jnp.concatenate([hot_x, hot_y], axis=0).astype(bf16)


def by_blocks(count, most, body):
    half = most * BLOCK // 2
    pl.when(count <= half)(functools.partial(body, half))
    pl.when(count > half)(functools.partial(body, 2 * half))


def forward_kernel(
    counts_ref,
    x_ref,
    meta_ref,
    rows_ref,
    bias_ref,
    toeplitz_ref,
    gathered_ref,
    qkv_ref,
    probs_ref,
    inverse_ref,
    context_ref,
    hidden_ref,
    weights,
    copy_sem,
    spread,
    scores,
):
    page = pl.program_id(0)
    width_model = x_ref.shape[1]
    heads = toeplitz_ref.shape[0] // 128
    bins = 64

    @pl.when(page == 0)
    def _():
        copies = [
            pltpu.make_async_copy(gathered_ref.at[:, kind], weights.at[kind], copy_sem.at[kind])
            for kind in range(4)
        ]
        for copy in copies:
            copy.start()
        for copy in copies:
            copy.wait()

    count = counts_ref[page]

    def body(width):
        tokens = x_ref[0:width, :].astype(f32)
        xhat, _ = norm_parts(tokens)
        low = (xhat * rows_ref[0:1, :] + rows_ref[1:2, :]).astype(bf16)
        for kind in range(3):
            weight = weights[kind].reshape(width_model, width_model)
            product = nt(weight, low)
            if kind == 0:
                product = (product + bias_ref[:, 0:1]) * (LOG2E * HEAD_DIM**-0.5)
            if kind == 2:
                product = product + bias_ref[:, 1:2]
            qkv_ref[0, kind, :, 0:width] = product.astype(bf16)
        hot = one_hot_columns(meta_ref, width, bins)
        spread[:, 0:width] = nn(toeplitz_ref[...], hot).astype(bf16)
        lane = lax.broadcasted_iota(jnp.int32, (1, width), 1)
        open_key = (lane < count) & (meta_ref[0, 0:1, 0:width] == 1)
        mask_row = jnp.where(open_key, 0.0, masked_score)
        first = lax.broadcasted_iota(jnp.int32, (HEAD_DIM, width), 0) == 0
        key_pad = jnp.where(first, mask_row, 0.0).astype(bf16)
        query_pad = jnp.where(first, 1.0, 0.0).astype(bf16)
        ones = jnp.ones((16, width), bf16)
        eye = lax.broadcasted_iota(jnp.int32, (BLOCK, BLOCK), 0) == lax.broadcasted_iota(
            jnp.int32, (BLOCK, BLOCK), 1
        )

        def rows_of(index):
            return pl.ds(pl.multiple_of(index * HEAD_DIM, HEAD_DIM), HEAD_DIM)

        def score(index, slot):
            rows = rows_of(index)
            query = qkv_ref[0, 0, rows, 0:width]
            key = qkv_ref[0, 1, rows, 0:width]
            bias = spread[pl.ds(pl.multiple_of(index * 128, 128), 128), 0:width]
            left = jnp.concatenate([key, key_pad, hot], axis=0)
            right = jnp.concatenate([query, query_pad, bias], axis=0)
            scores[slot, 0:width, 0:width] = tn(left, right)
            return jnp.sum(query.astype(f32) * key.astype(f32), axis=0, keepdims=True) + jnp.sum(
                bias.astype(f32) * hot.astype(f32), axis=0, keepdims=True
            )

        def soften(index, slot, own):
            for at in range(width // BLOCK):
                span = slice(at * BLOCK, (at + 1) * BLOCK)
                scores[slot, span, span] = jnp.where(eye, own[:, span], scores[slot, span, span])
            top = jnp.max(scores[slot, 0:width, 0:width], axis=0, keepdims=True)
            probs_ref[0, index, 0:width, 0:width] = jnp.exp2(scores[slot, 0:width, 0:width] - top).astype(bf16)

        def mix(index):
            rows = rows_of(index)
            value = qkv_ref[0, 2, rows, 0:width]
            mixed = nn(jnp.concatenate([value, ones], axis=0), probs_ref[0, index, 0:width, 0:width])
            inverse = 1.0 / mixed[HEAD_DIM : HEAD_DIM + 1]
            inverse_ref[0, index, :, 0:width] = inverse
            context_ref[0, rows, 0:width] = (mixed[0:HEAD_DIM] * inverse).astype(bf16)

        owns = [score(0, 0)]
        for at in range(heads):
            if at + 1 < heads:
                owns.append(score(at + 1, (at + 1) % 2))
            soften(at, at % 2, owns[at])
            if at > 0:
                mix(at - 1)
        mix(heads - 1)
        attended = tn(context_ref[0, :, 0:width], weights[3].reshape(width_model, width_model))
        hidden_ref[0:width, :] = tokens + attended + rows_ref[2:3, :]

    by_blocks(count, PAGE // BLOCK, body)


def mlp_kernel(
    counts_ref,
    place_ref,
    hidden_ref,
    cotangent_ref,
    rows_ref,
    bias_ref,
    up_ref,
    down_ref,
    out_ref,
    grad_hidden_ref,
    grad_up_ref,
    grad_down_ref,
    sums_ref,
    grad_bias_ref,
    up_total,
    down_total,
    low_ref,
    gl_ref,
    down_acc,
    gn_acc,
    act_ref,
    gu_ref,
    upper_ref,
    grad_ref,
):
    page = pl.program_id(0)
    shards = up_ref.shape[0]
    place = place_ref[0]

    @pl.when(page == 0)
    def _():
        up_total[...] = jnp.zeros_like(up_total)
        down_total[...] = jnp.zeros_like(down_total)
        sums_ref[...] = jnp.zeros_like(sums_ref)
        grad_bias_ref[...] = jnp.zeros_like(grad_bias_ref)

    count = counts_ref[page]

    def body(width):
        valid = lax.broadcasted_iota(jnp.int32, (width, 1), 0) < count
        hidden = hidden_ref[0:width, :]
        xhat, inverse = norm_parts(hidden)
        low = (xhat * rows_ref[0:1, :] + rows_ref[1:2, :]).astype(bf16)
        grad_result = jnp.where(valid, cotangent_ref[0:width, :].astype(f32), 0.0)
        grad_low = grad_result.astype(bf16)

        low_ref[0:width, :] = low
        gl_ref[0:width, :] = grad_low
        down_acc[0:width, :] = jnp.zeros((width, hidden.shape[1]), f32)
        gn_acc[0:width, :] = jnp.zeros((width, hidden.shape[1]), f32)

        def lead(at, slot):
            upper_ref[slot, 0:width, :] = nn(low_ref[0:width, :], up_ref[at]) + bias_ref[at]
            grad_ref[slot, 0:width, :] = nt(gl_ref[0:width, :], down_ref[at])

        def bend(at, slot):
            upper = upper_ref[slot, 0:width, :]
            half = 0.5 * (1.0 + lax.erf(upper * 0.7071067811865476))
            density = jnp.exp(-0.5 * upper * upper) * 0.3989422804014327
            act_ref[at, 0:width, :] = (upper * half).astype(bf16)
            slope = half + upper * density
            gu_ref[at, 0:width, :] = (grad_ref[slot, 0:width, :] * slope).astype(bf16)

        def mix(at):
            down_acc[0:width, :] += nn(act_ref[at, 0:width, :], down_ref[at])
            gn_acc[0:width, :] += nt(gu_ref[at, 0:width, :], up_ref[at])

        lead(0, 0)
        for at in range(shards):
            if at + 1 < shards:
                lead(at + 1, (at + 1) % 2)
            bend(at, at % 2)
            if at > 0:
                mix(at - 1)
        mix(shards - 1)
        down_proj = down_acc[0:width, :]
        grad_normed = gn_acc[0:width, :]
        up_total[...] += tn(low_ref[0:width, :], gu_ref[place, 0:width, :])
        down_total[...] += tn(act_ref[place, 0:width, :], gl_ref[0:width, :])
        grad_bias_ref[...] += jnp.sum(gu_ref[place, 0:width, :].astype(f32), axis=0, keepdims=True)
        result = jnp.where(valid, hidden + down_proj + rows_ref[2:3, :], 0.0)
        out_ref[0:width, :] = result.astype(bf16)
        grad_hidden = grad_result + norm_grad(grad_normed, xhat, inverse, rows_ref[0:1, :])
        grad_hidden_ref[0:width, :] = grad_hidden
        sums_ref[0:1, :] += jnp.sum(grad_normed * xhat, axis=0, keepdims=True)
        sums_ref[1:2, :] += jnp.sum(grad_normed, axis=0, keepdims=True)
        sums_ref[2:3, :] += jnp.sum(grad_hidden, axis=0, keepdims=True)
        sums_ref[3:4, :] += jnp.sum(grad_result, axis=0, keepdims=True)
        if width < PAGE:
            out_ref[width:PAGE, :] = jnp.zeros((PAGE - width, hidden.shape[1]), bf16)

    by_blocks(count, PAGE // BLOCK, body)

    @pl.when(page == pl.num_programs(0) - 1)
    def _():
        grad_up_ref[...] = up_total[...].astype(bf16)
        grad_down_ref[...] = down_total[...].astype(bf16)


def backward_kernel(
    counts_ref,
    place_ref,
    x_ref,
    meta_ref,
    rows_ref,
    grad_hidden_ref,
    qkv_ref,
    probs_ref,
    inverse_ref,
    context_ref,
    gathered_ref,
    grad_input_ref,
    grad_pack_ref,
    sums_ref,
    grad_bias_ref,
    levels_ref,
    weights,
    copy_sem,
    grad_qkv,
    grad_context,
    grad_probs,
    small_scores,
    pack_total,
):
    page = pl.program_id(0)
    place = place_ref[0]
    width_model = x_ref.shape[1]
    heads = probs_ref.shape[1]
    own_heads = levels_ref.shape[0]
    own = own_heads * HEAD_DIM
    bins = 64

    @pl.when(page == 0)
    def _():
        copies = [
            pltpu.make_async_copy(gathered_ref.at[:, kind], weights.at[kind], copy_sem.at[kind])
            for kind in range(4)
        ]
        for copy in copies:
            copy.start()
        pack_total[...] = jnp.zeros_like(pack_total)
        sums_ref[...] = jnp.zeros_like(sums_ref)
        grad_bias_ref[...] = jnp.zeros_like(grad_bias_ref)
        levels_ref[...] = jnp.zeros_like(levels_ref)
        for copy in copies:
            copy.wait()

    count = counts_ref[page]

    def body(width):
        grad_hidden = grad_hidden_ref[0:width, :]
        grad_low = grad_hidden.astype(bf16)
        grad_context[:, 0:width] = nt(weights[3].reshape(width_model, width_model), grad_low)
        hot = one_hot_columns(meta_ref, width, bins)

        def order(at):
            return lax.rem(place * own_heads + at, heads)

        def rows_of(index):
            return pl.ds(pl.multiple_of(index * HEAD_DIM, HEAD_DIM), HEAD_DIM)

        def lead(index, slot):
            rows = rows_of(index)
            value = qkv_ref[0, 2, rows, 0:width]
            grad_mixed = (grad_context[rows, 0:width] * inverse_ref[0, index, :, 0:width]).astype(bf16)
            grad_probs[slot, 0:width, 0:width] = tn(value, grad_mixed)
            delta = jnp.sum(
                grad_mixed.astype(f32) * context_ref[0, rows, 0:width].astype(f32),
                axis=0,
                keepdims=True,
            )
            return grad_mixed, delta

        def soften(index, slot, delta):
            probs = probs_ref[0, index, 0:width, 0:width].astype(f32)
            small_scores[slot, 0:width, 0:width] = (probs * (grad_probs[slot, 0:width, 0:width] - delta)).astype(bf16)

        def mix(at, slot, grad_mixed):
            index = order(at)
            rows = rows_of(index)
            query = qkv_ref[0, 0, rows, 0:width]
            key = qkv_ref[0, 1, rows, 0:width]
            grad_scores = small_scores[slot, 0:width, 0:width]
            grad_value = nt(grad_mixed, probs_ref[0, index, 0:width, 0:width])
            grad_key = nt(query, grad_scores) * LN2
            both = nn(jnp.concatenate([key, hot], axis=0) if at < own_heads else key, grad_scores)
            grad_qkv[0, rows, 0:width] = (both[0:HEAD_DIM] * HEAD_DIM**-0.5).astype(bf16)
            grad_qkv[1, rows, 0:width] = grad_key.astype(bf16)
            grad_qkv[2, rows, 0:width] = grad_value.astype(bf16)
            if at < own_heads:
                levels_ref[at] += nt(both[HEAD_DIM:].astype(bf16), hot)

        kept = [lead(order(0), 0)]
        for at in range(heads):
            if at + 1 < heads:
                kept.append(lead(order(at + 1), (at + 1) % 2))
            soften(order(at), at % 2, kept[at][1])
            if at > 0:
                mix(at - 1, (at - 1) % 2, kept[at - 1][0])
        mix(heads - 1, (heads - 1) % 2, kept[-1][0])
        tokens = x_ref[0:width, :].astype(f32)
        xhat, inverse = norm_parts(tokens)
        low = (xhat * rows_ref[0:1, :] + rows_ref[1:2, :]).astype(bf16)
        mine = pl.ds(pl.multiple_of(place * own, own), own)
        stacked = jnp.concatenate([grad_qkv[kind, mine, 0:width] for kind in range(3)], axis=0)
        pack_total[0 : 3 * own, :] += nn(stacked, low)
        pack_total[3 * own :, :] += nn(context_ref[0, mine, 0:width], grad_low)
        wide = stacked.astype(f32)
        folded = wide[:, 0:BLOCK]
        for at in range(1, width // BLOCK):
            folded = folded + wide[:, at * BLOCK : (at + 1) * BLOCK]
        grad_bias_ref[...] += folded
        grad_normed = tn(grad_qkv[0, :, 0:width], weights[0].reshape(width_model, width_model))
        for kind in (1, 2):
            grad_normed = grad_normed + tn(
                grad_qkv[kind, :, 0:width], weights[kind].reshape(width_model, width_model)
            )
        grad_total = grad_hidden + norm_grad(grad_normed, xhat, inverse, rows_ref[0:1, :])
        grad_input_ref[0:width, :] = grad_total.astype(bf16)
        sums_ref[0:1, :] += jnp.sum(grad_normed * xhat, axis=0, keepdims=True)
        sums_ref[1:2, :] += jnp.sum(grad_normed, axis=0, keepdims=True)
        if width < PAGE:
            grad_input_ref[width:PAGE, :] = jnp.zeros((PAGE - width, width_model), bf16)

    by_blocks(count, PAGE // BLOCK, body)

    @pl.when(page == pl.num_programs(0) - 1)
    def _():
        grad_pack_ref[...] = pack_total[...].astype(bf16)


def toeplitz(tables):
    bins = tables.shape[-1]
    half = bins // 2
    levels = jnp.arange(bins, dtype=jnp.int32)
    offsets = jnp.clip(levels[:, None] - levels[None, :], -half, half - 1) + half
    pick = (offsets[:, :, None] == levels).astype(f32)
    full = jnp.einsum("khc,bac->khba", tables, pick, precision=lax.Precision.HIGHEST)
    zero = jnp.zeros_like(full[0])
    top = jnp.concatenate([full[0], zero], axis=2)
    bottom = jnp.concatenate([zero, full[1]], axis=2)
    return jnp.concatenate([top, bottom], axis=1)


def fold_levels(levels_grad, bins):
    half = bins // 2
    levels = jnp.arange(bins, dtype=jnp.int32)
    offsets = jnp.clip(levels[:, None] - levels[None, :], -half, half - 1) + half
    pick = (offsets[:, :, None] == levels).astype(f32)
    both = jnp.stack([levels_grad[:, 0:bins, 0:bins], levels_grad[:, bins:, bins:]])
    return jnp.einsum("khba,bac->khc", both, pick, precision=lax.Precision.HIGHEST)


def whole(shape):
    return pl.BlockSpec(shape, lambda *_: (0,) * len(shape), pipeline_mode=pl.Buffered(1))


def page_rows(model):
    return pl.BlockSpec((PAGE, model), lambda p, *_: (p, 0))


def page_block(*shape):
    return pl.BlockSpec((1,) + shape, lambda p, *_: (p,) + (0,) * len(shape))


ANYWHERE = pl.BlockSpec(memory_space=pl.ANY)
PARAMS = pltpu.CompilerParams(dimension_semantics=("arbitrary",), vmem_limit_bytes=VMEM_LIMIT)


def weight_scratch(shards, own, model):
    return [pltpu.VMEM((4, shards, own, model), bf16), pltpu.SemaphoreType.DMA((4,))]


def attention_forward(counts, inputs, meta, rows_one, bias, toep, gathered):
    rows_here, model = inputs.shape
    pages = rows_here // PAGE
    shards, _, own, _ = gathered.shape
    bins = toep.shape[1] // 2
    heads = model // HEAD_DIM
    return pl.pallas_call(
        forward_kernel,
        out_shape=(
            jax.ShapeDtypeStruct((pages, 3, model, PAGE), bf16),
            jax.ShapeDtypeStruct((pages, heads, PAGE, PAGE), bf16),
            jax.ShapeDtypeStruct((pages, heads, 1, PAGE), f32),
            jax.ShapeDtypeStruct((pages, model, PAGE), bf16),
            jax.ShapeDtypeStruct((rows_here, model), f32),
        ),
        grid_spec=pltpu.PrefetchScalarGridSpec(
            num_scalar_prefetch=1,
            grid=(pages,),
            in_specs=[
                page_rows(model),
                page_block(8, PAGE),
                whole((3, model)),
                whole((model, 2)),
                whole((heads * 2 * bins, 2 * bins)),
                ANYWHERE,
            ],
            out_specs=(page_block(3, model, PAGE), page_block(heads, PAGE, PAGE), page_block(heads, 1, PAGE), page_block(model, PAGE), page_rows(model)),
            scratch_shapes=weight_scratch(shards, own, model)
            + [
                pltpu.VMEM((heads * 2 * bins, PAGE), bf16),
                pltpu.VMEM((2, PAGE, PAGE), f32),
            ],
        ),
        compiler_params=PARAMS,
        name="attention_forward",
    )(counts, inputs, meta, rows_one, bias, toep, gathered)


def feed_forward(counts, place, hidden, cotangent, rows_two, up_bias, up_all, down_all):
    rows_here, model = hidden.shape
    pages = rows_here // PAGE
    shards, _, hidden_units = up_all.shape
    return pl.pallas_call(
        mlp_kernel,
        out_shape=(
            jax.ShapeDtypeStruct((rows_here, model), bf16),
            jax.ShapeDtypeStruct((rows_here, model), f32),
            jax.ShapeDtypeStruct((model, hidden_units), bf16),
            jax.ShapeDtypeStruct((hidden_units, model), bf16),
            jax.ShapeDtypeStruct((8, model), f32),
            jax.ShapeDtypeStruct((1, hidden_units), f32),
        ),
        grid_spec=pltpu.PrefetchScalarGridSpec(
            num_scalar_prefetch=2,
            grid=(pages,),
            in_specs=[
                page_rows(model),
                page_rows(model),
                whole((3, model)),
                whole((shards, 1, hidden_units)),
                whole((shards, model, hidden_units)),
                whole((shards, hidden_units, model)),
            ],
            out_specs=(
                page_rows(model),
                page_rows(model),
                whole((model, hidden_units)),
                whole((hidden_units, model)),
                whole((8, model)),
                whole((1, hidden_units)),
            ),
            scratch_shapes=[
                pltpu.VMEM((model, hidden_units), f32),
                pltpu.VMEM((hidden_units, model), f32),
                pltpu.VMEM((PAGE, model), bf16),
                pltpu.VMEM((PAGE, model), bf16),
                pltpu.VMEM((PAGE, model), f32),
                pltpu.VMEM((PAGE, model), f32),
                pltpu.VMEM((shards, PAGE, hidden_units), bf16),
                pltpu.VMEM((shards, PAGE, hidden_units), bf16),
                pltpu.VMEM((2, PAGE, hidden_units), f32),
                pltpu.VMEM((2, PAGE, hidden_units), f32),
            ],
        ),
        compiler_params=PARAMS,
        name="feed_forward",
    )(counts, place, hidden, cotangent, rows_two, up_bias, up_all, down_all)


def attention_backward(counts, place, inputs, meta, rows_one, grad_hidden, qkv, probs, inverse, context, gathered):
    rows_here, model = inputs.shape
    pages, heads = probs.shape[:2]
    shards, _, own, _ = gathered.shape
    bins = 64
    return pl.pallas_call(
        backward_kernel,
        out_shape=(
            jax.ShapeDtypeStruct((rows_here, model), bf16),
            jax.ShapeDtypeStruct((4 * own, model), bf16),
            jax.ShapeDtypeStruct((8, model), f32),
            jax.ShapeDtypeStruct((3 * own, BLOCK), f32),
            jax.ShapeDtypeStruct((own // HEAD_DIM, 2 * bins, 2 * bins), f32),
        ),
        grid_spec=pltpu.PrefetchScalarGridSpec(
            num_scalar_prefetch=2,
            grid=(pages,),
            in_specs=[
                page_rows(model),
                page_block(8, PAGE),
                whole((3, model)),
                page_rows(model),
                page_block(3, model, PAGE),
                page_block(heads, PAGE, PAGE),
                page_block(heads, 1, PAGE),
                page_block(model, PAGE),
                ANYWHERE,
            ],
            out_specs=(
                page_rows(model),
                whole((4 * own, model)),
                whole((8, model)),
                whole((3 * own, BLOCK)),
                whole((own // HEAD_DIM, 2 * bins, 2 * bins)),
            ),
            scratch_shapes=weight_scratch(shards, own, model)
            + [
                pltpu.VMEM((3, model, PAGE), bf16),
                pltpu.VMEM((model, PAGE), f32),
                pltpu.VMEM((2, PAGE, PAGE), f32),
                pltpu.VMEM((2, PAGE, PAGE), bf16),
                pltpu.VMEM((4 * own, model), f32),
            ],
        ),
        compiler_params=PARAMS,
        name="attention_backward",
    )(counts, place, inputs, meta, rows_one, grad_hidden, qkv, probs, inverse, context, gathered)


def neighbours(axis):
    core = axis % 2
    side_x = (axis // 2) % 2
    side_y = (axis // 4) % 2
    to_core = 1 - 2 * core
    to_x = 2 - 4 * side_x
    to_y = 4 - 8 * side_y
    return core, side_x, side_y, to_core, to_x, to_y


KIND_Z, KIND_X, KIND_Y, KIND_VIA_X, KIND_VIA_Y, KIND_CORE = 0, 1, 2, 3, 4, 5
KINDS = 9


def flipped(index, mask):
    result, bit = index, 1
    while bit <= mask:
        if mask & bit:
            result = result + bit - 2 * bit * ((index // bit) % 2)
        bit *= 2
    return result


def gather_kernel(shards, *refs):
    arrays = 3
    sources, small = refs[0:arrays], refs[arrays]
    targets, small_target = refs[arrays + 1 : 2 * arrays + 1], refs[2 * arrays + 1]
    local_sem, send_sem, recv_sem, bounce = refs[2 * arrays + 2 :]
    place = lax.axis_index("tensor")
    lane = lax.axis_index("dp")
    core, side_x, side_y, to_core, to_x, to_y = neighbours(lane)
    mine = lane % 8
    rows = sources[0].shape[0] // 8
    half = rows // 2

    def piece(index, start=0, size=rows):
        return pl.ds(pl.multiple_of(index * rows + start, 16), size)

    def remote(kind, array, hop, source, target, dp, tensor):
        return pltpu.make_async_remote_copy(
            src_ref=source,
            dst_ref=target,
            send_sem=send_sem.at[kind, array, hop - 1],
            recv_sem=recv_sem.at[kind, array, hop - 1],
            device_id={"dp": dp, "tensor": tensor},
            device_id_type=pl.DeviceIdType.MESH,
        )

    def within(kind, array, hop, region, step):
        ref = targets[array].at[flipped(place, hop), region]
        return remote(kind, array, hop, ref, ref, lane + step, place)

    def along(array, hop):
        if array == arrays:
            source, target = small, small_target.at[place]
        else:
            source, target = sources[array].at[piece(mine)], targets[array].at[place, piece(mine)]
        return remote(KIND_Z, array, hop, source, target, lane, flipped(place, hop))

    hops = range(1, shards)
    barrier = pltpu.get_barrier_semaphore()
    for step in (to_core, to_x, to_y):
        pl.semaphore_signal(
            barrier, inc=1, device_id={"dp": lane + step, "tensor": place}, device_id_type=pl.DeviceIdType.MESH
        )
    for hop in hops:
        pl.semaphore_signal(
            barrier,
            inc=1,
            device_id={"dp": lane, "tensor": flipped(place, hop)},
            device_id_type=pl.DeviceIdType.MESH,
        )
    pl.semaphore_wait(barrier, 3 + len(hops))

    for array in (arrays, 0, 1, 2):
        for hop in hops:
            along(array, hop).start()
    loads = [pltpu.make_async_copy(sources[array], bounce.at[array], local_sem.at[array]) for array in range(arrays)]
    stores = [
        pltpu.make_async_copy(bounce.at[array], targets[array].at[place], local_sem.at[arrays + array])
        for array in range(arrays)
    ] + [pltpu.make_async_copy(small, small_target.at[place], local_sem.at[2 * arrays])]
    for copy in loads:
        copy.start()
    for copy in loads:
        copy.wait()
    for copy in stores:
        copy.start()

    def arrive(array, hop):
        along(array, hop).wait_recv()
        within(KIND_X, array, hop, piece(mine), to_x).start()
        within(KIND_Y, array, hop, piece(mine), to_y).start()
        within(KIND_CORE, array, hop, piece(mine), to_core).start()

    def spread_near(array, hop):
        at = mine + to_x
        within(KIND_X, array, hop, piece(at), to_x).wait_recv()
        within(KIND_VIA_Y, array, hop, piece(at, 0, half), to_y).start()
        within(KIND_CORE + 1, array, hop, piece(at), to_core).start()
        at = mine + to_y
        within(KIND_Y, array, hop, piece(at), to_y).wait_recv()
        within(KIND_VIA_X, array, hop, piece(at, half, half), to_x).start()
        within(KIND_CORE + 2, array, hop, piece(at), to_core).start()

    def spread_far(array, hop):
        at = mine + to_x + to_y
        within(KIND_VIA_Y, array, hop, piece(at, 0, half), to_y).wait_recv()
        within(KIND_VIA_X, array, hop, piece(at, half, half), to_x).wait_recv()
        within(KIND_CORE + 3, array, hop, piece(at), to_core).start()

    def finish(array, hop):
        for index, shift in enumerate((0, to_x, to_y, to_x + to_y)):
            within(KIND_CORE + index, array, hop, piece(mine + to_core + shift), to_core).wait_recv()

    def drain(array, hop):
        along(array, hop).wait_send()
        if array == arrays:
            along(array, hop).wait_recv()
            return
        within(KIND_X, array, hop, piece(mine), to_x).wait_send()
        within(KIND_Y, array, hop, piece(mine), to_y).wait_send()
        within(KIND_VIA_Y, array, hop, piece(mine + to_x, 0, half), to_y).wait_send()
        within(KIND_VIA_X, array, hop, piece(mine + to_y, half, half), to_x).wait_send()
        for index, shift in enumerate((0, to_x, to_y, to_x + to_y)):
            within(KIND_CORE + index, array, hop, piece(mine + shift), to_core).wait_send()

    items = [(array, hop) for array in range(arrays) for hop in hops]
    stages = (arrive, spread_near, spread_far, finish)
    for tick in range(len(items) + len(stages) - 1):
        for stage, act in enumerate(stages):
            if 0 <= tick - stage < len(items):
                act(*items[tick - stage])
    for array in range(arrays + 1):
        for hop in hops:
            drain(array, hop)
    for copy in stores:
        copy.wait()


def gather_weights(shards, pack, up, down, small):
    rows, model = pack.shape
    arrays = 3
    whole_array = jax.ShapeDtypeStruct((shards, rows, model), bf16)
    return pl.pallas_call(
        functools.partial(gather_kernel, shards),
        out_shape=(whole_array,) * arrays + (jax.ShapeDtypeStruct((shards,) + small.shape, f32),),
        in_specs=[ANYWHERE] * (arrays + 1),
        out_specs=(ANYWHERE,) * (arrays + 1),
        scratch_shapes=[
            pltpu.SemaphoreType.DMA((2 * arrays + 1,)),
            pltpu.SemaphoreType.DMA((KINDS, arrays + 1, shards - 1)),
            pltpu.SemaphoreType.DMA((KINDS, arrays + 1, shards - 1)),
            pltpu.VMEM((arrays, rows, model), bf16),
        ],
        compiler_params=pltpu.CompilerParams(
            collective_id=0, has_side_effects=True, vmem_limit_bytes=VMEM_LIMIT
        ),
        name="gather_weights",
    )(pack, up, down, small)


def reduce_kernel(bits, arrays, *refs):
    parts, small = refs[0:arrays], refs[arrays]
    sums, small_sum = refs[arrays + 1 : 2 * arrays + 1], refs[2 * arrays + 1]
    (
        got_core,
        got_one,
        got_two,
        got_more,
        kept_core,
        kept_one,
        small_got,
        send_sem,
        recv_sem,
        small_send,
        small_recv,
    ) = refs[2 * arrays + 2 :]
    place = lax.axis_index("tensor")
    lane = lax.axis_index("dp")
    core, side_x, side_y, to_core, to_x, to_y = neighbours(lane)
    steps = [to_core, to_x, to_y]
    for bit in range(3, bits):
        size = 2**bit
        steps.append(size - 2 * size * ((lane // size) % 2))
    rows = parts[0].shape[0]
    quarter, eighth, sixteenth = rows // 4, rows // 8, rows // 16

    barrier = pltpu.get_barrier_semaphore()
    for step in steps:
        pl.semaphore_signal(
            barrier, inc=1, device_id={"dp": lane + step, "tensor": place}, device_id_type=pl.DeviceIdType.MESH
        )
    pl.semaphore_wait(barrier, len(steps))

    def remote(stage, array, side, source, target, step):
        return pltpu.make_async_remote_copy(
            src_ref=source,
            dst_ref=target,
            send_sem=send_sem.at[stage, array, side],
            recv_sem=recv_sem.at[stage, array, side],
            device_id={"dp": lane + step, "tensor": place},
            device_id_type=pl.DeviceIdType.MESH,
        )

    def span(side, of_core, one=None, two=None):
        start = side * (rows // 2) + of_core * quarter
        if one is None:
            return pl.ds(pl.multiple_of(start, 16), quarter)
        start = start + one * eighth
        if two is None:
            return pl.ds(pl.multiple_of(start, 16), eighth)
        return pl.ds(pl.multiple_of(start + two * sixteenth, 16), sixteenth)

    order = ((side_x, side_y, to_x, to_y), (side_y, side_x, to_y, to_x))
    sides = range(2)

    def small_copy(bit):
        return pltpu.make_async_remote_copy(
            src_ref=small if bit == 0 else small_got.at[bits + bit - 1],
            dst_ref=small_got.at[bit],
            send_sem=small_send.at[bit],
            recv_sem=small_recv.at[bit],
            device_id={"dp": lane + steps[bit], "tensor": place},
            device_id_type=pl.DeviceIdType.MESH,
        )

    def core_copy(array, side):
        return remote(
            0, array, side, parts[array].at[span(side, 1 - core)], got_core.at[array, side], to_core
        )

    def one_copy(array, side):
        one, two, to_one, to_two = order[side]
        region = pl.ds(pl.multiple_of((1 - one) * eighth, 16), eighth)
        return remote(1, array, side, kept_core.at[array, side, region], got_one.at[array, side], to_one)

    def two_copy(array, side):
        one, two, to_one, to_two = order[side]
        region = pl.ds(pl.multiple_of((1 - two) * sixteenth, 16), sixteenth)
        return remote(2, array, side, kept_one.at[array, side, region], got_two.at[array, side], to_two)

    def more_copy(array, side, bit):
        source = got_more.at[bit - 3, array, side]
        return remote(bit + 3, array, side, source, got_more.at[bits - 3 + bit - 3, array, side], steps[bit])

    def back_copy(stage, array, side, inward):
        one, two, to_one, to_two = order[side]
        if stage == 3:
            region, step = span(side, core, one, two if not inward else 1 - two), to_two
        elif stage == 4:
            region, step = span(side, core, one if not inward else 1 - one), to_one
        else:
            region, step = span(side, core if not inward else 1 - core), to_core
        ref = sums[array].at[region]
        return remote(stage, array, side, ref, ref, step)

    for array in range(arrays):
        for side in sides:
            core_copy(array, side).start()
    for array in range(arrays):
        for side in sides:
            keep = span(side, core)
            core_copy(array, side).wait_recv()
            kept_core[array, side] = (
                parts[array][keep, :].astype(f32) + got_core[array, side].astype(f32)
            ).astype(bf16)
            one_copy(array, side).start()
    small_copy(0).start()
    for array in range(arrays):
        for side in sides:
            one, two, to_one, to_two = order[side]
            region = pl.ds(pl.multiple_of(one * eighth, 16), eighth)
            one_copy(array, side).wait_recv()
            kept_one[array, side] = (
                kept_core[array, side, region, :].astype(f32) + got_one[array, side].astype(f32)
            ).astype(bf16)
            two_copy(array, side).start()
    for bit in range(bits):
        small_copy(bit).wait()
        if bit == 0:
            small_got[bits] = small[...] + small_got[0]
        else:
            small_got[bits + bit] = small_got[bits + bit - 1] + small_got[bit]
        if bit + 1 < bits:
            small_copy(bit + 1).start()
    for array in range(arrays):
        for side in sides:
            one, two, to_one, to_two = order[side]
            keep = span(side, core, one, two)
            region = pl.ds(pl.multiple_of(two * sixteenth, 16), sixteenth)
            two_copy(array, side).wait_recv()
            total = (
                kept_one[array, side, region, :].astype(f32) + got_two[array, side].astype(f32)
            ).astype(bf16)
            for bit in range(3, bits):
                got_more[bit - 3, array, side] = total
                more_copy(array, side, bit).start()
                more_copy(array, side, bit).wait()
                total = (total.astype(f32) + got_more[bits - 3 + bit - 3, array, side].astype(f32)).astype(bf16)
            sums[array][keep, :] = total
            back_copy(3, array, side, False).start()
    for stage in (3, 4, 5):
        for array in range(arrays):
            for side in sides:
                back_copy(stage, array, side, True).wait_recv()
                if stage < 5:
                    back_copy(stage + 1, array, side, False).start()
    small_sum[...] = small_got[2 * bits - 1]
    for array in range(arrays):
        for side in sides:
            core_copy(array, side).wait_send()
            one_copy(array, side).wait_send()
            two_copy(array, side).wait_send()
            for stage in (3, 4, 5):
                back_copy(stage, array, side, False).wait_send()


def reduce_grads(devices, parts, small):
    arrays = len(parts)
    rows, model = parts[0].shape
    bits = devices.bit_length() - 1
    vmem = pl.BlockSpec(memory_space=pltpu.VMEM)
    more = max(2 * (bits - 3), 1)
    return pl.pallas_call(
        functools.partial(reduce_kernel, bits, arrays),
        out_shape=tuple(jax.ShapeDtypeStruct(part.shape, bf16) for part in parts)
        + (jax.ShapeDtypeStruct(small.shape, f32),),
        in_specs=[vmem] * (arrays + 1),
        out_specs=(vmem,) * (arrays + 1),
        scratch_shapes=[
            pltpu.VMEM((arrays, 2, rows // 4, model), bf16),
            pltpu.VMEM((arrays, 2, rows // 8, model), bf16),
            pltpu.VMEM((arrays, 2, rows // 16, model), bf16),
            pltpu.VMEM((more, arrays, 2, rows // 16, model), bf16),
            pltpu.VMEM((arrays, 2, rows // 4, model), bf16),
            pltpu.VMEM((arrays, 2, rows // 8, model), bf16),
            pltpu.VMEM((2 * bits,) + small.shape, f32),
            pltpu.SemaphoreType.DMA((bits + 3, arrays, 2)),
            pltpu.SemaphoreType.DMA((bits + 3, arrays, 2)),
            pltpu.SemaphoreType.DMA((bits,)),
            pltpu.SemaphoreType.DMA((bits,)),
        ],
        compiler_params=pltpu.CompilerParams(
            collective_id=1, has_side_effects=True, vmem_limit_bytes=VMEM_LIMIT
        ),
        name="reduce_grads",
    )(*parts, small)


def on_device(
    inputs,
    cotangent,
    counts,
    keep_mask,
    box_x,
    box_y,
    gain_one,
    shift_one,
    w_qkv,
    b_qv,
    w_out,
    b_out,
    gain_two,
    shift_two,
    w_up,
    b_up,
    w_down,
    b_down,
    rel_tables,
    *,
    devices,
):
    rows_here, model = inputs.shape
    pages = rows_here // PAGE
    own_heads, bins = rel_tables.shape[1:]
    own = own_heads * HEAD_DIM
    shards = model // own
    heads = own_heads * shards
    hidden_units = w_up.shape[1]
    place = lax.axis_index("tensor").astype(jnp.int32).reshape(1)

    pack = jnp.concatenate([w_qkv.transpose(0, 2, 1).reshape(3 * own, model), w_out], axis=0)
    small = jnp.concatenate([b_qv.reshape(-1), rel_tables.reshape(-1), b_up]).reshape(-1, model)
    small = jnp.pad(small, ((0, 8 - small.shape[0]), (0, 0)))
    gathered, up_all, down_all, small_all = gather_weights(shards, pack, w_up, w_down, small)
    gathered = gathered.reshape(shards, 4, own, model)
    bias_all = small_all[:, 0, 0 : 2 * own].reshape(shards, 2, own).transpose(0, 2, 1).reshape(model, 2)
    tables_all = small_all[:, 0, 2 * own : 2 * own + 2 * own_heads * bins]
    tables_all = tables_all.reshape(shards, 2, own_heads, bins).transpose(1, 0, 2, 3).reshape(2, heads, bins)
    up_bias = small_all[:, 1:2, :]

    toep = (toeplitz(tables_all) * LOG2E).astype(bf16).reshape(heads * 2 * bins, 2 * bins)
    meta = jnp.stack(
        [keep_mask.reshape(pages, PAGE), box_x.reshape(pages, PAGE), box_y.reshape(pages, PAGE)], axis=1
    )
    meta = jnp.pad(meta, ((0, 0), (0, 5), (0, 0)))
    rows_one = jnp.stack([gain_one, shift_one, b_out])
    rows_two = jnp.stack([gain_two, shift_two, b_down])

    qkv, probs, inverse, context, hidden = attention_forward(
        counts, inputs, meta, rows_one, bias_all, toep, gathered
    )
    out, grad_hidden, grad_up, grad_down, sums_two, grad_b_up = feed_forward(
        counts, place, hidden, cotangent, rows_two, up_bias, up_all, down_all
    )
    grad_input, grad_pack, sums_one, grad_bias, levels_grad = attention_backward(
        counts, place, inputs, meta, rows_one, grad_hidden, qkv, probs, inverse, context, gathered
    )

    grad_tables = fold_levels(levels_grad, bins)
    bias_sums = jnp.sum(grad_bias, axis=1).reshape(3, own)
    grad_b_qv = jnp.stack([bias_sums[0], bias_sums[2]])

    small = jnp.concatenate(
        [
            sums_one[0:2],
            sums_two[0:4],
            grad_b_up,
            jnp.concatenate([grad_b_qv.reshape(-1), grad_tables.reshape(-1)]).reshape(1, model),
        ]
    )
    grad_pack, grad_up, grad_down, small = reduce_grads(devices, (grad_pack, grad_up, grad_down), small)
    grad_pack, grad_up, grad_down = (part.astype(f32) for part in (grad_pack, grad_up, grad_down))
    sums_one, sums_two, grad_b_up = small[0:2], small[2:6], small[6]
    grad_b_qv = small[7, 0 : 2 * own].reshape(2, own)
    grad_tables = small[7, 2 * own :].reshape(2, own_heads, bins)
    grad_w_qkv = grad_pack[0 : 3 * own].reshape(3, own, model).transpose(0, 2, 1)
    return (
        out,
        grad_input,
        grad_w_qkv,
        grad_b_qv,
        grad_pack[3 * own :],
        sums_two[2],
        sums_one[0],
        sums_one[1],
        sums_two[0],
        sums_two[1],
        grad_up,
        grad_b_up.reshape(-1),
        grad_down,
        sums_two[3],
        grad_tables,
    )


def solution(mesh):
    placed = (
        P("dp", None),
        P("dp", None),
        P("dp"),
        P("dp"),
        P("dp"),
        P("dp"),
        P(),
        P(),
        P(None, None, "tensor"),
        P(None, "tensor"),
        P("tensor", None),
        P(),
        P(),
        P(),
        P(None, "tensor"),
        P("tensor"),
        P("tensor", None),
        P(),
        P(None, "tensor", None),
    )
    return jax.shard_map(
        functools.partial(on_device, devices=mesh.shape["dp"]),
        mesh=mesh,
        in_specs=placed,
        out_specs=(
            P("dp", None),
            P("dp", None),
            P(None, None, "tensor"),
            P(None, "tensor"),
            P("tensor", None),
            P(),
            P(),
            P(),
            P(),
            P(),
            P(None, "tensor"),
            P("tensor"),
            P("tensor", None),
            P(),
            P(None, "tensor", None),
        ),
        check_vma=False,
    )
```

```python
import functools
import jax
import jax.numpy as jnp
from jax import lax
from jax.experimental import pallas as pl
from jax.experimental.pallas import tpu as pltpu
from jax.sharding import PartitionSpec as P

HEAD_DIM = 64
PAGE = 512
BLOCK = 128
epsilon = 1e-05
masked_score = -1e30
LOG2E = 1.4426950408889634
LN2 = 0.6931471805599453
bf16 = jnp.bfloat16
f32 = jnp.float32
VMEM_LIMIT = 60 << 20


def dot(left, right, left_dim, right_dim):
    return lax.dot_general(
        left, right, (((left_dim,), (right_dim,)), ((), ())), preferred_element_type=f32
    )


def nn(left, right):
    return dot(left, right, 1, 0)


def nt(left, right):
    return dot(left, right, 1, 1)


def tn(left, right):
    return dot(left, right, 0, 0)


def norm_parts(rows):
    average = jnp.mean(rows, axis=-1, keepdims=True)
    centered = rows - average
    variance = jnp.mean(centered * centered, axis=-1, keepdims=True)
    inverse = lax.rsqrt(variance + epsilon)
    return centered * inverse, inverse


def norm_grad(grad_out, xhat, inverse, gain):
    scaled = grad_out * gain
    mean_one = jnp.mean(scaled, axis=-1, keepdims=True)
    mean_two = jnp.mean(scaled * xhat, axis=-1, keepdims=True)
    return inverse * (scaled - mean_one - xhat * mean_two)


def one_hot_columns(box_x_ref, box_y_ref, bins, reverse=False):
    width = box_x_ref.shape[-1]
    levels = lax.broadcasted_iota(jnp.int32, (bins, width), 0)
    if reverse:
        levels = (bins - 1) - levels
    hot_x = jnp.where(levels == box_x_ref[0], 1.0, 0.0)
    hot_y = jnp.where(levels == box_y_ref[0], 1.0, 0.0)
    return jnp.concatenate([hot_x, hot_y], axis=0).astype(bf16)


def by_halves(count, body):
    half = PAGE // 2
    pl.when(count <= half)(functools.partial(body, half))
    pl.when(count > half)(functools.partial(body, PAGE))


def neighbours(axis):
    core = axis % 2
    side_x = (axis // 2) % 2
    side_y = (axis // 4) % 2
    return core, side_x, side_y, 1 - 2 * core, 2 - 4 * side_x, 4 - 8 * side_y


def flipped(index, mask):
    result, bit = index, 1
    while bit <= mask:
        if mask & bit:
            result = result + bit - 2 * bit * ((index // bit) % 2)
        bit *= 2
    return result


def greet(peers):
    barrier = pltpu.get_barrier_semaphore()
    for dp, tensor in peers:
        pl.semaphore_signal(
            barrier, inc=1, device_id={"dp": dp, "tensor": tensor}, device_id_type=pl.DeviceIdType.MESH
        )
    pl.semaphore_wait(barrier, len(peers))


KIND_Z, KIND_X, KIND_Y, KIND_VIA_X, KIND_VIA_Y, KIND_CORE = 0, 1, 2, 3, 4, 5
KINDS = 9


def gather_steps(shards, sources, targets, small_sources, small_targets, send_sem, recv_sem):
    arrays = len(sources)
    place = lax.axis_index("tensor")
    lane = lax.axis_index("dp")
    core, side_x, side_y, to_core, to_x, to_y = neighbours(lane)
    mine = lane % 8
    rows = targets[0].shape[1] // 8
    half = rows // 2
    hops = range(1, shards)

    def piece(index, start=0, size=rows):
        return pl.ds(pl.multiple_of(index * rows + start, 16), size)

    def remote(kind, array, hop, source, target, dp, tensor):
        return pltpu.make_async_remote_copy(
            src_ref=source,
            dst_ref=target,
            send_sem=send_sem.at[kind, array, hop - 1],
            recv_sem=recv_sem.at[kind, array, hop - 1],
            device_id={"dp": dp, "tensor": tensor},
            device_id_type=pl.DeviceIdType.MESH,
        )

    def within(kind, array, hop, region, step):
        ref = targets[array].at[flipped(place, hop), region]
        return remote(kind, array, hop, ref, ref, lane + step, place)

    def along(array, hop):
        source, target = sources[array].at[piece(mine)], targets[array].at[place, piece(mine)]
        return remote(KIND_Z, array, hop, source, target, lane, flipped(place, hop))

    def along_small(index, hop):
        source, target = small_sources[index], small_targets[index].at[place]
        return remote(1 + index, arrays, hop, source, target, lane, flipped(place, hop))

    def enter():
        greet(
            [(lane + step, place) for step in (to_core, to_x, to_y)] + [(lane, flipped(place, hop)) for hop in hops]
        )

    def begin():
        for array in range(arrays):
            for hop in hops:
                along(array, hop).start()
            if array == 0:
                for index in range(len(small_sources)):
                    for hop in hops:
                        along_small(index, hop).start()

    def arrive(array, hop):
        along(array, hop).wait_recv()
        within(KIND_X, array, hop, piece(mine), to_x).start()
        within(KIND_Y, array, hop, piece(mine), to_y).start()
        within(KIND_CORE, array, hop, piece(mine), to_core).start()

    def spread_near(array, hop):
        at = mine + to_x
        within(KIND_X, array, hop, piece(at), to_x).wait_recv()
        within(KIND_VIA_Y, array, hop, piece(at, 0, half), to_y).start()
        within(KIND_CORE + 1, array, hop, piece(at), to_core).start()
        at = mine + to_y
        within(KIND_Y, array, hop, piece(at), to_y).wait_recv()
        within(KIND_VIA_X, array, hop, piece(at, half, half), to_x).start()
        within(KIND_CORE + 2, array, hop, piece(at), to_core).start()

    def spread_far(array, hop):
        at = mine + to_x + to_y
        within(KIND_VIA_Y, array, hop, piece(at, 0, half), to_y).wait_recv()
        within(KIND_VIA_X, array, hop, piece(at, half, half), to_x).wait_recv()
        within(KIND_CORE + 3, array, hop, piece(at), to_core).start()

    def finish(array, hop):
        for index, shift in enumerate((0, to_x, to_y, to_x + to_y)):
            within(KIND_CORE + index, array, hop, piece(mine + to_core + shift), to_core).wait_recv()

    def drain():
        for hop in hops:
            for index in range(len(small_sources)):
                along_small(index, hop).wait()
            for array in range(arrays):
                along(array, hop).wait_send()
                within(KIND_X, array, hop, piece(mine), to_x).wait_send()
                within(KIND_Y, array, hop, piece(mine), to_y).wait_send()
                within(KIND_VIA_Y, array, hop, piece(mine + to_x, 0, half), to_y).wait_send()
                within(KIND_VIA_X, array, hop, piece(mine + to_y, half, half), to_x).wait_send()
                for index, shift in enumerate((0, to_x, to_y, to_x + to_y)):
                    within(KIND_CORE + index, array, hop, piece(mine + shift), to_core).wait_send()

    items = [(array, hop) for array in range(arrays) for hop in hops]
    stages = (arrive, spread_near, spread_far, finish)

    def tick(at):
        for stage, act in enumerate(stages):
            if 0 <= at - stage < len(items):
                act(*items[at - stage])

    return enter, begin, tick, len(items) + len(stages) - 1, drain


def gather_semaphores(arrays, shards):
    return [pltpu.SemaphoreType.DMA((KINDS, arrays + 1, shards - 1))] * 2


def gather_first_kernel(shards, *refs):
    qkv, out, bias, tables, up_bias = refs[0:5]
    target, bias_all, tables_all, up_bias_all = refs[5:9]
    local_sem, send_sem, recv_sem, bounce = refs[9:]
    place = lax.axis_index("tensor")
    split = qkv.shape[0]
    loads = [
        pltpu.make_async_copy(qkv, bounce.at[0:split], local_sem.at[0]),
        pltpu.make_async_copy(out, bounce.at[split:], local_sem.at[1]),
    ]
    smalls, small_targets = (bias, tables, up_bias), (bias_all, tables_all, up_bias_all)
    stores = [pltpu.make_async_copy(bounce, target.at[place], local_sem.at[2])] + [
        pltpu.make_async_copy(source, into.at[place], local_sem.at[3 + index])
        for index, (source, into) in enumerate(zip(smalls, small_targets))
    ]
    for copy in loads:
        copy.start()
    enter, begin, tick, ticks, drain = gather_steps(
        shards, (bounce,), (target,), smalls, small_targets, send_sem, recv_sem
    )
    enter()
    for copy in loads:
        copy.wait()
    begin()
    for copy in stores:
        copy.start()
    for at in range(ticks):
        tick(at)
    drain()
    for copy in stores:
        copy.wait()


def forward_kernel(
    shards,
    counts_ref,
    x_ref,
    keep_ref,
    box_x_ref,
    box_y_ref,
    gain_ref,
    shift_ref,
    out_bias_ref,
    bias_ref,
    tables_ref,
    gathered_ref,
    up_ref,
    down_ref,
    qkv_ref,
    probs_ref,
    inverse_ref,
    context_ref,
    hidden_ref,
    up_all_ref,
    down_all_ref,
    weights,
    copy_sem,
    bounce,
    send_sem,
    recv_sem,
    bias_columns,
    toeplitz,
    spread,
    scores,
):
    page = pl.program_id(0)
    pages = counts_ref.shape[0]
    place = lax.axis_index("tensor")
    width, model = x_ref.shape
    heads = model // HEAD_DIM
    own = model // shards
    own_heads = heads // shards
    bins = tables_ref.shape[-1]
    enter, begin, tick, ticks, drain = gather_steps(
        shards, (up_ref, down_ref), (up_all_ref, down_all_ref), (), (), send_sem, recv_sem
    )
    weight_copies = [
        pltpu.make_async_copy(gathered_ref.at[:, kind], weights.at[kind], copy_sem.at[kind]) for kind in range(4)
    ]
    loads = [
        pltpu.make_async_copy(source, bounce.at[index], copy_sem.at[4 + index])
        for index, source in enumerate((up_ref, down_ref))
    ]
    stores = [
        pltpu.make_async_copy(bounce.at[index], target.at[place], copy_sem.at[6 + index])
        for index, target in enumerate((up_all_ref, down_all_ref))
    ]

    @pl.when(page == 0)
    def _():
        for copy in weight_copies:
            copy.start()
        enter()
        begin()
        for copy in loads:
            copy.start()
        for shard in range(shards):
            rows = slice(shard * own, (shard + 1) * own)
            for kind in range(2):
                wide = jnp.broadcast_to(bias_ref[shard, kind : kind + 1, :], (128, own))
                bias_columns[kind, rows, :] = wide.T
        m = lax.broadcasted_iota(jnp.int32, (bins, 2 * bins), 1)
        signed = jnp.where(m >= bins, 2 * bins - m, -m)
        level = lax.broadcasted_iota(jnp.int32, (bins, 2 * bins), 0)
        pick = jnp.where(jnp.clip(signed, -(bins // 2), bins // 2 - 1) + bins // 2 == level, 1.0, 0.0).astype(bf16)
        lane = lax.broadcasted_iota(jnp.int32, (bins, 2 * bins), 1)
        for shard in range(shards):
            for one in range(own_heads):
                at = (shard * own_heads + one) * 2 * bins
                for kind in range(2):
                    table = (tables_ref[shard, kind, one : one + 1, :] * LOG2E).astype(bf16)
                    line = nn(jnp.broadcast_to(table, (bins, bins)), pick)
                    rolled = pltpu.roll(line, kind * bins, 1, stride=1, stride_axis=0)
                    inside = lane >= bins if kind else lane < bins
                    toeplitz[at + kind * bins : at + (kind + 1) * bins, :] = jnp.where(inside, rolled, 0.0).astype(bf16)
        for copy in loads:
            copy.wait()
        for copy in stores:
            copy.start()
        for copy in weight_copies:
            copy.wait()

    points = 5
    spacing = max(points * pages // (ticks + 1), 1)

    def point(index):
        for at in range(ticks):
            where = min((at + 1) * spacing - 1, points * pages - 1)
            if where % points == index:
                pl.when(page == where // points)(functools.partial(tick, at))

    tokens = x_ref[...].astype(f32)
    xhat, _ = norm_parts(tokens)
    low = (xhat * gain_ref[...] + shift_ref[...]).astype(bf16)
    for kind in range(3):
        product = nt(weights[kind].reshape(model, model), low)
        if kind == 0:
            product = (product + bias_columns[0, :, 0:1]) * (LOG2E * HEAD_DIM**-0.5)
        if kind == 2:
            product = product + bias_columns[1, :, 0:1]
        qkv_ref[0, kind] = product.astype(bf16)
    hot = one_hot_columns(box_x_ref, box_y_ref, bins)
    spread[...] = nn(toeplitz[...], hot).astype(bf16)
    lane = lax.broadcasted_iota(jnp.int32, (1, width), 1)
    open_key = (lane < counts_ref[page]) & (keep_ref[0] == 1)
    mask_row = jnp.where(open_key, 0.0, masked_score)
    first = lax.broadcasted_iota(jnp.int32, (HEAD_DIM, width), 0) == 0
    key_pad = jnp.where(first, mask_row, 0.0).astype(bf16)
    query_pad = jnp.where(first, 1.0, 0.0).astype(bf16)
    ones = jnp.ones((16, width), bf16)
    eye = lax.broadcasted_iota(jnp.int32, (BLOCK, BLOCK), 0) == lax.broadcasted_iota(jnp.int32, (BLOCK, BLOCK), 1)

    def score(index, slot):
        rows = slice(index * HEAD_DIM, (index + 1) * HEAD_DIM)
        query = qkv_ref[0, 0, rows]
        key = qkv_ref[0, 1, rows]
        bias = spread[index * 2 * bins : (index + 1) * 2 * bins, :]
        left = jnp.concatenate([key, key_pad, hot], axis=0)
        right = jnp.concatenate([query, query_pad, bias], axis=0)
        scores[slot] = tn(left, right)
        return jnp.sum(query.astype(f32) * key.astype(f32), axis=0, keepdims=True) + jnp.sum(
            bias.astype(f32) * hot.astype(f32), axis=0, keepdims=True
        )

    def soften(index, slot, own_score):
        for at in range(width // BLOCK):
            span = slice(at * BLOCK, (at + 1) * BLOCK)
            scores[slot, span, span] = jnp.where(eye, own_score[:, span], scores[slot, span, span])
        top = jnp.max(scores[slot], axis=0, keepdims=True)
        probs_ref[0, index] = jnp.exp2(scores[slot] - top).astype(bf16)

    def mix(index):
        rows = slice(index * HEAD_DIM, (index + 1) * HEAD_DIM)
        mixed = nn(jnp.concatenate([qkv_ref[0, 2, rows], ones], axis=0), probs_ref[0, index])
        inverse = 1.0 / mixed[HEAD_DIM : HEAD_DIM + 1]
        inverse_ref[0, index] = inverse
        context_ref[0, rows] = (mixed[0:HEAD_DIM] * inverse).astype(bf16)

    point(0)
    owns = [score(0, 0)]
    for at in range(heads):
        if at + 1 < heads:
            owns.append(score(at + 1, (at + 1) % 2))
        soften(at, at % 2, owns[at])
        if at > 0:
            mix(at - 1)
        if at % 3 == 2 and at + 1 < heads:
            point(1 + at // 3)
    mix(heads - 1)
    point(4)
    attended = tn(context_ref[0], weights[3].reshape(model, model))
    hidden_ref[...] = tokens + attended + out_bias_ref[...]

    @pl.when(page == pages - 1)
    def _():
        drain()
        for copy in stores:
            copy.wait()


def mlp_kernel(
    counts_ref,
    place_ref,
    hidden_ref,
    cotangent_ref,
    gain_ref,
    shift_ref,
    down_bias_ref,
    bias_ref,
    up_ref,
    down_ref,
    out_ref,
    grad_hidden_ref,
    grad_up_ref,
    grad_down_ref,
    sums_ref,
    up_total,
    down_total,
    low_ref,
    gl_ref,
    down_acc,
    gn_acc,
    act_ref,
    gu_ref,
    upper_ref,
    grad_ref,
):
    page = pl.program_id(0)
    shards = up_ref.shape[0]
    place = place_ref[0]

    @pl.when(page == 0)
    def _():
        up_total[...] = jnp.zeros_like(up_total)
        down_total[...] = jnp.zeros_like(down_total)
        sums_ref[...] = jnp.zeros_like(sums_ref)

    count = counts_ref[page]

    def body(width):
        valid = lax.broadcasted_iota(jnp.int32, (width, 1), 0) < count
        hidden = hidden_ref[0:width, :]
        xhat, inverse = norm_parts(hidden)
        low = (xhat * gain_ref[...] + shift_ref[...]).astype(bf16)
        grad_result = jnp.where(valid, cotangent_ref[0:width, :].astype(f32), 0.0)
        grad_low = grad_result.astype(bf16)

        low_ref[0:width, :] = low
        gl_ref[0:width, :] = grad_low
        down_acc[0:width, :] = jnp.zeros((width, hidden.shape[1]), f32)
        gn_acc[0:width, :] = jnp.zeros((width, hidden.shape[1]), f32)

        def lead(at, slot):
            upper_ref[slot, 0:width, :] = nn(low_ref[0:width, :], up_ref[at]) + bias_ref[at]
            grad_ref[slot, 0:width, :] = nt(gl_ref[0:width, :], down_ref[at])

        def bend(at, slot):
            upper = upper_ref[slot, 0:width, :]
            half = 0.5 * (1.0 + lax.erf(upper * 0.7071067811865476))
            density = jnp.exp(-0.5 * upper * upper) * 0.3989422804014327
            act_ref[at, 0:width, :] = (upper * half).astype(bf16)
            slope = half + upper * density
            gu_ref[at, 0:width, :] = (grad_ref[slot, 0:width, :] * slope).astype(bf16)

        def mix(at):
            down_acc[0:width, :] += nn(act_ref[at, 0:width, :], down_ref[at])
            gn_acc[0:width, :] += nt(gu_ref[at, 0:width, :], up_ref[at])

        lead(0, 0)
        for at in range(shards):
            if at + 1 < shards:
                lead(at + 1, (at + 1) % 2)
            bend(at, at % 2)
            if at > 0:
                mix(at - 1)
        mix(shards - 1)
        down_proj = down_acc[0:width, :]
        grad_normed = gn_acc[0:width, :]
        up_total[...] += tn(low_ref[0:width, :], gu_ref[place, 0:width, :])
        down_total[...] += tn(act_ref[place, 0:width, :], gl_ref[0:width, :])
        sums_ref[4:5, :] += jnp.sum(gu_ref[place, 0:width, :].astype(f32), axis=0, keepdims=True)
        result = jnp.where(valid, hidden + down_proj + down_bias_ref[...], 0.0)
        out_ref[0:width, :] = result.astype(bf16)
        grad_hidden = grad_result + norm_grad(grad_normed, xhat, inverse, gain_ref[...])
        grad_hidden_ref[0:width, :] = grad_hidden
        sums_ref[0:1, :] += jnp.sum(grad_normed * xhat, axis=0, keepdims=True)
        sums_ref[1:2, :] += jnp.sum(grad_normed, axis=0, keepdims=True)
        sums_ref[2:3, :] += jnp.sum(grad_hidden, axis=0, keepdims=True)
        sums_ref[3:4, :] += jnp.sum(grad_result, axis=0, keepdims=True)
        if width < PAGE:
            out_ref[width:PAGE, :] = jnp.zeros((PAGE - width, hidden.shape[1]), bf16)
            grad_hidden_ref[width:PAGE, :] = jnp.zeros((PAGE - width, hidden.shape[1]), f32)

    by_halves(count, body)

    @pl.when(page == pl.num_programs(0) - 1)
    def _():
        grad_up_ref[...] = up_total[...].astype(bf16)
        grad_down_ref[...] = down_total[...].astype(bf16)


def reduce_steps(bits, parts, sums, smalls, scratch):
    arrays = len(parts)
    got_core, got_one, got_two, got_more, kept_core, kept_one, send_sem, recv_sem = scratch[0:8]
    place = lax.axis_index("tensor")
    lane = lax.axis_index("dp")
    core, side_x, side_y, to_core, to_x, to_y = neighbours(lane)
    steps = [to_core, to_x, to_y]
    for bit in range(3, bits):
        size = 2**bit
        steps.append(size - 2 * size * ((lane // size) % 2))
    rows = parts[0].shape[0]
    quarter, eighth, sixteenth = rows // 4, rows // 8, rows // 16
    order = ((side_x, side_y, to_x, to_y), (side_y, side_x, to_y, to_x))
    sides = range(2)

    def device(step):
        return {"dp": lane + step, "tensor": place}

    def remote(stage, array, side, source, target, step):
        return pltpu.make_async_remote_copy(
            src_ref=source,
            dst_ref=target,
            send_sem=send_sem.at[stage, array, side],
            recv_sem=recv_sem.at[stage, array, side],
            device_id=device(step),
            device_id_type=pl.DeviceIdType.MESH,
        )

    def span(side, of_core, one=None, two=None):
        start = side * (rows // 2) + of_core * quarter
        if one is None:
            return pl.ds(pl.multiple_of(start, 16), quarter)
        start = start + one * eighth
        if two is None:
            return pl.ds(pl.multiple_of(start, 16), eighth)
        return pl.ds(pl.multiple_of(start + two * sixteenth, 16), sixteenth)

    def part_of(index, size):
        return pl.ds(pl.multiple_of(index * size, 16), size)

    def core_copy(array, side):
        return remote(0, array, side, parts[array].at[span(side, 1 - core)], got_core.at[array, side], to_core)

    def one_copy(array, side):
        one, two, to_one, to_two = order[side]
        source = kept_core.at[array, side, part_of(1 - one, eighth)]
        return remote(1, array, side, source, got_one.at[array, side], to_one)

    def two_copy(array, side):
        one, two, to_one, to_two = order[side]
        source = kept_one.at[array, side, part_of(1 - two, sixteenth)]
        return remote(2, array, side, source, got_two.at[array, side], to_two)

    def more_copy(array, side, bit):
        source = got_more.at[bit - 3, array, side]
        return remote(bit + 3, array, side, source, got_more.at[bits - 3 + bit - 3, array, side], steps[bit])

    def back_copy(stage, array, side, inward):
        one, two, to_one, to_two = order[side]
        if stage == 3:
            region, step = span(side, core, one, 1 - two if inward else two), to_two
        elif stage == 4:
            region, step = span(side, core, 1 - one if inward else one), to_one
        else:
            region, step = span(side, 1 - core if inward else core), to_core
        ref = sums[array].at[region]
        return remote(stage, array, side, ref, ref, step)

    def enter():
        greet([(lane + step, place) for step in steps])

    def begin():
        for array in range(arrays):
            for side in sides:
                core_copy(array, side).start()

    def add_core(array):
        for side in sides:
            keep = span(side, core)
            core_copy(array, side).wait_recv()
            kept_core[array, side] = (
                parts[array][keep, :].astype(f32) + got_core[array, side].astype(f32)
            ).astype(bf16)
            one_copy(array, side).start()

    def add_one(array):
        for side in sides:
            one, two, to_one, to_two = order[side]
            one_copy(array, side).wait_recv()
            kept_one[array, side] = (
                kept_core[array, side, part_of(one, eighth), :].astype(f32) + got_one[array, side].astype(f32)
            ).astype(bf16)
            two_copy(array, side).start()

    def add_two(array):
        for side in sides:
            one, two, to_one, to_two = order[side]
            two_copy(array, side).wait_recv()
            total = (
                kept_one[array, side, part_of(two, sixteenth), :].astype(f32) + got_two[array, side].astype(f32)
            ).astype(bf16)
            for bit in range(3, bits):
                got_more[bit - 3, array, side] = total
                more_copy(array, side, bit).start()
                more_copy(array, side, bit).wait()
                total = (total.astype(f32) + got_more[bits - 3 + bit - 3, array, side].astype(f32)).astype(bf16)
            sums[array][span(side, core, one, two), :] = total
            back_copy(3, array, side, False).start()

    def back(stage, array):
        for side in sides:
            back_copy(stage, array, side, True).wait_recv()
            if stage < 5:
                back_copy(stage + 1, array, side, False).start()

    def small_copy(index, bit):
        got, small_send, small_recv = scratch[8:11]
        source = smalls[index] if bit == 0 else got.at[index, bits + bit - 1]
        return pltpu.make_async_remote_copy(
            src_ref=source,
            dst_ref=got.at[index, bit],
            send_sem=small_send.at[index, bit],
            recv_sem=small_recv.at[index, bit],
            device_id=device(steps[bit]),
            device_id_type=pl.DeviceIdType.MESH,
        )

    def small_begin():
        for index in range(len(smalls)):
            small_copy(index, 0).start()

    def small_step(bit):
        got = scratch[8]
        for index in range(len(smalls)):
            small_copy(index, bit).wait()
            before = smalls[index][...] if bit == 0 else got[index, bits + bit - 1]
            got[index, bits + bit] = before + got[index, bit]
            if bit + 1 < bits:
                small_copy(index, bit + 1).start()

    def drain():
        for array in range(arrays):
            for side in sides:
                core_copy(array, side).wait_send()
                one_copy(array, side).wait_send()
                two_copy(array, side).wait_send()
                for stage in (3, 4, 5):
                    back_copy(stage, array, side, False).wait_send()

    ticks = (
        [functools.partial(add_core, array) for array in range(arrays)]
        + [functools.partial(add_one, array) for array in range(arrays)]
        + [functools.partial(add_two, array) for array in range(arrays)]
        + [functools.partial(back, stage, array) for stage in (3, 4, 5) for array in range(arrays)]
    )
    return enter, begin, ticks, drain, small_begin, small_step


def reduce_scratch(arrays, rows, model, bits):
    more = max(2 * (bits - 3), 1)
    return [
        pltpu.VMEM((arrays, 2, rows // 4, model), bf16),
        pltpu.VMEM((arrays, 2, rows // 8, model), bf16),
        pltpu.VMEM((arrays, 2, rows // 16, model), bf16),
        pltpu.VMEM((more, arrays, 2, rows // 16, model), bf16),
        pltpu.VMEM((arrays, 2, rows // 4, model), bf16),
        pltpu.VMEM((arrays, 2, rows // 8, model), bf16),
        pltpu.SemaphoreType.DMA((bits + 3, arrays, 2)),
        pltpu.SemaphoreType.DMA((bits + 3, arrays, 2)),
    ]


def backward_kernel(
    shards,
    bits,
    x_ref,
    box_x_ref,
    box_y_ref,
    gain_ref,
    shift_ref,
    grad_hidden_ref,
    qkv_ref,
    probs_ref,
    inverse_ref,
    context_ref,
    gathered_ref,
    part_up_ref,
    part_down_ref,
    grad_input_ref,
    grad_pack_ref,
    sums_ref,
    grad_up_ref,
    grad_down_ref,
    weights,
    copy_sem,
    grad_qkv,
    grad_context,
    grad_probs,
    small_scores,
    pack_total,
    bias_total,
    levels_total,
    summed,
    *scratch,
):
    page = pl.program_id(0)
    pages = pl.num_programs(0)
    steps_here = 4
    place = lax.axis_index("tensor")
    width, model = x_ref.shape
    heads = model // HEAD_DIM
    own = model // shards
    own_heads = heads // shards
    bins = 64
    enter, begin, ticks, drain, _, _ = reduce_steps(
        bits, (part_up_ref, part_down_ref), (summed.at[0], summed.at[1]), (), scratch
    )
    weight_copies = [
        pltpu.make_async_copy(gathered_ref.at[:, kind], weights.at[kind], copy_sem.at[kind]) for kind in range(4)
    ]
    stores = [
        pltpu.make_async_copy(summed.at[index], target, copy_sem.at[4 + index])
        for index, target in enumerate((grad_up_ref, grad_down_ref))
    ]

    @pl.when(page == 0)
    def _():
        for copy in weight_copies:
            copy.start()
        enter()
        begin()
        pack_total[...] = jnp.zeros_like(pack_total)
        bias_total[...] = jnp.zeros_like(bias_total)
        levels_total[...] = jnp.zeros_like(levels_total)
        sums_ref[...] = jnp.zeros_like(sums_ref)
        for copy in weight_copies:
            copy.wait()

    points = 5

    def point(index):
        for at, act in enumerate(ticks):
            where = at + 1
            if where % points == index:
                pl.when(page == where // points)(act)

    grad_hidden = grad_hidden_ref[...]
    grad_low = grad_hidden.astype(bf16)
    grad_context[...] = nt(weights[3].reshape(model, model), grad_low)
    hot = one_hot_columns(box_x_ref, box_y_ref, bins)
    back_hot = one_hot_columns(box_x_ref, box_y_ref, bins, True)

    def order(at):
        return lax.rem(place * own_heads + at, heads)

    def rows_of(at):
        return pl.ds(pl.multiple_of(order(at) * HEAD_DIM, HEAD_DIM), HEAD_DIM)

    def lead(at):
        rows = rows_of(at)
        grad_mixed = (grad_context[rows] * inverse_ref[0, order(at)]).astype(bf16)
        grad_probs[at % 2] = tn(qkv_ref[0, 2, rows], grad_mixed)
        delta = jnp.sum(
            grad_mixed.astype(f32) * context_ref[0, rows].astype(f32), axis=0, keepdims=True
        )
        return grad_mixed, delta

    def soften(at, delta):
        probs = probs_ref[0, order(at)].astype(f32)
        small_scores[at % 2] = (probs * (grad_probs[at % 2] - delta)).astype(bf16)

    def mix(at, grad_mixed):
        rows = rows_of(at)
        query = qkv_ref[0, 0, rows]
        key = qkv_ref[0, 1, rows]
        grad_scores = small_scores[at % 2]
        grad_value = nt(grad_mixed, probs_ref[0, order(at)])
        grad_key = nt(query, grad_scores) * LN2
        both = nn(jnp.concatenate([key, hot], axis=0) if at < own_heads else key, grad_scores)
        grad_qkv[0, rows] = (both[0:HEAD_DIM] * HEAD_DIM**-0.5).astype(bf16)
        grad_qkv[1, rows] = grad_key.astype(bf16)
        grad_qkv[2, rows] = grad_value.astype(bf16)
        if at < own_heads:
            levels_total[at] += nt(both[HEAD_DIM:].astype(bf16), back_hot)

    point(0)
    kept = [lead(0)]
    for at in range(heads):
        if at + 1 < heads:
            kept.append(lead(at + 1))
        soften(at, kept[at][1])
        if at > 0:
            mix(at - 1, kept[at - 1][0])
        if at % 3 == 2 and at + 1 < heads:
            point(1 + at // 3)
    mix(heads - 1, kept[-1][0])
    point(4)
    tokens = x_ref[...].astype(f32)
    xhat, inverse = norm_parts(tokens)
    low = (xhat * gain_ref[...] + shift_ref[...]).astype(bf16)
    mine = pl.ds(pl.multiple_of(place * own, own), own)
    stacked = jnp.concatenate([grad_qkv[kind, mine] for kind in range(3)], axis=0)
    pack_total[0 : 3 * own, :] += nn(stacked, low)
    pack_total[3 * own :, :] += nn(context_ref[0, mine], grad_low)
    wide = stacked.astype(f32)
    folded = wide[:, 0:BLOCK]
    for at in range(1, width // BLOCK):
        folded = folded + wide[:, at * BLOCK : (at + 1) * BLOCK]
    bias_total[...] += folded
    grad_normed = tn(grad_qkv[0], weights[0].reshape(model, model))
    for kind in (1, 2):
        grad_normed = grad_normed + tn(grad_qkv[kind], weights[kind].reshape(model, model))
    grad_total = grad_hidden + norm_grad(grad_normed, xhat, inverse, gain_ref[...])
    grad_input_ref[...] = grad_total.astype(bf16)
    sums_ref[0:1, :] += jnp.sum(grad_normed * xhat, axis=0, keepdims=True)
    sums_ref[1:2, :] += jnp.sum(grad_normed, axis=0, keepdims=True)

    @pl.when(page == pages - 1)
    def _():
        grad_pack_ref[...] = pack_total[...].astype(bf16)
        row = jnp.sum(bias_total[...].T, axis=0, keepdims=True)
        sums_ref[2:3, 0:own] = row[:, 0:own]
        sums_ref[3:4, 0:own] = row[:, 2 * own : 3 * own]
        lane = lax.broadcasted_iota(jnp.int32, (bins, 2 * bins), 1)
        for one in range(own_heads):
            for kind in range(2):
                block = levels_total[one, kind * bins : (kind + 1) * bins, :]
                inside = lane >= bins if kind else lane < bins
                rolled = pltpu.roll(jnp.where(inside, block, 0.0), kind * bins, 1, stride=1, stride_axis=0)
                at = (kind * own_heads + one) * 2 * bins
                sums_ref[4:5, at : at + 2 * bins] = jnp.sum(rolled, axis=0, keepdims=True)
        for copy in stores:
            copy.start()
        drain()
        for copy in stores:
            copy.wait()


def reduce_kernel(bits, part_ref, small_one_ref, small_two_ref, sum_ref, sum_one_ref, sum_two_ref, *scratch):
    enter, begin, ticks, drain, small_begin, small_step = reduce_steps(
        bits, (part_ref,), (sum_ref,), (small_one_ref, small_two_ref), scratch
    )
    enter()
    begin()
    small_begin()
    for at, act in enumerate(ticks):
        act()
        if at < 3:
            small_step(at)
    for bit in range(3, bits):
        small_step(bit)
    drain()
    sum_one_ref[...] = scratch[8][0, 2 * bits - 1]
    sum_two_ref[...] = scratch[8][1, 2 * bits - 1]


def finish_kernel(pack_ref, up_ref, down_ref, one_ref, two_ref, *outs):
    qkv, qv_bias, out, out_bias, gain_one, shift_one, gain_two, shift_two, up, up_bias, down, down_bias, tables = outs
    own = out.shape[0]
    bins = tables.shape[-1]
    for kind in range(3):
        qkv[kind] = pack_ref[kind * own : (kind + 1) * own, :].astype(f32)
    out[...] = pack_ref[3 * own :, :].astype(f32)
    up[...] = up_ref[...].astype(f32)
    down[...] = down_ref[...].astype(f32)
    qv_bias[...] = one_ref[2:4, 0:own]
    gain_one[...] = one_ref[0:1, :]
    shift_one[...] = one_ref[1:2, :]
    gain_two[...] = two_ref[0:1, :]
    shift_two[...] = two_ref[1:2, :]
    out_bias[...] = two_ref[2:3, :]
    down_bias[...] = two_ref[3:4, :]
    up_bias[...] = two_ref[4:5, :]
    m = lax.broadcasted_iota(jnp.int32, (2 * bins, bins), 0)
    level = lax.broadcasted_iota(jnp.int32, (2 * bins, bins), 1)
    pick = jnp.where(jnp.clip(m - (bins - 1), -(bins // 2), bins // 2 - 1) + bins // 2 == level, 1.0, 0.0)
    own_heads = tables.shape[1]
    for kind in range(2):
        for one in range(own_heads):
            at = (kind * own_heads + one) * 2 * bins
            line = jnp.broadcast_to(one_ref[4:5, at : at + 2 * bins], (8, 2 * bins))
            folded = lax.dot_general(
                line, pick, (((1,), (0,)), ((), ())), precision=lax.Precision.HIGHEST, preferred_element_type=f32
            )
            tables[kind, one : one + 1, :] = folded[0:1]


ANYWHERE = pl.BlockSpec(memory_space=pl.ANY)
IN_VMEM = pl.BlockSpec(memory_space=pltpu.VMEM)


def whole(shape):
    return pl.BlockSpec(shape, lambda *_: (0,) * len(shape), pipeline_mode=pl.Buffered(1))


def page_rows(model):
    return pl.BlockSpec((PAGE, model), lambda p, *_: (p, 0))


def page_block(*shape):
    return pl.BlockSpec((1,) + shape, lambda p, *_: (p,) + (0,) * len(shape))


def params(collective_id=None):
    if collective_id is None:
        return pltpu.CompilerParams(vmem_limit_bytes=VMEM_LIMIT)
    return pltpu.CompilerParams(
        vmem_limit_bytes=VMEM_LIMIT, collective_id=collective_id, has_side_effects=True
    )


def gather_first(shards, qkv, out, bias, tables, up_bias):
    model = qkv.shape[1]
    rows = qkv.shape[0] + out.shape[0]
    return pl.pallas_call(
        functools.partial(gather_first_kernel, shards),
        out_shape=(jax.ShapeDtypeStruct((shards, rows, model), bf16),)
        + tuple(jax.ShapeDtypeStruct((shards,) + small.shape, f32) for small in (bias, tables, up_bias)),
        in_specs=[ANYWHERE] * 5,
        out_specs=(ANYWHERE,) * 4,
        scratch_shapes=[pltpu.SemaphoreType.DMA((6,))]
        + gather_semaphores(1, shards)
        + [pltpu.VMEM((rows, model), bf16)],
        compiler_params=params(0),
        name="gather_first",
    )(qkv, out, bias, tables, up_bias)


def attention_forward(
    shards, counts, inputs, keep, box_x, box_y, gain, shift, out_bias, bias, tables, gathered, up, down
):
    rows_here, model = inputs.shape
    pages = rows_here // PAGE
    own = model // shards
    bins = tables.shape[-1]
    heads = model // HEAD_DIM
    units = up.shape[1]
    whole_up = jax.ShapeDtypeStruct((shards,) + up.shape, bf16)
    whole_down = jax.ShapeDtypeStruct((shards,) + down.shape, bf16)
    return pl.pallas_call(
        functools.partial(forward_kernel, shards),
        out_shape=(
            jax.ShapeDtypeStruct((pages, 3, model, PAGE), bf16),
            jax.ShapeDtypeStruct((pages, heads, PAGE, PAGE), bf16),
            jax.ShapeDtypeStruct((pages, heads, 1, PAGE), f32),
            jax.ShapeDtypeStruct((pages, model, PAGE), bf16),
            jax.ShapeDtypeStruct((rows_here, model), f32),
            whole_up,
            whole_down,
        ),
        grid_spec=pltpu.PrefetchScalarGridSpec(
            num_scalar_prefetch=1,
            grid=(pages,),
            in_specs=[page_rows(model)]
            + [page_block(1, PAGE)] * 3
            + [whole((1, model))] * 3
            + [whole(bias.shape), whole(tables.shape)]
            + [ANYWHERE] * 3,
            out_specs=(
                page_block(3, model, PAGE),
                page_block(heads, PAGE, PAGE),
                page_block(heads, 1, PAGE),
                page_block(model, PAGE),
                page_rows(model),
                ANYWHERE,
                ANYWHERE,
            ),
            scratch_shapes=[
                pltpu.VMEM((4, shards, own, model), bf16),
                pltpu.SemaphoreType.DMA((8,)),
                pltpu.VMEM((2, model, units), bf16),
            ]
            + gather_semaphores(2, shards)
            + [
                pltpu.VMEM((2, model, 128), f32),
                pltpu.VMEM((heads * 2 * bins, 2 * bins), bf16),
                pltpu.VMEM((heads * 2 * bins, PAGE), bf16),
                pltpu.VMEM((2, PAGE, PAGE), f32),
            ],
        ),
        compiler_params=params(1),
        name="attention_forward",
    )(counts, inputs, keep, box_x, box_y, gain, shift, out_bias, bias, tables, gathered, up, down)


def feed_forward(counts, place, hidden, cotangent, gain, shift, down_bias, up_bias, up_all, down_all):
    rows_here, model = hidden.shape
    pages = rows_here // PAGE
    shards, _, hidden_units = up_all.shape
    return pl.pallas_call(
        mlp_kernel,
        out_shape=(
            jax.ShapeDtypeStruct((rows_here, model), bf16),
            jax.ShapeDtypeStruct((rows_here, model), f32),
            jax.ShapeDtypeStruct((model, hidden_units), bf16),
            jax.ShapeDtypeStruct((hidden_units, model), bf16),
            jax.ShapeDtypeStruct((8, model), f32),
        ),
        grid_spec=pltpu.PrefetchScalarGridSpec(
            num_scalar_prefetch=2,
            grid=(pages,),
            in_specs=[
                page_rows(model),
                page_rows(model),
                whole((1, model)),
                whole((1, model)),
                whole((1, model)),
                whole((shards, 1, hidden_units)),
                whole((shards, model, hidden_units)),
                whole((shards, hidden_units, model)),
            ],
            out_specs=(
                page_rows(model),
                page_rows(model),
                whole((model, hidden_units)),
                whole((hidden_units, model)),
                whole((8, model)),
            ),
            scratch_shapes=[
                pltpu.VMEM((model, hidden_units), f32),
                pltpu.VMEM((hidden_units, model), f32),
                pltpu.VMEM((PAGE, model), bf16),
                pltpu.VMEM((PAGE, model), bf16),
                pltpu.VMEM((PAGE, model), f32),
                pltpu.VMEM((PAGE, model), f32),
                pltpu.VMEM((shards, PAGE, hidden_units), bf16),
                pltpu.VMEM((shards, PAGE, hidden_units), bf16),
                pltpu.VMEM((2, PAGE, hidden_units), f32),
                pltpu.VMEM((2, PAGE, hidden_units), f32),
            ],
        ),
        compiler_params=params(),
        name="feed_forward",
    )(counts, place, hidden, cotangent, gain, shift, down_bias, up_bias, up_all, down_all)


def attention_backward(
    shards,
    devices,
    inputs,
    box_x,
    box_y,
    gain,
    shift,
    grad_hidden,
    qkv,
    probs,
    inverse,
    context,
    gathered,
    part_up,
    part_down,
):
    rows_here, model = inputs.shape
    pages, heads = probs.shape[:2]
    own = model // shards
    bins = 64
    bits = devices.bit_length() - 1
    return pl.pallas_call(
        functools.partial(backward_kernel, shards, bits),
        out_shape=(
            jax.ShapeDtypeStruct((rows_here, model), bf16),
            jax.ShapeDtypeStruct((4 * own, model), bf16),
            jax.ShapeDtypeStruct((8, model), f32),
            jax.ShapeDtypeStruct(part_up.shape, bf16),
            jax.ShapeDtypeStruct(part_down.shape, bf16),
        ),
        grid_spec=pltpu.PrefetchScalarGridSpec(
            num_scalar_prefetch=0,
            grid=(pages,),
            in_specs=[page_rows(model)]
            + [page_block(1, PAGE)] * 2
            + [whole((1, model))] * 2
            + [
                page_rows(model),
                page_block(3, model, PAGE),
                page_block(heads, PAGE, PAGE),
                page_block(heads, 1, PAGE),
                page_block(model, PAGE),
                ANYWHERE,
                whole(part_up.shape),
                whole(part_down.shape),
            ],
            out_specs=(
                page_rows(model),
                whole((4 * own, model)),
                whole((8, model)),
                ANYWHERE,
                ANYWHERE,
            ),
            scratch_shapes=[
                pltpu.VMEM((4, shards, own, model), bf16),
                pltpu.SemaphoreType.DMA((6,)),
                pltpu.VMEM((3, model, PAGE), bf16),
                pltpu.VMEM((model, PAGE), f32),
                pltpu.VMEM((2, PAGE, PAGE), f32),
                pltpu.VMEM((2, PAGE, PAGE), bf16),
                pltpu.VMEM((4 * own, model), f32),
                pltpu.VMEM((3 * own, BLOCK), f32),
                pltpu.VMEM((own // HEAD_DIM, 2 * bins, 2 * bins), f32),
                pltpu.VMEM((2,) + part_up.shape, bf16),
            ]
            + reduce_scratch(2, part_up.shape[0], model, bits),
        ),
        compiler_params=params(2),
        name="attention_backward",
    )(
        inputs,
        box_x,
        box_y,
        gain,
        shift,
        grad_hidden,
        qkv,
        probs,
        inverse,
        context,
        gathered,
        part_up,
        part_down,
    )


def reduce_grads(devices, part, small_one, small_two):
    rows, model = part.shape
    bits = devices.bit_length() - 1
    return pl.pallas_call(
        functools.partial(reduce_kernel, bits),
        out_shape=(jax.ShapeDtypeStruct(part.shape, bf16),)
        + tuple(jax.ShapeDtypeStruct(small.shape, f32) for small in (small_one, small_two)),
        in_specs=[IN_VMEM] * 3,
        out_specs=(IN_VMEM,) * 3,
        scratch_shapes=reduce_scratch(1, rows, model, bits)
        + [
            pltpu.VMEM((2, 2 * bits) + small_one.shape, f32),
            pltpu.SemaphoreType.DMA((2, bits)),
            pltpu.SemaphoreType.DMA((2, bits)),
        ],
        compiler_params=params(3),
        name="reduce_grads",
    )(part, small_one, small_two)


def finish_grads(pack, up, down, small_one, small_two, bins):
    own, model = pack.shape[0] // 4, pack.shape[1]
    row = jax.ShapeDtypeStruct((1, model), f32)
    return pl.pallas_call(
        finish_kernel,
        out_shape=(
            jax.ShapeDtypeStruct((3, own, model), f32),
            jax.ShapeDtypeStruct((2, own), f32),
            jax.ShapeDtypeStruct((own, model), f32),
            row,
            row,
            row,
            row,
            row,
            jax.ShapeDtypeStruct(up.shape, f32),
            jax.ShapeDtypeStruct((1, up.shape[1]), f32),
            jax.ShapeDtypeStruct(down.shape, f32),
            row,
            jax.ShapeDtypeStruct((2, own // HEAD_DIM, bins), f32),
        ),
        in_specs=[IN_VMEM] * 5,
        out_specs=(IN_VMEM,) * 13,
        compiler_params=params(),
        name="finish_grads",
    )(pack, up, down, small_one, small_two)


def on_device(
    inputs,
    cotangent,
    counts,
    keep_mask,
    box_x,
    box_y,
    gain_one,
    shift_one,
    w_qkv,
    b_qv,
    w_out,
    b_out,
    gain_two,
    shift_two,
    w_up,
    b_up,
    w_down,
    b_down,
    rel_tables,
    *,
    devices,
):
    rows_here, model = inputs.shape
    pages = rows_here // PAGE
    own_heads, bins = rel_tables.shape[1:]
    own = own_heads * HEAD_DIM
    shards = model // own
    place = lax.axis_index("tensor").astype(jnp.int32).reshape(1)
    paged = lambda array: array.reshape(pages, 1, PAGE)
    row = lambda vector: vector.reshape(1, -1)
    keep_mask, box_x, box_y = paged(keep_mask), paged(box_x), paged(box_y)
    gain_one, shift_one, gain_two, shift_two = row(gain_one), row(shift_one), row(gain_two), row(shift_two)

    gathered, bias_all, tables_all, up_bias_all = gather_first(
        shards, w_qkv.transpose(0, 2, 1).reshape(3 * own, model), w_out, b_qv, rel_tables, row(b_up)
    )
    gathered = gathered.reshape(shards, 4, own, model)
    qkv, probs, inverse, context, hidden, up_all, down_all = attention_forward(
        shards,
        counts,
        inputs,
        keep_mask,
        box_x,
        box_y,
        gain_one,
        shift_one,
        row(b_out),
        bias_all,
        tables_all,
        gathered,
        w_up,
        w_down,
    )
    out, grad_hidden, part_up, part_down, small_two = feed_forward(
        counts, place, hidden, cotangent, gain_two, shift_two, row(b_down), up_bias_all, up_all, down_all
    )
    grad_input, part_pack, small_one, grad_up, grad_down = attention_backward(
        shards,
        devices,
        inputs,
        box_x,
        box_y,
        gain_one,
        shift_one,
        grad_hidden,
        qkv,
        probs,
        inverse,
        context,
        gathered,
        part_up,
        part_down,
    )
    grad_pack, small_one, small_two = reduce_grads(devices, part_pack, small_one, small_two)
    results = finish_grads(grad_pack, grad_up, grad_down, small_one, small_two, bins)
    (
        grad_qkv,
        grad_b_qv,
        grad_w_out,
        grad_b_out,
        grad_gain_one,
        grad_shift_one,
        grad_gain_two,
        grad_shift_two,
        grad_w_up,
        grad_b_up,
        grad_w_down,
        grad_b_down,
        grad_tables,
    ) = results
    flat = lambda vector: vector.reshape(-1)
    return (
        out,
        grad_input,
        grad_qkv.transpose(0, 2, 1),
        grad_b_qv,
        grad_w_out,
        flat(grad_b_out),
        flat(grad_gain_one),
        flat(grad_shift_one),
        flat(grad_gain_two),
        flat(grad_shift_two),
        grad_w_up,
        flat(grad_b_up),
        grad_w_down,
        flat(grad_b_down),
        grad_tables,
    )


def solution(mesh):
    placed = (
        P("dp", None),
        P("dp", None),
        P("dp"),
        P("dp"),
        P("dp"),
        P("dp"),
        P(),
        P(),
        P(None, None, "tensor"),
        P(None, "tensor"),
        P("tensor", None),
        P(),
        P(),
        P(),
        P(None, "tensor"),
        P("tensor"),
        P("tensor", None),
        P(),
        P(None, "tensor", None),
    )
    return jax.shard_map(
        functools.partial(on_device, devices=mesh.shape["dp"]),
        mesh=mesh,
        in_specs=placed,
        out_specs=(
            P("dp", None),
            P("dp", None),
            P(None, None, "tensor"),
            P(None, "tensor"),
            P("tensor", None),
            P(),
            P(),
            P(),
            P(),
            P(),
            P(None, "tensor"),
            P("tensor"),
            P("tensor", None),
            P(),
            P(None, "tensor", None),
        ),
        check_vma=False,
    )
```

```python
import functools
import jax
import jax.numpy as jnp
from jax import lax
from jax.experimental import pallas as pl
from jax.experimental.pallas import tpu as pltpu
from jax.sharding import PartitionSpec as P

HEAD_DIM = 64
PAGE = 512
BLOCK = 128
epsilon = 1e-05
masked_score = -1e30
LOG2E = 1.4426950408889634
LN2 = 0.6931471805599453
bf16 = jnp.bfloat16
f32 = jnp.float32
VMEM_LIMIT = 60 << 20


def dot(left, right, left_dim, right_dim):
    return lax.dot_general(
        left, right, (((left_dim,), (right_dim,)), ((), ())), preferred_element_type=f32
    )


def nn(left, right):
    return dot(left, right, 1, 0)


def nt(left, right):
    return dot(left, right, 1, 1)


def tn(left, right):
    return dot(left, right, 0, 0)


def norm_parts(rows):
    average = jnp.mean(rows, axis=-1, keepdims=True)
    centered = rows - average
    variance = jnp.mean(centered * centered, axis=-1, keepdims=True)
    inverse = lax.rsqrt(variance + epsilon)
    return centered * inverse, inverse


def norm_grad(grad_out, xhat, inverse, gain):
    scaled = grad_out * gain
    mean_one = jnp.mean(scaled, axis=-1, keepdims=True)
    mean_two = jnp.mean(scaled * xhat, axis=-1, keepdims=True)
    return inverse * (scaled - mean_one - xhat * mean_two)


def one_hot_columns(box_x_ref, box_y_ref, bins, reverse=False):
    width = box_x_ref.shape[-1]
    levels = lax.broadcasted_iota(jnp.int32, (bins, width), 0)
    if reverse:
        levels = (bins - 1) - levels
    hot_x = jnp.where(levels == box_x_ref[0], 1.0, 0.0)
    hot_y = jnp.where(levels == box_y_ref[0], 1.0, 0.0)
    return jnp.concatenate([hot_x, hot_y], axis=0).astype(bf16)


def by_halves(count, body):
    body(PAGE)


def neighbours(axis):
    core = axis % 2
    side_x = (axis // 2) % 2
    side_y = (axis // 4) % 2
    return core, side_x, side_y, 1 - 2 * core, 2 - 4 * side_x, 4 - 8 * side_y


def flipped(index, mask):
    result, bit = index, 1
    while bit <= mask:
        if mask & bit:
            result = result + bit - 2 * bit * ((index // bit) % 2)
        bit *= 2
    return result


def greet(peers):
    barrier = pltpu.get_barrier_semaphore()
    for dp, tensor in peers:
        pl.semaphore_signal(
            barrier, inc=1, device_id={"dp": dp, "tensor": tensor}, device_id_type=pl.DeviceIdType.MESH
        )
    pl.semaphore_wait(barrier, len(peers))


KIND_Z, KIND_X, KIND_Y, KIND_VIA_X, KIND_VIA_Y, KIND_CORE = 0, 1, 2, 3, 4, 5
KINDS = 9


def gather_steps(shards, sources, targets, small_sources, small_targets, send_sem, recv_sem):
    arrays = len(sources)
    place = lax.axis_index("tensor")
    lane = lax.axis_index("dp")
    core, side_x, side_y, to_core, to_x, to_y = neighbours(lane)
    mine = lane % 8
    rows = targets[0].shape[1] // 8
    half = rows // 2
    hops = range(1, shards)

    def piece(index, start=0, size=rows):
        return pl.ds(pl.multiple_of(index * rows + start, 16), size)

    def remote(kind, array, hop, source, target, dp, tensor):
        return pltpu.make_async_remote_copy(
            src_ref=source,
            dst_ref=target,
            send_sem=send_sem.at[kind, array, hop - 1],
            recv_sem=recv_sem.at[kind, array, hop - 1],
            device_id={"dp": dp, "tensor": tensor},
            device_id_type=pl.DeviceIdType.MESH,
        )

    def within(kind, array, hop, region, step):
        ref = targets[array].at[flipped(place, hop), region]
        return remote(kind, array, hop, ref, ref, lane + step, place)

    def along(array, hop):
        source, target = sources[array].at[piece(mine)], targets[array].at[place, piece(mine)]
        return remote(KIND_Z, array, hop, source, target, lane, flipped(place, hop))

    def along_small(index, hop):
        source, target = small_sources[index], small_targets[index].at[place]
        return remote(1 + index, arrays, hop, source, target, lane, flipped(place, hop))

    def enter():
        greet(
            [(lane + step, place) for step in (to_core, to_x, to_y)] + [(lane, flipped(place, hop)) for hop in hops]
        )

    def begin():
        for array in range(arrays):
            for hop in hops:
                along(array, hop).start()
            if array == 0:
                for index in range(len(small_sources)):
                    for hop in hops:
                        along_small(index, hop).start()

    def arrive(array, hop):
        along(array, hop).wait_recv()
        within(KIND_X, array, hop, piece(mine), to_x).start()
        within(KIND_Y, array, hop, piece(mine), to_y).start()
        within(KIND_CORE, array, hop, piece(mine), to_core).start()

    def spread_near(array, hop):
        at = mine + to_x
        within(KIND_X, array, hop, piece(at), to_x).wait_recv()
        within(KIND_VIA_Y, array, hop, piece(at, 0, half), to_y).start()
        within(KIND_CORE + 1, array, hop, piece(at), to_core).start()
        at = mine + to_y
        within(KIND_Y, array, hop, piece(at), to_y).wait_recv()
        within(KIND_VIA_X, array, hop, piece(at, half, half), to_x).start()
        within(KIND_CORE + 2, array, hop, piece(at), to_core).start()

    def spread_far(array, hop):
        at = mine + to_x + to_y
        within(KIND_VIA_Y, array, hop, piece(at, 0, half), to_y).wait_recv()
        within(KIND_VIA_X, array, hop, piece(at, half, half), to_x).wait_recv()
        within(KIND_CORE + 3, array, hop, piece(at), to_core).start()

    def finish(array, hop):
        for index, shift in enumerate((0, to_x, to_y, to_x + to_y)):
            within(KIND_CORE + index, array, hop, piece(mine + to_core + shift), to_core).wait_recv()

    def drain(early):
        for hop in hops:
            if early:
                for index in range(len(small_sources)):
                    along_small(index, hop).wait()
                continue
            for array in range(arrays):
                along(array, hop).wait_send()
                within(KIND_X, array, hop, piece(mine), to_x).wait_send()
                within(KIND_Y, array, hop, piece(mine), to_y).wait_send()
                within(KIND_VIA_Y, array, hop, piece(mine + to_x, 0, half), to_y).wait_send()
                within(KIND_VIA_X, array, hop, piece(mine + to_y, half, half), to_x).wait_send()
                for index, shift in enumerate((0, to_x, to_y, to_x + to_y)):
                    within(KIND_CORE + index, array, hop, piece(mine + shift), to_core).wait_send()

    items = [(array, hop) for array in range(arrays) for hop in hops]
    stages = (arrive, spread_near, spread_far, finish)

    def tick(at):
        for stage, act in enumerate(stages):
            if 0 <= at - stage < len(items):
                act(*items[at - stage])

    return enter, begin, tick, len(items) + len(stages) - 1, drain


def gather_semaphores(arrays, shards):
    return [pltpu.SemaphoreType.DMA((KINDS, arrays + 1, shards - 1))] * 2


def forward_kernel(
    shards,
    counts_ref,
    x_ref,
    keep_ref,
    box_x_ref,
    box_y_ref,
    rows_ref,
    bias_ref,
    tables_ref,
    qkv_weight_ref,
    out_weight_ref,
    up_ref,
    down_ref,
    qkv_ref,
    probs_ref,
    inverse_ref,
    context_ref,
    hidden_ref,
    gathered_ref,
    up_all_ref,
    down_all_ref,
    rows_all_ref,
    weights,
    copy_sem,
    bounce,
    bias_all,
    tables_all,
    send_sem,
    recv_sem,
    bias_columns,
    toeplitz,
    spread,
    scores,
):
    page = pl.program_id(0)
    pages = counts_ref.shape[0]
    place = lax.axis_index("tensor")
    width, model = x_ref.shape
    heads = model // HEAD_DIM
    own = model // shards
    own_heads = heads // shards
    bins = tables_ref.shape[-1]
    split = qkv_weight_ref.shape[0]
    smalls, small_targets = (rows_ref, bias_ref, tables_ref), (rows_all_ref, bias_all, tables_all)
    enter, begin, tick, ticks, drain = gather_steps(
        shards,
        (bounce.at[0], up_ref, down_ref),
        (gathered_ref, up_all_ref, down_all_ref),
        smalls,
        small_targets,
        send_sem,
        recv_sem,
    )
    loads = [
        pltpu.make_async_copy(qkv_weight_ref, bounce.at[0, 0:split], copy_sem.at[0]),
        pltpu.make_async_copy(out_weight_ref, bounce.at[0, split:], copy_sem.at[1]),
        pltpu.make_async_copy(up_ref, bounce.at[1], copy_sem.at[2]),
        pltpu.make_async_copy(down_ref, bounce.at[2], copy_sem.at[3]),
    ]
    stores = [
        pltpu.make_async_copy(bounce.at[index], target.at[place], copy_sem.at[4 + index])
        for index, target in enumerate((gathered_ref, up_all_ref, down_all_ref))
    ] + [
        pltpu.make_async_copy(source, target.at[place], copy_sem.at[7 + index])
        for index, (source, target) in enumerate(zip(smalls, small_targets))
    ]
    weight_copies = [
        pltpu.make_async_copy(
            gathered_ref.at[:, pl.ds(kind * own, own)], weights.at[kind], copy_sem.at[10 + kind]
        )
        for kind in range(4)
    ]
    before = shards - 1 + 3

    @pl.when(page == 0)
    def _():
        for copy in loads:
            copy.start()
        enter()
        for copy in loads[0:2]:
            copy.wait()
        begin()
        for copy in loads[2:4]:
            copy.wait()
        for copy in stores:
            copy.start()
        for copy in stores:
            copy.wait()
        for at in range(before):
            tick(at)
        for copy in weight_copies:
            copy.start()
        drain(True)
        for shard in range(shards):
            rows = slice(shard * own, (shard + 1) * own)
            for kind in range(2):
                wide = jnp.broadcast_to(bias_all[shard, kind : kind + 1, :], (128, own))
                bias_columns[kind, rows, :] = wide.T
        m = lax.broadcasted_iota(jnp.int32, (bins, 2 * bins), 1)
        signed = jnp.where(m >= bins, 2 * bins - m, -m)
        level = lax.broadcasted_iota(jnp.int32, (bins, 2 * bins), 0)
        pick = jnp.where(jnp.clip(signed, -(bins // 2), bins // 2 - 1) + bins // 2 == level, 1.0, 0.0).astype(bf16)
        lane = lax.broadcasted_iota(jnp.int32, (bins, 2 * bins), 1)
        for shard in range(shards):
            for one in range(own_heads):
                at = (shard * own_heads + one) * 2 * bins
                for kind in range(2):
                    table = (tables_all[shard, one, kind : kind + 1, :] * LOG2E).astype(bf16)
                    line = nn(jnp.broadcast_to(table, (bins, bins)), pick)
                    rolled = pltpu.roll(line, kind * bins, 1, stride=1, stride_axis=0)
                    inside = lane >= bins if kind else lane < bins
                    toeplitz[at + kind * bins : at + (kind + 1) * bins, :] = jnp.where(inside, rolled, 0.0).astype(bf16)
        for copy in weight_copies:
            copy.wait()

    points = 5
    left = ticks - before

    def point(index):
        for at in range(before, ticks):
            where = (at - before + 1) * points * pages // (left + 1) - 1
            if where % points == index:
                pl.when(page == where // points)(functools.partial(tick, at))

    tokens = x_ref[...].astype(f32)
    xhat, _ = norm_parts(tokens)
    low = (xhat * rows_ref[0:1, :] + rows_ref[1:2, :]).astype(bf16)
    for kind in range(3):
        product = nt(weights[kind].reshape(model, model), low)
        if kind == 0:
            product = (product + bias_columns[0, :, 0:1]) * (LOG2E * HEAD_DIM**-0.5)
        if kind == 2:
            product = product + bias_columns[1, :, 0:1]
        qkv_ref[0, kind] = product.astype(bf16)
    hot = one_hot_columns(box_x_ref, box_y_ref, bins)
    spread[...] = nn(toeplitz[...], hot).astype(bf16)
    lane = lax.broadcasted_iota(jnp.int32, (1, width), 1)
    open_key = (lane < counts_ref[page]) & (keep_ref[0] == 1)
    mask_row = jnp.where(open_key, 0.0, masked_score)
    first = lax.broadcasted_iota(jnp.int32, (HEAD_DIM, width), 0) == 0
    key_pad = jnp.where(first, mask_row, 0.0).astype(bf16)
    query_pad = jnp.where(first, 1.0, 0.0).astype(bf16)
    ones = jnp.ones((16, width), bf16)
    eye = lax.broadcasted_iota(jnp.int32, (BLOCK, BLOCK), 0) == lax.broadcasted_iota(jnp.int32, (BLOCK, BLOCK), 1)

    def score(index, slot):
        rows = slice(index * HEAD_DIM, (index + 1) * HEAD_DIM)
        query = qkv_ref[0, 0, rows]
        key = qkv_ref[0, 1, rows]
        bias = spread[index * 2 * bins : (index + 1) * 2 * bins, :]
        left = jnp.concatenate([key, key_pad, hot], axis=0)
        right = jnp.concatenate([query, query_pad, bias], axis=0)
        scores[slot] = tn(left, right)
        return jnp.sum(query.astype(f32) * key.astype(f32), axis=0, keepdims=True) + jnp.sum(
            bias.astype(f32) * hot.astype(f32), axis=0, keepdims=True
        )

    def soften(index, slot, own_score):
        for at in range(width // BLOCK):
            span = slice(at * BLOCK, (at + 1) * BLOCK)
            scores[slot, span, span] = jnp.where(eye, own_score[:, span], scores[slot, span, span])
        top = jnp.max(scores[slot], axis=0, keepdims=True)
        probs_ref[0, index] = jnp.exp2(scores[slot] - top).astype(bf16)

    def mix(index):
        rows = slice(index * HEAD_DIM, (index + 1) * HEAD_DIM)
        mixed = nn(jnp.concatenate([qkv_ref[0, 2, rows], ones], axis=0), probs_ref[0, index])
        inverse = 1.0 / mixed[HEAD_DIM : HEAD_DIM + 1]
        inverse_ref[0, index] = inverse
        context_ref[0, rows] = (mixed[0:HEAD_DIM] * inverse).astype(bf16)

    point(0)
    owns = [score(0, 0)]
    for at in range(heads):
        if at + 1 < heads:
            owns.append(score(at + 1, (at + 1) % 2))
        soften(at, at % 2, owns[at])
        if at > 0:
            mix(at - 1)
        if at % 3 == 2 and at + 1 < heads:
            point(1 + at // 3)
    mix(heads - 1)
    point(4)
    attended = tn(context_ref[0], weights[3].reshape(model, model))
    hidden_ref[...] = tokens + attended + rows_ref[2:3, :]

    @pl.when(page == pages - 1)
    def _():
        drain(False)


def mlp_kernel(
    counts_ref,
    place_ref,
    hidden_ref,
    cotangent_ref,
    rows_ref,
    bias_ref,
    up_ref,
    down_ref,
    out_ref,
    grad_hidden_ref,
    grad_up_ref,
    grad_down_ref,
    sums_ref,
    up_total,
    down_total,
    low_ref,
    gl_ref,
    down_acc,
    gn_acc,
    act_ref,
    gu_ref,
    upper_ref,
    grad_ref,
):
    page = pl.program_id(0)
    shards = up_ref.shape[0]
    place = place_ref[0]

    @pl.when(page == 0)
    def _():
        up_total[...] = jnp.zeros_like(up_total)
        down_total[...] = jnp.zeros_like(down_total)
        sums_ref[...] = jnp.zeros_like(sums_ref)

    count = counts_ref[page]

    def body(width):
        valid = lax.broadcasted_iota(jnp.int32, (width, 1), 0) < count
        hidden = hidden_ref[0:width, :]
        xhat, inverse = norm_parts(hidden)
        low = (xhat * rows_ref[3:4, :] + rows_ref[4:5, :]).astype(bf16)
        grad_result = jnp.where(valid, cotangent_ref[0:width, :].astype(f32), 0.0)
        grad_low = grad_result.astype(bf16)

        low_ref[0:width, :] = low
        gl_ref[0:width, :] = grad_low
        down_acc[0:width, :] = jnp.zeros((width, hidden.shape[1]), f32)
        gn_acc[0:width, :] = jnp.zeros((width, hidden.shape[1]), f32)

        def lead(at, slot):
            upper_ref[slot, 0:width, :] = nn(low_ref[0:width, :], up_ref[at]) + bias_ref[at, 6:7, :]
            grad_ref[slot, 0:width, :] = nt(gl_ref[0:width, :], down_ref[at])

        def bend(at, slot):
            upper = upper_ref[slot, 0:width, :]
            half = 0.5 * (1.0 + lax.erf(upper * 0.7071067811865476))
            density = jnp.exp(-0.5 * upper * upper) * 0.3989422804014327
            act_ref[at, 0:width, :] = (upper * half).astype(bf16)
            slope = half + upper * density
            gu_ref[at, 0:width, :] = (grad_ref[slot, 0:width, :] * slope).astype(bf16)

        def mix(at):
            down_acc[0:width, :] += nn(act_ref[at, 0:width, :], down_ref[at])
            gn_acc[0:width, :] += nt(gu_ref[at, 0:width, :], up_ref[at])

        lead(0, 0)
        for at in range(shards):
            if at + 1 < shards:
                lead(at + 1, (at + 1) % 2)
            bend(at, at % 2)
            if at > 0:
                mix(at - 1)
        mix(shards - 1)
        down_proj = down_acc[0:width, :]
        grad_normed = gn_acc[0:width, :]
        up_total[...] += tn(low_ref[0:width, :], gu_ref[place, 0:width, :])
        down_total[...] += tn(act_ref[place, 0:width, :], gl_ref[0:width, :])
        sums_ref[4:5, :] += jnp.sum(gu_ref[place, 0:width, :].astype(f32), axis=0, keepdims=True)
        result = jnp.where(valid, hidden + down_proj + rows_ref[5:6, :], 0.0)
        out_ref[0:width, :] = result.astype(bf16)
        grad_hidden = grad_result + norm_grad(grad_normed, xhat, inverse, rows_ref[3:4, :])
        grad_hidden_ref[0:width, :] = grad_hidden
        sums_ref[0:1, :] += jnp.sum(grad_normed * xhat, axis=0, keepdims=True)
        sums_ref[1:2, :] += jnp.sum(grad_normed, axis=0, keepdims=True)
        sums_ref[2:3, :] += jnp.sum(grad_hidden, axis=0, keepdims=True)
        sums_ref[3:4, :] += jnp.sum(grad_result, axis=0, keepdims=True)
        if width < PAGE:
            out_ref[width:PAGE, :] = jnp.zeros((PAGE - width, hidden.shape[1]), bf16)
            grad_hidden_ref[width:PAGE, :] = jnp.zeros((PAGE - width, hidden.shape[1]), f32)

    by_halves(count, body)

    @pl.when(page == pl.num_programs(0) - 1)
    def _():
        grad_up_ref[...] = up_total[...].astype(bf16)
        grad_down_ref[...] = down_total[...].astype(bf16)


def reduce_steps(bits, parts, sums, smalls, scratch):
    arrays = len(parts)
    got_core, got_one, got_two, got_more, kept_core, kept_one, send_sem, recv_sem = scratch[0:8]
    place = lax.axis_index("tensor")
    lane = lax.axis_index("dp")
    core, side_x, side_y, to_core, to_x, to_y = neighbours(lane)
    steps = [to_core, to_x, to_y]
    for bit in range(3, bits):
        size = 2**bit
        steps.append(size - 2 * size * ((lane // size) % 2))
    rows = parts[0].shape[0]
    quarter, eighth, sixteenth = rows // 4, rows // 8, rows // 16
    order = ((side_x, side_y, to_x, to_y), (side_y, side_x, to_y, to_x))
    sides = range(2)

    def device(step):
        return {"dp": lane + step, "tensor": place}

    def remote(stage, array, side, source, target, step):
        return pltpu.make_async_remote_copy(
            src_ref=source,
            dst_ref=target,
            send_sem=send_sem.at[stage, array, side],
            recv_sem=recv_sem.at[stage, array, side],
            device_id=device(step),
            device_id_type=pl.DeviceIdType.MESH,
        )

    def span(side, of_core, one=None, two=None):
        start = side * (rows // 2) + of_core * quarter
        if one is None:
            return pl.ds(pl.multiple_of(start, 16), quarter)
        start = start + one * eighth
        if two is None:
            return pl.ds(pl.multiple_of(start, 16), eighth)
        return pl.ds(pl.multiple_of(start + two * sixteenth, 16), sixteenth)

    def part_of(index, size):
        return pl.ds(pl.multiple_of(index * size, 16), size)

    def core_copy(array, side):
        return remote(0, array, side, parts[array].at[span(side, 1 - core)], got_core.at[array, side], to_core)

    def one_copy(array, side):
        one, two, to_one, to_two = order[side]
        source = kept_core.at[array, side, part_of(1 - one, eighth)]
        return remote(1, array, side, source, got_one.at[array, side], to_one)

    def two_copy(array, side):
        one, two, to_one, to_two = order[side]
        source = kept_one.at[array, side, part_of(1 - two, sixteenth)]
        return remote(2, array, side, source, got_two.at[array, side], to_two)

    def more_copy(array, side, bit):
        source = got_more.at[bit - 3, array, side]
        return remote(bit + 3, array, side, source, got_more.at[bits - 3 + bit - 3, array, side], steps[bit])

    def back_copy(stage, array, side, inward):
        one, two, to_one, to_two = order[side]
        if stage == 3:
            region, step = span(side, core, one, 1 - two if inward else two), to_two
        elif stage == 4:
            region, step = span(side, core, 1 - one if inward else one), to_one
        else:
            region, step = span(side, 1 - core if inward else core), to_core
        ref = sums[array].at[region]
        return remote(stage, array, side, ref, ref, step)

    def enter():
        greet([(lane + step, place) for step in steps])

    def begin():
        for array in range(arrays):
            for side in sides:
                core_copy(array, side).start()

    def add_core(array):
        for side in sides:
            keep = span(side, core)
            core_copy(array, side).wait_recv()
            kept_core[array, side] = (
                parts[array][keep, :].astype(f32) + got_core[array, side].astype(f32)
            ).astype(bf16)
            one_copy(array, side).start()

    def add_one(array):
        for side in sides:
            one, two, to_one, to_two = order[side]
            one_copy(array, side).wait_recv()
            kept_one[array, side] = (
                kept_core[array, side, part_of(one, eighth), :].astype(f32) + got_one[array, side].astype(f32)
            ).astype(bf16)
            two_copy(array, side).start()

    def add_two(array):
        for side in sides:
            one, two, to_one, to_two = order[side]
            two_copy(array, side).wait_recv()
            total = (
                kept_one[array, side, part_of(two, sixteenth), :].astype(f32) + got_two[array, side].astype(f32)
            ).astype(bf16)
            for bit in range(3, bits):
                got_more[bit - 3, array, side] = total
                more_copy(array, side, bit).start()
                more_copy(array, side, bit).wait()
                total = (total.astype(f32) + got_more[bits - 3 + bit - 3, array, side].astype(f32)).astype(bf16)
            sums[array][span(side, core, one, two), :] = total
            back_copy(3, array, side, False).start()

    def back(stage, array):
        for side in sides:
            back_copy(stage, array, side, True).wait_recv()
            if stage < 5:
                back_copy(stage + 1, array, side, False).start()

    def small_copy(index, bit):
        got, small_send, small_recv = scratch[8:11]
        source = smalls[index] if bit == 0 else got.at[index, bits + bit - 1]
        return pltpu.make_async_remote_copy(
            src_ref=source,
            dst_ref=got.at[index, bit],
            send_sem=small_send.at[index, bit],
            recv_sem=small_recv.at[index, bit],
            device_id=device(steps[bit]),
            device_id_type=pl.DeviceIdType.MESH,
        )

    def small_begin():
        for index in range(len(smalls)):
            small_copy(index, 0).start()

    def small_step(bit):
        got = scratch[8]
        for index in range(len(smalls)):
            small_copy(index, bit).wait()
            before = smalls[index][...] if bit == 0 else got[index, bits + bit - 1]
            got[index, bits + bit] = before + got[index, bit]
            if bit + 1 < bits:
                small_copy(index, bit + 1).start()

    def drain():
        for array in range(arrays):
            for side in sides:
                core_copy(array, side).wait_send()
                one_copy(array, side).wait_send()
                two_copy(array, side).wait_send()
                for stage in (3, 4, 5):
                    back_copy(stage, array, side, False).wait_send()

    ticks = (
        [functools.partial(add_core, array) for array in range(arrays)]
        + [functools.partial(add_one, array) for array in range(arrays)]
        + [functools.partial(add_two, array) for array in range(arrays)]
        + [functools.partial(back, stage, array) for stage in (3, 4, 5) for array in range(arrays)]
    )
    return enter, begin, ticks, drain, small_begin, small_step


def reduce_scratch(arrays, rows, model, bits):
    more = max(2 * (bits - 3), 1)
    return [
        pltpu.VMEM((arrays, 2, rows // 4, model), bf16),
        pltpu.VMEM((arrays, 2, rows // 8, model), bf16),
        pltpu.VMEM((arrays, 2, rows // 16, model), bf16),
        pltpu.VMEM((more, arrays, 2, rows // 16, model), bf16),
        pltpu.VMEM((arrays, 2, rows // 4, model), bf16),
        pltpu.VMEM((arrays, 2, rows // 8, model), bf16),
        pltpu.SemaphoreType.DMA((bits + 3, arrays, 2)),
        pltpu.SemaphoreType.DMA((bits + 3, arrays, 2)),
    ]


def backward_kernel(
    shards,
    bits,
    pages_here,
    x_ref,
    box_x_ref,
    box_y_ref,
    rows_ref,
    grad_hidden_ref,
    qkv_ref,
    probs_ref,
    inverse_ref,
    context_ref,
    gathered_ref,
    part_up_ref,
    part_down_ref,
    grad_input_ref,
    grad_pack_ref,
    sums_ref,
    grad_up_ref,
    grad_down_ref,
    weights,
    copy_sem,
    grad_qkv,
    grad_context,
    grad_probs,
    small_scores,
    pack_total,
    bias_total,
    levels_total,
    summed,
    *scratch,
):
    page = pl.program_id(0)
    pages = pl.num_programs(0)
    steps_here = pages_here
    place = lax.axis_index("tensor")
    width, model = x_ref.shape
    heads = model // HEAD_DIM
    own = model // shards
    own_heads = heads // shards
    bins = 64
    enter, begin, ticks, drain, _, _ = reduce_steps(
        bits, (part_up_ref, part_down_ref), (summed.at[0], summed.at[1]), (), scratch
    )
    weight_copies = [
        pltpu.make_async_copy(gathered_ref.at[:, pl.ds(kind * own, own)], weights.at[kind], copy_sem.at[kind])
        for kind in range(4)
    ]
    stores = [
        pltpu.make_async_copy(summed.at[index], target, copy_sem.at[4 + index])
        for index, target in enumerate((grad_up_ref, grad_down_ref))
    ]

    @pl.when(page == 0)
    def _():
        for copy in weight_copies:
            copy.start()
        enter()
        begin()
        pack_total[...] = jnp.zeros_like(pack_total)
        bias_total[...] = jnp.zeros_like(bias_total)
        levels_total[...] = jnp.zeros_like(levels_total)
        sums_ref[...] = jnp.zeros_like(sums_ref)
        for copy in weight_copies:
            copy.wait()

    points = 5

    def point(index):
        for at, act in enumerate(ticks):
            where = (at + 1) * points * steps_here // (len(ticks) + 1) - 1
            if where % points == index:
                pl.when(page == where // points)(act)

    grad_hidden = grad_hidden_ref[...]
    grad_low = grad_hidden.astype(bf16)
    grad_context[...] = nt(weights[3].reshape(model, model), grad_low)
    hot = one_hot_columns(box_x_ref, box_y_ref, bins)
    back_hot = one_hot_columns(box_x_ref, box_y_ref, bins, True)

    def order(at):
        return lax.rem(place * own_heads + at, heads)

    def rows_of(at):
        return pl.ds(pl.multiple_of(order(at) * HEAD_DIM, HEAD_DIM), HEAD_DIM)

    def lead(at):
        rows = rows_of(at)
        grad_mixed = (grad_context[rows] * inverse_ref[0, order(at)]).astype(bf16)
        grad_probs[at % 2] = tn(qkv_ref[0, 2, rows], grad_mixed)
        delta = jnp.sum(
            grad_mixed.astype(f32) * context_ref[0, rows].astype(f32), axis=0, keepdims=True
        )
        return grad_mixed, delta

    def soften(at, delta):
        probs = probs_ref[0, order(at)].astype(f32)
        small_scores[at % 2] = (probs * (grad_probs[at % 2] - delta)).astype(bf16)

    def mix(at, grad_mixed):
        rows = rows_of(at)
        query = qkv_ref[0, 0, rows]
        key = qkv_ref[0, 1, rows]
        grad_scores = small_scores[at % 2]
        grad_value = nt(grad_mixed, probs_ref[0, order(at)])
        grad_key = nt(query, grad_scores) * LN2
        both = nn(jnp.concatenate([key, hot], axis=0) if at < own_heads else key, grad_scores)
        grad_qkv[0, rows] = (both[0:HEAD_DIM] * HEAD_DIM**-0.5).astype(bf16)
        grad_qkv[1, rows] = grad_key.astype(bf16)
        grad_qkv[2, rows] = grad_value.astype(bf16)
        if at < own_heads:
            levels_total[at] += nt(both[HEAD_DIM:].astype(bf16), back_hot)

    point(0)
    kept = [lead(0)]
    for at in range(heads):
        if at + 1 < heads:
            kept.append(lead(at + 1))
        soften(at, kept[at][1])
        if at > 0:
            mix(at - 1, kept[at - 1][0])
        if at % 3 == 2 and at + 1 < heads:
            point(1 + at // 3)
    mix(heads - 1, kept[-1][0])
    point(4)
    tokens = x_ref[...].astype(f32)
    xhat, inverse = norm_parts(tokens)
    low = (xhat * rows_ref[0:1, :] + rows_ref[1:2, :]).astype(bf16)
    mine = pl.ds(pl.multiple_of(place * own, own), own)
    stacked = jnp.concatenate([grad_qkv[kind, mine] for kind in range(3)], axis=0)
    pack_total[0 : 3 * own, :] += nn(stacked, low)
    pack_total[3 * own :, :] += nn(context_ref[0, mine], grad_low)
    wide = stacked.astype(f32)
    folded = wide[:, 0:BLOCK]
    for at in range(1, width // BLOCK):
        folded = folded + wide[:, at * BLOCK : (at + 1) * BLOCK]
    bias_total[...] += folded
    grad_normed = tn(grad_qkv[0], weights[0].reshape(model, model))
    for kind in (1, 2):
        grad_normed = grad_normed + tn(grad_qkv[kind], weights[kind].reshape(model, model))
    grad_total = grad_hidden + norm_grad(grad_normed, xhat, inverse, rows_ref[0:1, :])
    grad_input_ref[...] = grad_total.astype(bf16)
    sums_ref[0:1, :] += jnp.sum(grad_normed * xhat, axis=0, keepdims=True)
    sums_ref[1:2, :] += jnp.sum(grad_normed, axis=0, keepdims=True)

    @pl.when(page == pages - 1)
    def _():
        grad_pack_ref[...] = pack_total[...].astype(bf16)
        row = jnp.sum(bias_total[...].T, axis=0, keepdims=True)
        sums_ref[2:3, 0:own] = row[:, 0:own]
        sums_ref[3:4, 0:own] = row[:, 2 * own : 3 * own]
        lane = lax.broadcasted_iota(jnp.int32, (bins, 2 * bins), 1)
        for one in range(own_heads):
            for kind in range(2):
                block = levels_total[one, kind * bins : (kind + 1) * bins, :]
                inside = lane >= bins if kind else lane < bins
                rolled = pltpu.roll(jnp.where(inside, block, 0.0), kind * bins, 1, stride=1, stride_axis=0)
                at = (kind * own_heads + one) * 2 * bins
                sums_ref[4:5, at : at + 2 * bins] = jnp.sum(rolled, axis=0, keepdims=True)
        for copy in stores:
            copy.start()
        drain()
        for copy in stores:
            copy.wait()


def reduce_kernel(bits, part_ref, small_one_ref, small_two_ref, sum_ref, sum_one_ref, sum_two_ref, *scratch):
    enter, begin, ticks, drain, small_begin, small_step = reduce_steps(
        bits, (part_ref,), (sum_ref,), (small_one_ref, small_two_ref), scratch
    )
    enter()
    begin()
    small_begin()
    for at, act in enumerate(ticks):
        act()
        if at < 3:
            small_step(at)
    for bit in range(3, bits):
        small_step(bit)
    drain()
    sum_one_ref[...] = scratch[8][0, 2 * bits - 1]
    sum_two_ref[...] = scratch[8][1, 2 * bits - 1]


def finish_kernel(pack_ref, up_ref, down_ref, one_ref, two_ref, qkv, qv_bias, out, up, down, tables, rows):
    own = out.shape[0]
    bins = tables.shape[-1]
    for kind in range(3):
        qkv[kind] = pack_ref[kind * own : (kind + 1) * own, :].astype(f32)
    out[...] = pack_ref[3 * own :, :].astype(f32)
    up[...] = up_ref[...].astype(f32)
    down[...] = down_ref[...].astype(f32)
    qv_bias[...] = one_ref[2:4, 0:own]
    rows[0:2, :] = one_ref[0:2, :]
    rows[2:7, :] = two_ref[0:5, :]
    rows[7:8, :] = one_ref[7:8, :]
    m = lax.broadcasted_iota(jnp.int32, (2 * bins, bins), 0)
    level = lax.broadcasted_iota(jnp.int32, (2 * bins, bins), 1)
    pick = jnp.where(jnp.clip(m - (bins - 1), -(bins // 2), bins // 2 - 1) + bins // 2 == level, 1.0, 0.0)
    own_heads = tables.shape[0]
    for one in range(own_heads):
        for kind in range(2):
            at = (kind * own_heads + one) * 2 * bins
            line = jnp.broadcast_to(one_ref[4:5, at : at + 2 * bins], (8, 2 * bins))
            folded = lax.dot_general(
                line, pick, (((1,), (0,)), ((), ())), precision=lax.Precision.HIGHEST, preferred_element_type=f32
            )
            tables[one, kind : kind + 1, :] = folded[0:1]


ANYWHERE = pl.BlockSpec(memory_space=pl.ANY)
IN_VMEM = pl.BlockSpec(memory_space=pltpu.VMEM)


def whole(shape):
    return pl.BlockSpec(shape, lambda *_: (0,) * len(shape), pipeline_mode=pl.Buffered(1))


def page_rows(model):
    return pl.BlockSpec((PAGE, model), lambda p, *_: (p, 0))


def page_block(*shape):
    return pl.BlockSpec((1,) + shape, lambda p, *_: (p,) + (0,) * len(shape))


def params(collective_id=None):
    if collective_id is None:
        return pltpu.CompilerParams(vmem_limit_bytes=VMEM_LIMIT)
    return pltpu.CompilerParams(
        vmem_limit_bytes=VMEM_LIMIT, collective_id=collective_id, has_side_effects=True
    )


def attention_forward(shards, counts, inputs, keep, box_x, box_y, rows, bias, tables, qkv_weight, out_weight, up, down):
    rows_here, model = inputs.shape
    pages = rows_here // PAGE
    own = model // shards
    bins = tables.shape[-1]
    heads = model // HEAD_DIM
    gathered = jax.ShapeDtypeStruct((shards,) + up.shape, bf16)
    return pl.pallas_call(
        functools.partial(forward_kernel, shards),
        out_shape=(
            jax.ShapeDtypeStruct((pages, 3, model, PAGE), bf16),
            jax.ShapeDtypeStruct((pages, heads, PAGE, PAGE), bf16),
            jax.ShapeDtypeStruct((pages, heads, 1, PAGE), f32),
            jax.ShapeDtypeStruct((pages, model, PAGE), bf16),
            jax.ShapeDtypeStruct((rows_here, model), f32),
            gathered,
            gathered,
            gathered,
            jax.ShapeDtypeStruct((shards,) + rows.shape, f32),
        ),
        grid_spec=pltpu.PrefetchScalarGridSpec(
            num_scalar_prefetch=1,
            grid=(pages,),
            in_specs=[page_rows(model)]
            + [page_block(1, PAGE)] * 3
            + [whole(rows.shape), whole(bias.shape), whole(tables.shape)]
            + [ANYWHERE] * 4,
            out_specs=(
                page_block(3, model, PAGE),
                page_block(heads, PAGE, PAGE),
                page_block(heads, 1, PAGE),
                page_block(model, PAGE),
                page_rows(model),
                ANYWHERE,
                ANYWHERE,
                ANYWHERE,
                ANYWHERE,
            ),
            scratch_shapes=[
                pltpu.VMEM((4, shards, own, model), bf16),
                pltpu.SemaphoreType.DMA((14,)),
                pltpu.VMEM((3,) + up.shape, bf16),
                pltpu.VMEM((shards,) + bias.shape, f32),
                pltpu.VMEM((shards,) + tables.shape, f32),
            ]
            + gather_semaphores(3, shards)
            + [
                pltpu.VMEM((2, model, 128), f32),
                pltpu.VMEM((heads * 2 * bins, 2 * bins), bf16),
                pltpu.VMEM((heads * 2 * bins, PAGE), bf16),
                pltpu.VMEM((2, PAGE, PAGE), f32),
            ],
        ),
        compiler_params=params(1),
        name="attention_forward",
    )(counts, inputs, keep, box_x, box_y, rows, bias, tables, qkv_weight, out_weight, up, down)


def feed_forward(counts, place, hidden, cotangent, rows, rows_all, up_all, down_all):
    rows_here, model = hidden.shape
    pages = rows_here // PAGE
    shards, _, hidden_units = up_all.shape
    return pl.pallas_call(
        mlp_kernel,
        out_shape=(
            jax.ShapeDtypeStruct((rows_here, model), bf16),
            jax.ShapeDtypeStruct((rows_here, model), f32),
            jax.ShapeDtypeStruct((model, hidden_units), bf16),
            jax.ShapeDtypeStruct((hidden_units, model), bf16),
            jax.ShapeDtypeStruct((8, model), f32),
        ),
        grid_spec=pltpu.PrefetchScalarGridSpec(
            num_scalar_prefetch=2,
            grid=(pages,),
            in_specs=[
                page_rows(model),
                page_rows(model),
                whole(rows.shape),
                whole(rows_all.shape),
                whole((shards, model, hidden_units)),
                whole((shards, hidden_units, model)),
            ],
            out_specs=(
                page_rows(model),
                page_rows(model),
                whole((model, hidden_units)),
                whole((hidden_units, model)),
                whole((8, model)),
            ),
            scratch_shapes=[
                pltpu.VMEM((model, hidden_units), f32),
                pltpu.VMEM((hidden_units, model), f32),
                pltpu.VMEM((PAGE, model), bf16),
                pltpu.VMEM((PAGE, model), bf16),
                pltpu.VMEM((PAGE, model), f32),
                pltpu.VMEM((PAGE, model), f32),
                pltpu.VMEM((shards, PAGE, hidden_units), bf16),
                pltpu.VMEM((shards, PAGE, hidden_units), bf16),
                pltpu.VMEM((2, PAGE, hidden_units), f32),
                pltpu.VMEM((2, PAGE, hidden_units), f32),
            ],
        ),
        compiler_params=params(),
        name="feed_forward",
    )(counts, place, hidden, cotangent, rows, rows_all, up_all, down_all)


def attention_backward(
    shards,
    devices,
    inputs,
    box_x,
    box_y,
    rows,
    grad_hidden,
    qkv,
    probs,
    inverse,
    context,
    gathered,
    part_up,
    part_down,
):
    rows_here, model = inputs.shape
    pages, heads = probs.shape[:2]
    own = model // shards
    bins = 64
    bits = devices.bit_length() - 1
    return pl.pallas_call(
        functools.partial(backward_kernel, shards, bits, pages),
        out_shape=(
            jax.ShapeDtypeStruct((rows_here, model), bf16),
            jax.ShapeDtypeStruct((4 * own, model), bf16),
            jax.ShapeDtypeStruct((8, model), f32),
            jax.ShapeDtypeStruct(part_up.shape, bf16),
            jax.ShapeDtypeStruct(part_down.shape, bf16),
        ),
        grid_spec=pltpu.PrefetchScalarGridSpec(
            num_scalar_prefetch=0,
            grid=(pages,),
            in_specs=[page_rows(model)]
            + [page_block(1, PAGE)] * 2
            + [whole(rows.shape)]
            + [
                page_rows(model),
                page_block(3, model, PAGE),
                page_block(heads, PAGE, PAGE),
                page_block(heads, 1, PAGE),
                page_block(model, PAGE),
                ANYWHERE,
                whole(part_up.shape),
                whole(part_down.shape),
            ],
            out_specs=(
                page_rows(model),
                whole((4 * own, model)),
                whole((8, model)),
                ANYWHERE,
                ANYWHERE,
            ),
            scratch_shapes=[
                pltpu.VMEM((4, shards, own, model), bf16),
                pltpu.SemaphoreType.DMA((6,)),
                pltpu.VMEM((3, model, PAGE), bf16),
                pltpu.VMEM((model, PAGE), f32),
                pltpu.VMEM((2, PAGE, PAGE), f32),
                pltpu.VMEM((2, PAGE, PAGE), bf16),
                pltpu.VMEM((4 * own, model), f32),
                pltpu.VMEM((3 * own, BLOCK), f32),
                pltpu.VMEM((own // HEAD_DIM, 2 * bins, 2 * bins), f32),
                pltpu.VMEM((2,) + part_up.shape, bf16),
            ]
            + reduce_scratch(2, part_up.shape[0], model, bits),
        ),
        compiler_params=params(2),
        name="attention_backward",
    )(
        inputs,
        box_x,
        box_y,
        rows,
        grad_hidden,
        qkv,
        probs,
        inverse,
        context,
        gathered,
        part_up,
        part_down,
    )


def reduce_grads(devices, part, small_one, small_two):
    rows, model = part.shape
    bits = devices.bit_length() - 1
    return pl.pallas_call(
        functools.partial(reduce_kernel, bits),
        out_shape=(jax.ShapeDtypeStruct(part.shape, bf16),)
        + tuple(jax.ShapeDtypeStruct(small.shape, f32) for small in (small_one, small_two)),
        in_specs=[IN_VMEM] * 3,
        out_specs=(IN_VMEM,) * 3,
        scratch_shapes=reduce_scratch(1, rows, model, bits)
        + [
            pltpu.VMEM((2, 2 * bits) + small_one.shape, f32),
            pltpu.SemaphoreType.DMA((2, bits)),
            pltpu.SemaphoreType.DMA((2, bits)),
        ],
        compiler_params=params(3),
        name="reduce_grads",
    )(part, small_one, small_two)


def finish_grads(pack, up, down, small_one, small_two, bins):
    own, model = pack.shape[0] // 4, pack.shape[1]
    return pl.pallas_call(
        finish_kernel,
        out_shape=(
            jax.ShapeDtypeStruct((3, own, model), f32),
            jax.ShapeDtypeStruct((2, own), f32),
            jax.ShapeDtypeStruct((own, model), f32),
            jax.ShapeDtypeStruct(up.shape, f32),
            jax.ShapeDtypeStruct(down.shape, f32),
            jax.ShapeDtypeStruct((own // HEAD_DIM, 2, bins), f32),
            jax.ShapeDtypeStruct(small_one.shape, f32),
        ),
        in_specs=[IN_VMEM] * 5,
        out_specs=(IN_VMEM,) * 7,
        compiler_params=params(),
        name="finish_grads",
    )(pack, up, down, small_one, small_two)


def on_device(
    inputs,
    cotangent,
    counts,
    keep_mask,
    box_x,
    box_y,
    gain_one,
    shift_one,
    w_qkv,
    b_qv,
    w_out,
    b_out,
    gain_two,
    shift_two,
    w_up,
    b_up,
    w_down,
    b_down,
    rel_tables,
    *,
    devices,
):
    rows_here, model = inputs.shape
    pages = rows_here // PAGE
    own_heads, bins = rel_tables.shape[1:]
    own = own_heads * HEAD_DIM
    shards = model // own
    place = lax.axis_index("tensor").astype(jnp.int32).reshape(1)
    paged = lambda array: array.reshape(pages, 1, PAGE)
    keep_mask, box_x, box_y = paged(keep_mask), paged(box_x), paged(box_y)
    rows = jnp.concatenate([gain_one, shift_one, b_out, gain_two, shift_two, b_down, b_up, b_up]).reshape(8, model)

    qkv, probs, inverse, context, hidden, gathered, up_all, down_all, rows_all = attention_forward(
        shards,
        counts,
        inputs,
        keep_mask,
        box_x,
        box_y,
        rows,
        b_qv,
        rel_tables.transpose(1, 0, 2),
        w_qkv.transpose(0, 2, 1).reshape(3 * own, model),
        w_out,
        w_up,
        w_down,
    )
    out, grad_hidden, part_up, part_down, small_two = feed_forward(
        counts, place, hidden, cotangent, rows, rows_all, up_all, down_all
    )
    grad_input, part_pack, small_one, grad_up, grad_down = attention_backward(
        shards,
        devices,
        inputs,
        box_x,
        box_y,
        rows,
        grad_hidden,
        qkv,
        probs,
        inverse,
        context,
        gathered,
        part_up,
        part_down,
    )
    grad_pack, small_one, small_two = reduce_grads(devices, part_pack, small_one, small_two)
    grad_qkv, grad_b_qv, grad_w_out, grad_w_up, grad_w_down, grad_tables, sums = finish_grads(
        grad_pack, grad_up, grad_down, small_one, small_two, bins
    )
    return (
        out,
        grad_input,
        grad_qkv.transpose(0, 2, 1),
        grad_b_qv,
        grad_w_out,
        sums[4],
        sums[0],
        sums[1],
        sums[2],
        sums[3],
        grad_w_up,
        sums[6],
        grad_w_down,
        sums[5],
        grad_tables.transpose(1, 0, 2),
    )


def solution(mesh):
    placed = (
        P("dp", None),
        P("dp", None),
        P("dp"),
        P("dp"),
        P("dp"),
        P("dp"),
        P(),
        P(),
        P(None, None, "tensor"),
        P(None, "tensor"),
        P("tensor", None),
        P(),
        P(),
        P(),
        P(None, "tensor"),
        P("tensor"),
        P("tensor", None),
        P(),
        P(None, "tensor", None),
    )
    return jax.shard_map(
        functools.partial(on_device, devices=mesh.shape["dp"]),
        mesh=mesh,
        in_specs=placed,
        out_specs=(
            P("dp", None),
            P("dp", None),
            P(None, None, "tensor"),
            P(None, "tensor"),
            P("tensor", None),
            P(),
            P(),
            P(),
            P(),
            P(),
            P(None, "tensor"),
            P("tensor"),
            P("tensor", None),
            P(),
            P(None, "tensor", None),
        ),
        check_vma=False,
    )
```

```python
import functools
import jax
import jax.numpy as jnp
from jax import lax
from jax.experimental import pallas as pl
from jax.experimental.pallas import tpu as pltpu
from jax.sharding import PartitionSpec as P

HEAD_DIM = 64
PAGE = 512
BLOCK = 128
epsilon = 1e-05
masked_score = -1e30
LOG2E = 1.4426950408889634
LN2 = 0.6931471805599453
bf16 = jnp.bfloat16
f32 = jnp.float32
VMEM_LIMIT = 60 << 20


def dot(left, right, left_dim, right_dim):
    return lax.dot_general(
        left, right, (((left_dim,), (right_dim,)), ((), ())), preferred_element_type=f32
    )


def nn(left, right):
    return dot(left, right, 1, 0)


def nt(left, right):
    return dot(left, right, 1, 1)


def tn(left, right):
    return dot(left, right, 0, 0)


def norm_parts(rows):
    average = jnp.mean(rows, axis=-1, keepdims=True)
    centered = rows - average
    variance = jnp.mean(centered * centered, axis=-1, keepdims=True)
    inverse = lax.rsqrt(variance + epsilon)
    return centered * inverse, inverse


def norm_grad(grad_out, xhat, inverse, gain):
    scaled = grad_out * gain
    mean_one = jnp.mean(scaled, axis=-1, keepdims=True)
    mean_two = jnp.mean(scaled * xhat, axis=-1, keepdims=True)
    return inverse * (scaled - mean_one - xhat * mean_two)


def one_hot_columns(box_x_ref, box_y_ref, bins, reverse=False):
    width = box_x_ref.shape[-1]
    levels = lax.broadcasted_iota(jnp.int32, (bins, width), 0)
    if reverse:
        levels = (bins - 1) - levels
    hot_x = jnp.where(levels == box_x_ref[0], 1.0, 0.0)
    hot_y = jnp.where(levels == box_y_ref[0], 1.0, 0.0)
    return jnp.concatenate([hot_x, hot_y], axis=0).astype(bf16)


def by_halves(count, body):
    body(PAGE)


def neighbours(axis):
    core = axis % 2
    side_x = (axis // 2) % 2
    side_y = (axis // 4) % 2
    return core, side_x, side_y, 1 - 2 * core, 2 - 4 * side_x, 4 - 8 * side_y


def flipped(index, mask):
    result, bit = index, 1
    while bit <= mask:
        if mask & bit:
            result = result + bit - 2 * bit * ((index // bit) % 2)
        bit *= 2
    return result


def greet(peers):
    barrier = pltpu.get_barrier_semaphore()
    for dp, tensor in peers:
        pl.semaphore_signal(
            barrier, inc=1, device_id={"dp": dp, "tensor": tensor}, device_id_type=pl.DeviceIdType.MESH
        )
    pl.semaphore_wait(barrier, len(peers))


KIND_Z, KIND_X, KIND_Y, KIND_VIA_X, KIND_VIA_Y, KIND_CORE = 0, 1, 2, 3, 4, 5
KINDS = 9


def gather_steps(shards, sources, targets, small_sources, small_targets, send_sem, recv_sem):
    arrays = len(sources)
    place = lax.axis_index("tensor")
    lane = lax.axis_index("dp")
    core, side_x, side_y, to_core, to_x, to_y = neighbours(lane)
    mine = lane % 8
    rows = targets[0].shape[1] // 8
    half = rows // 2
    hops = range(1, shards)

    def piece(index, start=0, size=rows):
        return pl.ds(pl.multiple_of(index * rows + start, 16), size)

    def remote(kind, array, hop, source, target, dp, tensor):
        return pltpu.make_async_remote_copy(
            src_ref=source,
            dst_ref=target,
            send_sem=send_sem.at[kind, array, hop - 1],
            recv_sem=recv_sem.at[kind, array, hop - 1],
            device_id={"dp": dp, "tensor": tensor},
            device_id_type=pl.DeviceIdType.MESH,
        )

    def within(kind, array, hop, region, step):
        ref = targets[array].at[flipped(place, hop), region]
        return remote(kind, array, hop, ref, ref, lane + step, place)

    def along(array, hop):
        source, target = sources[array].at[piece(mine)], targets[array].at[place, piece(mine)]
        return remote(KIND_Z, array, hop, source, target, lane, flipped(place, hop))

    def along_small(index, hop):
        source, target = small_sources[index], small_targets[index].at[place]
        return remote(1 + index, arrays, hop, source, target, lane, flipped(place, hop))

    def enter():
        greet(
            [(lane + step, place) for step in (to_core, to_x, to_y)] + [(lane, flipped(place, hop)) for hop in hops]
        )

    def begin():
        for array in range(arrays):
            for hop in hops:
                along(array, hop).start()
            if array == 0:
                for index in range(len(small_sources)):
                    for hop in hops:
                        along_small(index, hop).start()

    def arrive(array, hop):
        along(array, hop).wait_recv()
        within(KIND_X, array, hop, piece(mine), to_x).start()
        within(KIND_Y, array, hop, piece(mine), to_y).start()
        within(KIND_CORE, array, hop, piece(mine), to_core).start()

    def spread_near(array, hop):
        at = mine + to_x
        within(KIND_X, array, hop, piece(at), to_x).wait_recv()
        within(KIND_VIA_Y, array, hop, piece(at, 0, half), to_y).start()
        within(KIND_CORE + 1, array, hop, piece(at), to_core).start()
        at = mine + to_y
        within(KIND_Y, array, hop, piece(at), to_y).wait_recv()
        within(KIND_VIA_X, array, hop, piece(at, half, half), to_x).start()
        within(KIND_CORE + 2, array, hop, piece(at), to_core).start()

    def spread_far(array, hop):
        at = mine + to_x + to_y
        within(KIND_VIA_Y, array, hop, piece(at, 0, half), to_y).wait_recv()
        within(KIND_VIA_X, array, hop, piece(at, half, half), to_x).wait_recv()
        within(KIND_CORE + 3, array, hop, piece(at), to_core).start()

    def finish(array, hop):
        for index, shift in enumerate((0, to_x, to_y, to_x + to_y)):
            within(KIND_CORE + index, array, hop, piece(mine + to_core + shift), to_core).wait_recv()

    def drain(early):
        for hop in hops:
            if early:
                for index in range(len(small_sources)):
                    along_small(index, hop).wait()
                continue
            for array in range(arrays):
                along(array, hop).wait_send()
                within(KIND_X, array, hop, piece(mine), to_x).wait_send()
                within(KIND_Y, array, hop, piece(mine), to_y).wait_send()
                within(KIND_VIA_Y, array, hop, piece(mine + to_x, 0, half), to_y).wait_send()
                within(KIND_VIA_X, array, hop, piece(mine + to_y, half, half), to_x).wait_send()
                for index, shift in enumerate((0, to_x, to_y, to_x + to_y)):
                    within(KIND_CORE + index, array, hop, piece(mine + shift), to_core).wait_send()

    items = [(array, hop) for array in range(arrays) for hop in hops]
    stages = (arrive, spread_near, spread_far, finish)

    def act(stage, item):
        stages[stage](*items[item])

    return enter, begin, act, len(items), drain


def gather_order(items, first):
    start = []
    for tick in range(first + 2):
        for stage in (0, 1, 2):
            if 0 <= tick - stage < first:
                start.append((stage, tick - stage))
            elif stage == 0 and tick < min(items, first + 2):
                later = (stage, tick)
                start.append(later)
    start += [(3, item) for item in range(first)]
    ready = first + 2
    groups = []
    for tick in range(first + 1, items + 3):
        group = [(stage, tick - stage) for stage in (3, 2, 1) if first <= tick - stage < items]
        if ready <= tick + 1 < items:
            group.append((0, tick + 1))
        groups.append(group)
    return start, groups


def gather_semaphores(arrays, shards):
    return [pltpu.SemaphoreType.DMA((KINDS, arrays + 1, shards - 1))] * 2


def forward_kernel(
    shards,
    counts_ref,
    x_ref,
    keep_ref,
    box_x_ref,
    box_y_ref,
    gain_one_ref,
    shift_one_ref,
    out_bias_ref,
    gain_two_ref,
    shift_two_ref,
    down_bias_ref,
    up_bias_ref,
    bias_ref,
    tables_ref,
    qkv_weight_ref,
    out_weight_ref,
    up_ref,
    down_ref,
    qkv_ref,
    probs_ref,
    inverse_ref,
    context_ref,
    hidden_ref,
    gathered_ref,
    up_all_ref,
    down_all_ref,
    rows_ref,
    rows_all_ref,
    rows,
    weights,
    copy_sem,
    bounce,
    bias_all,
    tables_all,
    send_sem,
    recv_sem,
    bias_columns,
    toeplitz,
    spread,
    scores,
):
    page = pl.program_id(0)
    pages = counts_ref.shape[0]
    place = lax.axis_index("tensor")
    width, model = x_ref.shape
    heads = model // HEAD_DIM
    own = model // shards
    own_heads = heads // shards
    bins = tables_ref.shape[-1]
    split = qkv_weight_ref.shape[0]
    smalls, small_targets = (rows, bias_ref, tables_ref), (rows_all_ref, bias_all, tables_all)
    enter, begin, act, items, drain = gather_steps(
        shards,
        (bounce.at[0], up_ref, down_ref),
        (gathered_ref, up_all_ref, down_all_ref),
        smalls,
        small_targets,
        send_sem,
        recv_sem,
    )
    loads = [
        pltpu.make_async_copy(qkv_weight_ref, bounce.at[0, 0:split], copy_sem.at[0]),
        pltpu.make_async_copy(out_weight_ref, bounce.at[0, split:], copy_sem.at[1]),
        pltpu.make_async_copy(up_ref, bounce.at[1], copy_sem.at[2]),
        pltpu.make_async_copy(down_ref, bounce.at[2], copy_sem.at[3]),
    ]
    stores = [
        pltpu.make_async_copy(bounce.at[index], target.at[place], copy_sem.at[4 + index])
        for index, target in enumerate((gathered_ref, up_all_ref, down_all_ref))
    ] + [
        pltpu.make_async_copy(source, target.at[place], copy_sem.at[7 + index])
        for index, (source, target) in enumerate(zip(smalls, small_targets))
    ]
    weight_copies = [
        pltpu.make_async_copy(
            gathered_ref.at[:, pl.ds(kind * own, own)], weights.at[kind], copy_sem.at[10 + kind]
        )
        for kind in range(4)
    ]
    start, groups = gather_order(items, shards - 1)

    @pl.when(page == 0)
    def _():
        for copy in loads:
            copy.start()
        vectors = (
            gain_one_ref,
            shift_one_ref,
            out_bias_ref,
            gain_two_ref,
            shift_two_ref,
            down_bias_ref,
            up_bias_ref,
            up_bias_ref,
        )
        for index, vector in enumerate(vectors):
            for part in range(model // 128):
                rows[index : index + 1, part * 128 : (part + 1) * 128] = vector[part : part + 1, :]
        rows_ref[...] = rows[...]
        enter()
        for copy in loads[0:2]:
            copy.wait()
        begin()
        for copy in loads[2:4]:
            copy.wait()
        for copy in stores:
            copy.start()
        for stage, item in start:
            act(stage, item)
        for copy in stores:
            copy.wait()
        for copy in weight_copies:
            copy.start()
        drain(True)
        for shard in range(shards):
            span = slice(shard * own, (shard + 1) * own)
            for kind in range(2):
                wide = jnp.broadcast_to(bias_all[shard, kind : kind + 1, :], (128, own))
                bias_columns[kind, span, :] = wide.T
        m = lax.broadcasted_iota(jnp.int32, (bins, 2 * bins), 1)
        signed = jnp.where(m >= bins, 2 * bins - m, -m)
        level = lax.broadcasted_iota(jnp.int32, (bins, 2 * bins), 0)
        pick = jnp.where(jnp.clip(signed, -(bins // 2), bins // 2 - 1) + bins // 2 == level, 1.0, 0.0).astype(bf16)
        lane = lax.broadcasted_iota(jnp.int32, (bins, 2 * bins), 1)
        for shard in range(shards):
            for one in range(own_heads):
                at = (shard * own_heads + one) * 2 * bins
                for kind in range(2):
                    table = (tables_all[shard, one, kind : kind + 1, :] * LOG2E).astype(bf16)
                    line = nn(jnp.broadcast_to(table, (bins, bins)), pick)
                    rolled = pltpu.roll(line, kind * bins, 1, stride=1, stride_axis=0)
                    inside = lane >= bins if kind else lane < bins
                    toeplitz[at + kind * bins : at + (kind + 1) * bins, :] = jnp.where(inside, rolled, 0.0).astype(bf16)
        for copy in weight_copies:
            copy.wait()

    points = 5

    def run_group(group):
        for stage, item in group:
            act(stage, item)

    def point(index):
        for at, group in enumerate(groups):
            where = (at + 1) * points * pages // (len(groups) + 1) - 1
            if where % points == index:
                pl.when(page == where // points)(functools.partial(run_group, group))

    tokens = x_ref[...].astype(f32)
    xhat, _ = norm_parts(tokens)
    low = (xhat * rows[0:1, :] + rows[1:2, :]).astype(bf16)
    for kind in range(3):
        product = nt(weights[kind].reshape(model, model), low)
        if kind == 0:
            product = (product + bias_columns[0, :, 0:1]) * (LOG2E * HEAD_DIM**-0.5)
        if kind == 2:
            product = product + bias_columns[1, :, 0:1]
        qkv_ref[0, kind] = product.astype(bf16)
    hot = one_hot_columns(box_x_ref, box_y_ref, bins)
    spread[...] = nn(toeplitz[...], hot).astype(bf16)
    lane = lax.broadcasted_iota(jnp.int32, (1, width), 1)
    open_key = (lane < counts_ref[page]) & (keep_ref[0] == 1)
    mask_row = jnp.where(open_key, 0.0, masked_score)
    first = lax.broadcasted_iota(jnp.int32, (HEAD_DIM, width), 0) == 0
    key_pad = jnp.where(first, mask_row, 0.0).astype(bf16)
    query_pad = jnp.where(first, 1.0, 0.0).astype(bf16)
    ones = jnp.ones((16, width), bf16)
    eye = lax.broadcasted_iota(jnp.int32, (BLOCK, BLOCK), 0) == lax.broadcasted_iota(jnp.int32, (BLOCK, BLOCK), 1)

    def score(index, slot):
        span = slice(index * HEAD_DIM, (index + 1) * HEAD_DIM)
        query = qkv_ref[0, 0, span]
        key = qkv_ref[0, 1, span]
        bias = spread[index * 2 * bins : (index + 1) * 2 * bins, :]
        left = jnp.concatenate([key, key_pad, hot], axis=0)
        right = jnp.concatenate([query, query_pad, bias], axis=0)
        scores[slot] = tn(left, right)
        return jnp.sum(query.astype(f32) * key.astype(f32), axis=0, keepdims=True) + jnp.sum(
            bias.astype(f32) * hot.astype(f32), axis=0, keepdims=True
        )

    def soften(index, slot, own_score):
        for at in range(width // BLOCK):
            span = slice(at * BLOCK, (at + 1) * BLOCK)
            scores[slot, span, span] = jnp.where(eye, own_score[:, span], scores[slot, span, span])
        top = jnp.max(scores[slot], axis=0, keepdims=True)
        probs_ref[0, index] = jnp.exp2(scores[slot] - top).astype(bf16)

    def mix(index):
        span = slice(index * HEAD_DIM, (index + 1) * HEAD_DIM)
        mixed = nn(jnp.concatenate([qkv_ref[0, 2, span], ones], axis=0), probs_ref[0, index])
        inverse = 1.0 / mixed[HEAD_DIM : HEAD_DIM + 1]
        inverse_ref[0, index] = inverse
        context_ref[0, span] = (mixed[0:HEAD_DIM] * inverse).astype(bf16)

    point(0)
    owns = [score(0, 0)]
    for at in range(heads):
        if at + 1 < heads:
            owns.append(score(at + 1, (at + 1) % 2))
        soften(at, at % 2, owns[at])
        if at > 0:
            mix(at - 1)
        if at % 3 == 2 and at + 1 < heads:
            point(1 + at // 3)
    mix(heads - 1)
    point(4)
    attended = tn(context_ref[0], weights[3].reshape(model, model))
    hidden_ref[...] = tokens + attended + rows[2:3, :]

    @pl.when(page == pages - 1)
    def _():
        drain(False)


def mlp_kernel(
    counts_ref,
    place_ref,
    hidden_ref,
    cotangent_ref,
    rows_ref,
    bias_ref,
    up_ref,
    down_ref,
    out_ref,
    grad_hidden_ref,
    grad_up_ref,
    grad_down_ref,
    sums_ref,
    up_total,
    down_total,
    low_ref,
    gl_ref,
    down_acc,
    gn_acc,
    act_ref,
    gu_ref,
    upper_ref,
    grad_ref,
):
    page = pl.program_id(0)
    shards = up_ref.shape[0]
    place = place_ref[0]

    @pl.when(page == 0)
    def _():
        up_total[...] = jnp.zeros_like(up_total)
        down_total[...] = jnp.zeros_like(down_total)
        sums_ref[...] = jnp.zeros_like(sums_ref)

    count = counts_ref[page]

    def body(width):
        valid = lax.broadcasted_iota(jnp.int32, (width, 1), 0) < count
        hidden = hidden_ref[0:width, :]
        xhat, inverse = norm_parts(hidden)
        low = (xhat * rows_ref[3:4, :] + rows_ref[4:5, :]).astype(bf16)
        grad_result = jnp.where(valid, cotangent_ref[0:width, :].astype(f32), 0.0)
        grad_low = grad_result.astype(bf16)

        low_ref[0:width, :] = low
        gl_ref[0:width, :] = grad_low
        down_acc[0:width, :] = jnp.zeros((width, hidden.shape[1]), f32)
        gn_acc[0:width, :] = jnp.zeros((width, hidden.shape[1]), f32)

        def lead(at, slot):
            upper_ref[slot, 0:width, :] = nn(low_ref[0:width, :], up_ref[at]) + bias_ref[at, 6:7, :]
            grad_ref[slot, 0:width, :] = nt(gl_ref[0:width, :], down_ref[at])

        def bend(at, slot):
            upper = upper_ref[slot, 0:width, :]
            half = 0.5 * (1.0 + lax.erf(upper * 0.7071067811865476))
            density = jnp.exp(-0.5 * upper * upper) * 0.3989422804014327
            act_ref[at, 0:width, :] = (upper * half).astype(bf16)
            slope = half + upper * density
            gu_ref[at, 0:width, :] = (grad_ref[slot, 0:width, :] * slope).astype(bf16)

        def mix(at):
            down_acc[0:width, :] += nn(act_ref[at, 0:width, :], down_ref[at])
            gn_acc[0:width, :] += nt(gu_ref[at, 0:width, :], up_ref[at])

        lead(0, 0)
        for at in range(shards):
            if at + 1 < shards:
                lead(at + 1, (at + 1) % 2)
            bend(at, at % 2)
            if at > 0:
                mix(at - 1)
        mix(shards - 1)
        down_proj = down_acc[0:width, :]
        grad_normed = gn_acc[0:width, :]
        up_total[...] += tn(low_ref[0:width, :], gu_ref[place, 0:width, :])
        down_total[...] += tn(act_ref[place, 0:width, :], gl_ref[0:width, :])
        sums_ref[4:5, :] += jnp.sum(gu_ref[place, 0:width, :].astype(f32), axis=0, keepdims=True)
        result = jnp.where(valid, hidden + down_proj + rows_ref[5:6, :], 0.0)
        out_ref[0:width, :] = result.astype(bf16)
        grad_hidden = grad_result + norm_grad(grad_normed, xhat, inverse, rows_ref[3:4, :])
        grad_hidden_ref[0:width, :] = grad_hidden
        sums_ref[0:1, :] += jnp.sum(grad_normed * xhat, axis=0, keepdims=True)
        sums_ref[1:2, :] += jnp.sum(grad_normed, axis=0, keepdims=True)
        sums_ref[2:3, :] += jnp.sum(grad_hidden, axis=0, keepdims=True)
        sums_ref[3:4, :] += jnp.sum(grad_result, axis=0, keepdims=True)
        if width < PAGE:
            out_ref[width:PAGE, :] = jnp.zeros((PAGE - width, hidden.shape[1]), bf16)
            grad_hidden_ref[width:PAGE, :] = jnp.zeros((PAGE - width, hidden.shape[1]), f32)

    by_halves(count, body)

    @pl.when(page == pl.num_programs(0) - 1)
    def _():
        grad_up_ref[...] = up_total[...].astype(bf16)
        grad_down_ref[...] = down_total[...].astype(bf16)


def reduce_steps(bits, parts, sums, smalls, scratch):
    arrays = len(parts)
    got_core, got_one, got_two, got_more, kept_core, kept_one, send_sem, recv_sem = scratch[0:8]
    place = lax.axis_index("tensor")
    lane = lax.axis_index("dp")
    core, side_x, side_y, to_core, to_x, to_y = neighbours(lane)
    steps = [to_core, to_x, to_y]
    for bit in range(3, bits):
        size = 2**bit
        steps.append(size - 2 * size * ((lane // size) % 2))
    rows = parts[0].shape[0]
    quarter, eighth, sixteenth = rows // 4, rows // 8, rows // 16
    order = ((side_x, side_y, to_x, to_y), (side_y, side_x, to_y, to_x))
    sides = range(2)

    def device(step):
        return {"dp": lane + step, "tensor": place}

    def remote(stage, array, side, source, target, step):
        return pltpu.make_async_remote_copy(
            src_ref=source,
            dst_ref=target,
            send_sem=send_sem.at[stage, array, side],
            recv_sem=recv_sem.at[stage, array, side],
            device_id=device(step),
            device_id_type=pl.DeviceIdType.MESH,
        )

    def span(side, of_core, one=None, two=None):
        start = side * (rows // 2) + of_core * quarter
        if one is None:
            return pl.ds(pl.multiple_of(start, 16), quarter)
        start = start + one * eighth
        if two is None:
            return pl.ds(pl.multiple_of(start, 16), eighth)
        return pl.ds(pl.multiple_of(start + two * sixteenth, 16), sixteenth)

    def part_of(index, size):
        return pl.ds(pl.multiple_of(index * size, 16), size)

    def core_copy(array, side):
        return remote(0, array, side, parts[array].at[span(side, 1 - core)], got_core.at[array, side], to_core)

    def one_copy(array, side):
        one, two, to_one, to_two = order[side]
        source = kept_core.at[array, side, part_of(1 - one, eighth)]
        return remote(1, array, side, source, got_one.at[array, side], to_one)

    def two_copy(array, side):
        one, two, to_one, to_two = order[side]
        source = kept_one.at[array, side, part_of(1 - two, sixteenth)]
        return remote(2, array, side, source, got_two.at[array, side], to_two)

    def more_copy(array, side, bit):
        source = got_more.at[bit - 3, array, side]
        return remote(bit + 3, array, side, source, got_more.at[bits - 3 + bit - 3, array, side], steps[bit])

    def back_copy(stage, array, side, inward):
        one, two, to_one, to_two = order[side]
        if stage == 3:
            region, step = span(side, core, one, 1 - two if inward else two), to_two
        elif stage == 4:
            region, step = span(side, core, 1 - one if inward else one), to_one
        else:
            region, step = span(side, 1 - core if inward else core), to_core
        ref = sums[array].at[region]
        return remote(stage, array, side, ref, ref, step)

    def enter():
        greet([(lane + step, place) for step in steps])

    def begin():
        for array in range(arrays):
            for side in sides:
                core_copy(array, side).start()

    def add_core(array):
        for side in sides:
            keep = span(side, core)
            core_copy(array, side).wait_recv()
            kept_core[array, side] = (
                parts[array][keep, :].astype(f32) + got_core[array, side].astype(f32)
            ).astype(bf16)
            one_copy(array, side).start()

    def add_one(array):
        for side in sides:
            one, two, to_one, to_two = order[side]
            one_copy(array, side).wait_recv()
            kept_one[array, side] = (
                kept_core[array, side, part_of(one, eighth), :].astype(f32) + got_one[array, side].astype(f32)
            ).astype(bf16)
            two_copy(array, side).start()

    def add_two(array):
        for side in sides:
            one, two, to_one, to_two = order[side]
            two_copy(array, side).wait_recv()
            total = (
                kept_one[array, side, part_of(two, sixteenth), :].astype(f32) + got_two[array, side].astype(f32)
            ).astype(bf16)
            for bit in range(3, bits):
                got_more[bit - 3, array, side] = total
                more_copy(array, side, bit).start()
                more_copy(array, side, bit).wait()
                total = (total.astype(f32) + got_more[bits - 3 + bit - 3, array, side].astype(f32)).astype(bf16)
            sums[array][span(side, core, one, two), :] = total
            back_copy(3, array, side, False).start()

    def back(stage, array):
        for side in sides:
            back_copy(stage, array, side, True).wait_recv()
            if stage < 5:
                back_copy(stage + 1, array, side, False).start()

    def small_copy(index, bit):
        got, small_send, small_recv = scratch[8:11]
        source = smalls[index] if bit == 0 else got.at[index, bits + bit - 1]
        return pltpu.make_async_remote_copy(
            src_ref=source,
            dst_ref=got.at[index, bit],
            send_sem=small_send.at[index, bit],
            recv_sem=small_recv.at[index, bit],
            device_id=device(steps[bit]),
            device_id_type=pl.DeviceIdType.MESH,
        )

    def small_begin():
        for index in range(len(smalls)):
            small_copy(index, 0).start()

    def small_step(bit):
        got = scratch[8]
        for index in range(len(smalls)):
            small_copy(index, bit).wait()
            before = smalls[index][...] if bit == 0 else got[index, bits + bit - 1]
            got[index, bits + bit] = before + got[index, bit]
            if bit + 1 < bits:
                small_copy(index, bit + 1).start()

    def drain():
        for array in range(arrays):
            for side in sides:
                core_copy(array, side).wait_send()
                one_copy(array, side).wait_send()
                two_copy(array, side).wait_send()
                for stage in (3, 4, 5):
                    back_copy(stage, array, side, False).wait_send()

    ticks = (
        [functools.partial(add_core, array) for array in range(arrays)]
        + [functools.partial(add_one, array) for array in range(arrays)]
        + [functools.partial(add_two, array) for array in range(arrays)]
        + [functools.partial(back, stage, array) for stage in (3, 4, 5) for array in range(arrays)]
    )
    return enter, begin, ticks, drain, small_begin, small_step


def reduce_scratch(arrays, rows, model, bits):
    more = max(2 * (bits - 3), 1)
    return [
        pltpu.VMEM((arrays, 2, rows // 4, model), bf16),
        pltpu.VMEM((arrays, 2, rows // 8, model), bf16),
        pltpu.VMEM((arrays, 2, rows // 16, model), bf16),
        pltpu.VMEM((more, arrays, 2, rows // 16, model), bf16),
        pltpu.VMEM((arrays, 2, rows // 4, model), bf16),
        pltpu.VMEM((arrays, 2, rows // 8, model), bf16),
        pltpu.SemaphoreType.DMA((bits + 3, arrays, 2)),
        pltpu.SemaphoreType.DMA((bits + 3, arrays, 2)),
    ]


def backward_kernel(
    shards,
    bits,
    pages_here,
    x_ref,
    box_x_ref,
    box_y_ref,
    rows_ref,
    grad_hidden_ref,
    qkv_ref,
    probs_ref,
    inverse_ref,
    context_ref,
    gathered_ref,
    part_up_ref,
    part_down_ref,
    grad_input_ref,
    grad_pack_ref,
    sums_ref,
    grad_up_ref,
    grad_down_ref,
    weights,
    copy_sem,
    grad_qkv,
    grad_context,
    grad_probs,
    small_scores,
    pack_total,
    bias_total,
    levels_total,
    summed,
    *scratch,
):
    page = pl.program_id(0)
    pages = pl.num_programs(0)
    steps_here = pages_here
    place = lax.axis_index("tensor")
    width, model = x_ref.shape
    heads = model // HEAD_DIM
    own = model // shards
    own_heads = heads // shards
    bins = 64
    enter, begin, ticks, drain, _, _ = reduce_steps(
        bits, (part_up_ref, part_down_ref), (summed.at[0], summed.at[1]), (), scratch
    )
    weight_copies = [
        pltpu.make_async_copy(gathered_ref.at[:, pl.ds(kind * own, own)], weights.at[kind], copy_sem.at[kind])
        for kind in range(4)
    ]
    stores = [
        pltpu.make_async_copy(summed.at[index], target, copy_sem.at[4 + index])
        for index, target in enumerate((grad_up_ref, grad_down_ref))
    ]

    @pl.when(page == 0)
    def _():
        for copy in weight_copies:
            copy.start()
        enter()
        begin()
        pack_total[...] = jnp.zeros_like(pack_total)
        bias_total[...] = jnp.zeros_like(bias_total)
        levels_total[...] = jnp.zeros_like(levels_total)
        sums_ref[...] = jnp.zeros_like(sums_ref)
        for copy in weight_copies:
            copy.wait()

    points = 5

    def point(index):
        for at, act in enumerate(ticks):
            where = (at + 1) * points * steps_here // (len(ticks) + 1) - 1
            if where % points == index:
                pl.when(page == where // points)(act)

    grad_hidden = grad_hidden_ref[...]
    grad_low = grad_hidden.astype(bf16)
    grad_context[...] = nt(weights[3].reshape(model, model), grad_low)
    hot = one_hot_columns(box_x_ref, box_y_ref, bins)
    back_hot = one_hot_columns(box_x_ref, box_y_ref, bins, True)

    def order(at):
        return lax.rem(place * own_heads + at, heads)

    def rows_of(at):
        return pl.ds(pl.multiple_of(order(at) * HEAD_DIM, HEAD_DIM), HEAD_DIM)

    def lead(at):
        rows = rows_of(at)
        grad_mixed = (grad_context[rows] * inverse_ref[0, order(at)]).astype(bf16)
        grad_probs[at % 2] = tn(qkv_ref[0, 2, rows], grad_mixed)
        delta = jnp.sum(
            grad_mixed.astype(f32) * context_ref[0, rows].astype(f32), axis=0, keepdims=True
        )
        return grad_mixed, delta

    def soften(at, delta):
        probs = probs_ref[0, order(at)].astype(f32)
        small_scores[at % 2] = (probs * (grad_probs[at % 2] - delta)).astype(bf16)

    def mix(at, grad_mixed):
        rows = rows_of(at)
        query = qkv_ref[0, 0, rows]
        key = qkv_ref[0, 1, rows]
        grad_scores = small_scores[at % 2]
        grad_value = nt(grad_mixed, probs_ref[0, order(at)])
        grad_key = nt(query, grad_scores) * LN2
        both = nn(jnp.concatenate([key, hot], axis=0) if at < own_heads else key, grad_scores)
        grad_qkv[0, rows] = (both[0:HEAD_DIM] * HEAD_DIM**-0.5).astype(bf16)
        grad_qkv[1, rows] = grad_key.astype(bf16)
        grad_qkv[2, rows] = grad_value.astype(bf16)
        if at < own_heads:
            levels_total[at] += nt(both[HEAD_DIM:].astype(bf16), back_hot)

    point(0)
    kept = [lead(0)]
    for at in range(heads):
        if at + 1 < heads:
            kept.append(lead(at + 1))
        soften(at, kept[at][1])
        if at > 0:
            mix(at - 1, kept[at - 1][0])
        if at % 3 == 2 and at + 1 < heads:
            point(1 + at // 3)
    mix(heads - 1, kept[-1][0])
    point(4)
    tokens = x_ref[...].astype(f32)
    xhat, inverse = norm_parts(tokens)
    low = (xhat * rows_ref[0:1, :] + rows_ref[1:2, :]).astype(bf16)
    mine = pl.ds(pl.multiple_of(place * own, own), own)
    stacked = jnp.concatenate([grad_qkv[kind, mine] for kind in range(3)], axis=0)
    pack_total[0 : 3 * own, :] += nn(stacked, low)
    pack_total[3 * own :, :] += nn(context_ref[0, mine], grad_low)
    wide = stacked.astype(f32)
    folded = wide[:, 0:BLOCK]
    for at in range(1, width // BLOCK):
        folded = folded + wide[:, at * BLOCK : (at + 1) * BLOCK]
    bias_total[...] += folded
    grad_normed = tn(grad_qkv[0], weights[0].reshape(model, model))
    for kind in (1, 2):
        grad_normed = grad_normed + tn(grad_qkv[kind], weights[kind].reshape(model, model))
    grad_total = grad_hidden + norm_grad(grad_normed, xhat, inverse, rows_ref[0:1, :])
    grad_input_ref[...] = grad_total.astype(bf16)
    sums_ref[0:1, :] += jnp.sum(grad_normed * xhat, axis=0, keepdims=True)
    sums_ref[1:2, :] += jnp.sum(grad_normed, axis=0, keepdims=True)

    @pl.when(page == pages - 1)
    def _():
        grad_pack_ref[...] = pack_total[...].astype(bf16)
        row = jnp.sum(bias_total[...].T, axis=0, keepdims=True)
        sums_ref[2:3, 0:own] = row[:, 0:own]
        sums_ref[3:4, 0:own] = row[:, 2 * own : 3 * own]
        lane = lax.broadcasted_iota(jnp.int32, (bins, 2 * bins), 1)
        for one in range(own_heads):
            for kind in range(2):
                block = levels_total[one, kind * bins : (kind + 1) * bins, :]
                inside = lane >= bins if kind else lane < bins
                rolled = pltpu.roll(jnp.where(inside, block, 0.0), kind * bins, 1, stride=1, stride_axis=0)
                at = (kind * own_heads + one) * 2 * bins
                sums_ref[4:5, at : at + 2 * bins] = jnp.sum(rolled, axis=0, keepdims=True)
        for copy in stores:
            copy.start()
        drain()
        for copy in stores:
            copy.wait()


def reduce_kernel(bits, part_ref, small_one_ref, small_two_ref, sum_ref, sum_one_ref, sum_two_ref, *scratch):
    enter, begin, ticks, drain, small_begin, small_step = reduce_steps(
        bits, (part_ref,), (sum_ref,), (small_one_ref, small_two_ref), scratch
    )
    enter()
    begin()
    small_begin()
    for at, act in enumerate(ticks):
        act()
        if at < 3:
            small_step(at)
    for bit in range(3, bits):
        small_step(bit)
    drain()
    sum_one_ref[...] = scratch[8][0, 2 * bits - 1]
    sum_two_ref[...] = scratch[8][1, 2 * bits - 1]


def finish_kernel(pack_ref, up_ref, down_ref, one_ref, two_ref, qkv, qv_bias, out, up, down, tables, rows):
    own = out.shape[0]
    bins = tables.shape[-1]
    for kind in range(3):
        qkv[kind] = pack_ref[kind * own : (kind + 1) * own, :].astype(f32)
    out[...] = pack_ref[3 * own :, :].astype(f32)
    up[...] = up_ref[...].astype(f32)
    down[...] = down_ref[...].astype(f32)
    qv_bias[...] = one_ref[2:4, 0:own]
    rows[0:2, :] = one_ref[0:2, :]
    rows[2:7, :] = two_ref[0:5, :]
    rows[7:8, :] = one_ref[7:8, :]
    m = lax.broadcasted_iota(jnp.int32, (2 * bins, bins), 0)
    level = lax.broadcasted_iota(jnp.int32, (2 * bins, bins), 1)
    pick = jnp.where(jnp.clip(m - (bins - 1), -(bins // 2), bins // 2 - 1) + bins // 2 == level, 1.0, 0.0)
    own_heads = tables.shape[0]
    for one in range(own_heads):
        for kind in range(2):
            at = (kind * own_heads + one) * 2 * bins
            line = jnp.broadcast_to(one_ref[4:5, at : at + 2 * bins], (8, 2 * bins))
            folded = lax.dot_general(
                line, pick, (((1,), (0,)), ((), ())), precision=lax.Precision.HIGHEST, preferred_element_type=f32
            )
            tables[one, kind : kind + 1, :] = folded[0:1]


ANYWHERE = pl.BlockSpec(memory_space=pl.ANY)
IN_VMEM = pl.BlockSpec(memory_space=pltpu.VMEM)


def whole(shape):
    return pl.BlockSpec(shape, lambda *_: (0,) * len(shape), pipeline_mode=pl.Buffered(1))


def page_rows(model):
    return pl.BlockSpec((PAGE, model), lambda p, *_: (p, 0))


def page_block(*shape):
    return pl.BlockSpec((1,) + shape, lambda p, *_: (p,) + (0,) * len(shape))


def params(collective_id=None):
    if collective_id is None:
        return pltpu.CompilerParams(vmem_limit_bytes=VMEM_LIMIT)
    return pltpu.CompilerParams(
        vmem_limit_bytes=VMEM_LIMIT, collective_id=collective_id, has_side_effects=True
    )


def attention_forward(shards, counts, inputs, keep, box_x, box_y, vectors, bias, tables, qkv_weight, out_weight, up, down):
    rows_here, model = inputs.shape
    pages = rows_here // PAGE
    own = model // shards
    bins = tables.shape[-1]
    heads = model // HEAD_DIM
    gathered = jax.ShapeDtypeStruct((shards,) + up.shape, bf16)
    return pl.pallas_call(
        functools.partial(forward_kernel, shards),
        out_shape=(
            jax.ShapeDtypeStruct((pages, 3, model, PAGE), bf16),
            jax.ShapeDtypeStruct((pages, heads, PAGE, PAGE), bf16),
            jax.ShapeDtypeStruct((pages, heads, 1, PAGE), f32),
            jax.ShapeDtypeStruct((pages, model, PAGE), bf16),
            jax.ShapeDtypeStruct((rows_here, model), f32),
            gathered,
            gathered,
            gathered,
            jax.ShapeDtypeStruct((8, model), f32),
            jax.ShapeDtypeStruct((shards, 8, model), f32),
        ),
        grid_spec=pltpu.PrefetchScalarGridSpec(
            num_scalar_prefetch=1,
            grid=(pages,),
            in_specs=[page_rows(model)]
            + [page_block(1, PAGE)] * 3
            + [whole(vector.shape) for vector in vectors]
            + [whole(bias.shape), whole(tables.shape)]
            + [ANYWHERE] * 4,
            out_specs=(
                page_block(3, model, PAGE),
                page_block(heads, PAGE, PAGE),
                page_block(heads, 1, PAGE),
                page_block(model, PAGE),
                page_rows(model),
                ANYWHERE,
                ANYWHERE,
                ANYWHERE,
                whole((8, model)),
                ANYWHERE,
            ),
            scratch_shapes=[
                pltpu.VMEM((8, model), f32),
                pltpu.VMEM((4, shards, own, model), bf16),
                pltpu.SemaphoreType.DMA((14,)),
                pltpu.VMEM((3,) + up.shape, bf16),
                pltpu.VMEM((shards,) + bias.shape, f32),
                pltpu.VMEM((shards,) + tables.shape, f32),
            ]
            + gather_semaphores(3, shards)
            + [
                pltpu.VMEM((2, model, 128), f32),
                pltpu.VMEM((heads * 2 * bins, 2 * bins), bf16),
                pltpu.VMEM((heads * 2 * bins, PAGE), bf16),
                pltpu.VMEM((2, PAGE, PAGE), f32),
            ],
        ),
        compiler_params=params(1),
        name="attention_forward",
    )(counts, inputs, keep, box_x, box_y, *vectors, bias, tables, qkv_weight, out_weight, up, down)


def feed_forward(counts, place, hidden, cotangent, rows, rows_all, up_all, down_all):
    rows_here, model = hidden.shape
    pages = rows_here // PAGE
    shards, _, hidden_units = up_all.shape
    return pl.pallas_call(
        mlp_kernel,
        out_shape=(
            jax.ShapeDtypeStruct((rows_here, model), bf16),
            jax.ShapeDtypeStruct((rows_here, model), f32),
            jax.ShapeDtypeStruct((model, hidden_units), bf16),
            jax.ShapeDtypeStruct((hidden_units, model), bf16),
            jax.ShapeDtypeStruct((8, model), f32),
        ),
        grid_spec=pltpu.PrefetchScalarGridSpec(
            num_scalar_prefetch=2,
            grid=(pages,),
            in_specs=[
                page_rows(model),
                page_rows(model),
                whole(rows.shape),
                whole(rows_all.shape),
                whole((shards, model, hidden_units)),
                whole((shards, hidden_units, model)),
            ],
            out_specs=(
                page_rows(model),
                page_rows(model),
                whole((model, hidden_units)),
                whole((hidden_units, model)),
                whole((8, model)),
            ),
            scratch_shapes=[
                pltpu.VMEM((model, hidden_units), f32),
                pltpu.VMEM((hidden_units, model), f32),
                pltpu.VMEM((PAGE, model), bf16),
                pltpu.VMEM((PAGE, model), bf16),
                pltpu.VMEM((PAGE, model), f32),
                pltpu.VMEM((PAGE, model), f32),
                pltpu.VMEM((shards, PAGE, hidden_units), bf16),
                pltpu.VMEM((shards, PAGE, hidden_units), bf16),
                pltpu.VMEM((2, PAGE, hidden_units), f32),
                pltpu.VMEM((2, PAGE, hidden_units), f32),
            ],
        ),
        compiler_params=params(),
        name="feed_forward",
    )(counts, place, hidden, cotangent, rows, rows_all, up_all, down_all)


def attention_backward(
    shards,
    devices,
    inputs,
    box_x,
    box_y,
    rows,
    grad_hidden,
    qkv,
    probs,
    inverse,
    context,
    gathered,
    part_up,
    part_down,
):
    rows_here, model = inputs.shape
    pages, heads = probs.shape[:2]
    own = model // shards
    bins = 64
    bits = devices.bit_length() - 1
    return pl.pallas_call(
        functools.partial(backward_kernel, shards, bits, pages),
        out_shape=(
            jax.ShapeDtypeStruct((rows_here, model), bf16),
            jax.ShapeDtypeStruct((4 * own, model), bf16),
            jax.ShapeDtypeStruct((8, model), f32),
            jax.ShapeDtypeStruct(part_up.shape, bf16),
            jax.ShapeDtypeStruct(part_down.shape, bf16),
        ),
        grid_spec=pltpu.PrefetchScalarGridSpec(
            num_scalar_prefetch=0,
            grid=(pages,),
            in_specs=[page_rows(model)]
            + [page_block(1, PAGE)] * 2
            + [whole(rows.shape)]
            + [
                page_rows(model),
                page_block(3, model, PAGE),
                page_block(heads, PAGE, PAGE),
                page_block(heads, 1, PAGE),
                page_block(model, PAGE),
                ANYWHERE,
                whole(part_up.shape),
                whole(part_down.shape),
            ],
            out_specs=(
                page_rows(model),
                whole((4 * own, model)),
                whole((8, model)),
                ANYWHERE,
                ANYWHERE,
            ),
            scratch_shapes=[
                pltpu.VMEM((4, shards, own, model), bf16),
                pltpu.SemaphoreType.DMA((6,)),
                pltpu.VMEM((3, model, PAGE), bf16),
                pltpu.VMEM((model, PAGE), f32),
                pltpu.VMEM((2, PAGE, PAGE), f32),
                pltpu.VMEM((2, PAGE, PAGE), bf16),
                pltpu.VMEM((4 * own, model), f32),
                pltpu.VMEM((3 * own, BLOCK), f32),
                pltpu.VMEM((own // HEAD_DIM, 2 * bins, 2 * bins), f32),
                pltpu.VMEM((2,) + part_up.shape, bf16),
            ]
            + reduce_scratch(2, part_up.shape[0], model, bits),
        ),
        compiler_params=params(2),
        name="attention_backward",
    )(
        inputs,
        box_x,
        box_y,
        rows,
        grad_hidden,
        qkv,
        probs,
        inverse,
        context,
        gathered,
        part_up,
        part_down,
    )


def reduce_grads(devices, part, small_one, small_two):
    rows, model = part.shape
    bits = devices.bit_length() - 1
    return pl.pallas_call(
        functools.partial(reduce_kernel, bits),
        out_shape=(jax.ShapeDtypeStruct(part.shape, bf16),)
        + tuple(jax.ShapeDtypeStruct(small.shape, f32) for small in (small_one, small_two)),
        in_specs=[IN_VMEM] * 3,
        out_specs=(IN_VMEM,) * 3,
        scratch_shapes=reduce_scratch(1, rows, model, bits)
        + [
            pltpu.VMEM((2, 2 * bits) + small_one.shape, f32),
            pltpu.SemaphoreType.DMA((2, bits)),
            pltpu.SemaphoreType.DMA((2, bits)),
        ],
        compiler_params=params(3),
        name="reduce_grads",
    )(part, small_one, small_two)


def finish_grads(pack, up, down, small_one, small_two, bins):
    own, model = pack.shape[0] // 4, pack.shape[1]
    return pl.pallas_call(
        finish_kernel,
        out_shape=(
            jax.ShapeDtypeStruct((3, own, model), f32),
            jax.ShapeDtypeStruct((2, own), f32),
            jax.ShapeDtypeStruct((own, model), f32),
            jax.ShapeDtypeStruct(up.shape, f32),
            jax.ShapeDtypeStruct(down.shape, f32),
            jax.ShapeDtypeStruct((own // HEAD_DIM, 2, bins), f32),
            jax.ShapeDtypeStruct(small_one.shape, f32),
        ),
        in_specs=[IN_VMEM] * 5,
        out_specs=(IN_VMEM,) * 7,
        compiler_params=params(),
        name="finish_grads",
    )(pack, up, down, small_one, small_two)


def on_device(
    inputs,
    cotangent,
    counts,
    keep_mask,
    box_x,
    box_y,
    gain_one,
    shift_one,
    w_qkv,
    b_qv,
    w_out,
    b_out,
    gain_two,
    shift_two,
    w_up,
    b_up,
    w_down,
    b_down,
    rel_tables,
    *,
    devices,
):
    rows_here, model = inputs.shape
    pages = rows_here // PAGE
    own_heads, bins = rel_tables.shape[1:]
    own = own_heads * HEAD_DIM
    shards = model // own
    place = lax.axis_index("tensor").astype(jnp.int32).reshape(1)
    paged = lambda array: array.reshape(pages, 1, PAGE)
    keep_mask, box_x, box_y = paged(keep_mask), paged(box_x), paged(box_y)
    vectors = [
        vector.reshape(-1, 128) for vector in (gain_one, shift_one, b_out, gain_two, shift_two, b_down, b_up)
    ]

    qkv, probs, inverse, context, hidden, gathered, up_all, down_all, rows, rows_all = attention_forward(
        shards,
        counts,
        inputs,
        keep_mask,
        box_x,
        box_y,
        vectors,
        b_qv,
        rel_tables.transpose(1, 0, 2),
        w_qkv.transpose(0, 2, 1).reshape(3 * own, model),
        w_out,
        w_up,
        w_down,
    )
    out, grad_hidden, part_up, part_down, small_two = feed_forward(
        counts, place, hidden, cotangent, rows, rows_all, up_all, down_all
    )
    grad_input, part_pack, small_one, grad_up, grad_down = attention_backward(
        shards,
        devices,
        inputs,
        box_x,
        box_y,
        rows,
        grad_hidden,
        qkv,
        probs,
        inverse,
        context,
        gathered,
        part_up,
        part_down,
    )
    grad_pack, small_one, small_two = reduce_grads(devices, part_pack, small_one, small_two)
    grad_qkv, grad_b_qv, grad_w_out, grad_w_up, grad_w_down, grad_tables, sums = finish_grads(
        grad_pack, grad_up, grad_down, small_one, small_two, bins
    )
    return (
        out,
        grad_input,
        grad_qkv.transpose(0, 2, 1),
        grad_b_qv,
        grad_w_out,
        sums[4],
        sums[0],
        sums[1],
        sums[2],
        sums[3],
        grad_w_up,
        sums[6],
        grad_w_down,
        sums[5],
        grad_tables.transpose(1, 0, 2),
    )


def solution(mesh):
    placed = (
        P("dp", None),
        P("dp", None),
        P("dp"),
        P("dp"),
        P("dp"),
        P("dp"),
        P(),
        P(),
        P(None, None, "tensor"),
        P(None, "tensor"),
        P("tensor", None),
        P(),
        P(),
        P(),
        P(None, "tensor"),
        P("tensor"),
        P("tensor", None),
        P(),
        P(None, "tensor", None),
    )
    return jax.shard_map(
        functools.partial(on_device, devices=mesh.shape["dp"]),
        mesh=mesh,
        in_specs=placed,
        out_specs=(
            P("dp", None),
            P("dp", None),
            P(None, None, "tensor"),
            P(None, "tensor"),
            P("tensor", None),
            P(),
            P(),
            P(),
            P(),
            P(),
            P(None, "tensor"),
            P("tensor"),
            P("tensor", None),
            P(),
            P(None, "tensor", None),
        ),
        check_vma=False,
    )
```

```python
import functools
import jax
import jax.numpy as jnp
from jax import lax
from jax.experimental import pallas as pl
from jax.experimental.pallas import tpu as pltpu
from jax.sharding import PartitionSpec as P

HEAD_DIM = 64
PAGE = 512
BLOCK = 128
epsilon = 1e-05
masked_score = -1e30
LOG2E = 1.4426950408889634
LN2 = 0.6931471805599453
bf16 = jnp.bfloat16
f32 = jnp.float32
VMEM_LIMIT = 60 << 20


def dot(left, right, left_dim, right_dim):
    return lax.dot_general(
        left, right, (((left_dim,), (right_dim,)), ((), ())), preferred_element_type=f32
    )


def nn(left, right):
    return dot(left, right, 1, 0)


def nt(left, right):
    return dot(left, right, 1, 1)


def tn(left, right):
    return dot(left, right, 0, 0)


def norm_parts(rows):
    average = jnp.mean(rows, axis=-1, keepdims=True)
    centered = rows - average
    variance = jnp.mean(centered * centered, axis=-1, keepdims=True)
    inverse = lax.rsqrt(variance + epsilon)
    return centered * inverse, inverse


def norm_grad(grad_out, xhat, inverse, gain):
    scaled = grad_out * gain
    mean_one = jnp.mean(scaled, axis=-1, keepdims=True)
    mean_two = jnp.mean(scaled * xhat, axis=-1, keepdims=True)
    return inverse * (scaled - mean_one - xhat * mean_two)


def one_hot_columns(box_x_ref, box_y_ref, bins, reverse=False):
    width = box_x_ref.shape[-1]
    levels = lax.broadcasted_iota(jnp.int32, (bins, width), 0)
    if reverse:
        levels = (bins - 1) - levels
    hot_x = jnp.where(levels == box_x_ref[0], 1.0, 0.0)
    hot_y = jnp.where(levels == box_y_ref[0], 1.0, 0.0)
    return jnp.concatenate([hot_x, hot_y], axis=0).astype(bf16)


def by_halves(count, body):
    body(PAGE)


def neighbours(axis):
    core = axis % 2
    side_x = (axis // 2) % 2
    side_y = (axis // 4) % 2
    return core, side_x, side_y, 1 - 2 * core, 2 - 4 * side_x, 4 - 8 * side_y


def flipped(index, mask):
    result, bit = index, 1
    while bit <= mask:
        if mask & bit:
            result = result + bit - 2 * bit * ((index // bit) % 2)
        bit *= 2
    return result


def greet(peers):
    barrier = pltpu.get_barrier_semaphore()
    for dp, tensor in peers:
        pl.semaphore_signal(
            barrier, inc=1, device_id={"dp": dp, "tensor": tensor}, device_id_type=pl.DeviceIdType.MESH
        )
    pl.semaphore_wait(barrier, len(peers))


KIND_Z, KIND_X, KIND_Y, KIND_VIA_X, KIND_VIA_Y, KIND_CORE = 0, 1, 2, 3, 4, 5
KINDS = 9


def gather_steps(shards, sources, targets, small_sources, small_targets, send_sem, recv_sem):
    arrays = len(sources)
    place = lax.axis_index("tensor")
    lane = lax.axis_index("dp")
    core, side_x, side_y, to_core, to_x, to_y = neighbours(lane)
    mine = lane % 8
    rows = targets[0].shape[1] // 8
    half = rows // 2
    hops = range(1, shards)

    def piece(index, start=0, size=rows):
        return pl.ds(pl.multiple_of(index * rows + start, 16), size)

    def remote(kind, array, hop, source, target, dp, tensor):
        return pltpu.make_async_remote_copy(
            src_ref=source,
            dst_ref=target,
            send_sem=send_sem.at[kind, array, hop - 1],
            recv_sem=recv_sem.at[kind, array, hop - 1],
            device_id={"dp": dp, "tensor": tensor},
            device_id_type=pl.DeviceIdType.MESH,
        )

    def within(kind, array, hop, region, step):
        ref = targets[array].at[flipped(place, hop), region]
        return remote(kind, array, hop, ref, ref, lane + step, place)

    def along(array, hop):
        source, target = sources[array].at[piece(mine)], targets[array].at[place, piece(mine)]
        return remote(KIND_Z, array, hop, source, target, lane, flipped(place, hop))

    def along_small(index, hop):
        source, target = small_sources[index], small_targets[index].at[place]
        return remote(1 + index, arrays, hop, source, target, lane, flipped(place, hop))

    def enter():
        greet(
            [(lane + step, place) for step in (to_core, to_x, to_y)] + [(lane, flipped(place, hop)) for hop in hops]
        )

    def begin():
        for array in range(arrays):
            for hop in hops:
                along(array, hop).start()
            if array == 0:
                for index in range(len(small_sources)):
                    for hop in hops:
                        along_small(index, hop).start()

    def arrive(array, hop):
        along(array, hop).wait_recv()
        within(KIND_X, array, hop, piece(mine), to_x).start()
        within(KIND_Y, array, hop, piece(mine), to_y).start()
        within(KIND_CORE, array, hop, piece(mine), to_core).start()

    def spread_near(array, hop):
        at = mine + to_x
        within(KIND_X, array, hop, piece(at), to_x).wait_recv()
        within(KIND_VIA_Y, array, hop, piece(at, 0, half), to_y).start()
        within(KIND_CORE + 1, array, hop, piece(at), to_core).start()
        at = mine + to_y
        within(KIND_Y, array, hop, piece(at), to_y).wait_recv()
        within(KIND_VIA_X, array, hop, piece(at, half, half), to_x).start()
        within(KIND_CORE + 2, array, hop, piece(at), to_core).start()

    def spread_far(array, hop):
        at = mine + to_x + to_y
        within(KIND_VIA_Y, array, hop, piece(at, 0, half), to_y).wait_recv()
        within(KIND_VIA_X, array, hop, piece(at, half, half), to_x).wait_recv()
        within(KIND_CORE + 3, array, hop, piece(at), to_core).start()

    def finish(array, hop):
        for index, shift in enumerate((0, to_x, to_y, to_x + to_y)):
            within(KIND_CORE + index, array, hop, piece(mine + to_core + shift), to_core).wait_recv()

    def drain(early):
        for hop in hops:
            if early:
                for index in range(len(small_sources)):
                    along_small(index, hop).wait()
                continue
            for array in range(arrays):
                along(array, hop).wait_send()
                within(KIND_X, array, hop, piece(mine), to_x).wait_send()
                within(KIND_Y, array, hop, piece(mine), to_y).wait_send()
                within(KIND_VIA_Y, array, hop, piece(mine + to_x, 0, half), to_y).wait_send()
                within(KIND_VIA_X, array, hop, piece(mine + to_y, half, half), to_x).wait_send()
                for index, shift in enumerate((0, to_x, to_y, to_x + to_y)):
                    within(KIND_CORE + index, array, hop, piece(mine + shift), to_core).wait_send()

    items = [(array, hop) for array in range(arrays) for hop in hops]
    stages = (arrive, spread_near, spread_far, finish)

    def act(stage, item):
        stages[stage](*items[item])

    return enter, begin, act, len(items), drain


def gather_order(items, first):
    start = []
    for tick in range(first + 2):
        for stage in (0, 1, 2):
            if 0 <= tick - stage < first:
                start.append((stage, tick - stage))
            elif stage == 0 and tick < min(items, first + 2):
                later = (stage, tick)
                start.append(later)
    start += [(3, item) for item in range(first)]
    ready = min(items, first + 3)
    start += [(0, item) for item in range(first + 2, ready)]
    groups = []
    for tick in range(first, items + 4):
        group = [(stage, tick - lag) for stage, lag in ((3, 4), (2, 2), (1, 0)) if first <= tick - lag < items]
        if ready <= tick + 3 < items:
            group.append((0, tick + 3))
        groups.append(group)
    last = groups.pop()
    groups[-1] = groups[-1] + last
    return start, groups


def gather_semaphores(arrays, shards):
    return [pltpu.SemaphoreType.DMA((KINDS, arrays + 1, shards - 1))] * 2


def forward_kernel(
    shards,
    counts_ref,
    x_ref,
    keep_ref,
    box_x_ref,
    box_y_ref,
    gain_one_ref,
    shift_one_ref,
    out_bias_ref,
    gain_two_ref,
    shift_two_ref,
    down_bias_ref,
    up_bias_ref,
    bias_ref,
    tables_ref,
    qkv_weight_ref,
    out_weight_ref,
    up_ref,
    down_ref,
    qkv_ref,
    probs_ref,
    inverse_ref,
    context_ref,
    hidden_ref,
    gathered_ref,
    up_all_ref,
    down_all_ref,
    rows_ref,
    rows_all_ref,
    rows,
    weights,
    copy_sem,
    bounce,
    bias_all,
    tables_all,
    send_sem,
    recv_sem,
    bias_columns,
    toeplitz,
    spread,
    scores,
):
    page = pl.program_id(0)
    pages = counts_ref.shape[0]
    place = lax.axis_index("tensor")
    width, model = x_ref.shape
    heads = model // HEAD_DIM
    own = model // shards
    own_heads = heads // shards
    bins = tables_ref.shape[-1]
    split = qkv_weight_ref.shape[0]
    smalls, small_targets = (rows, bias_ref, tables_ref), (rows_all_ref, bias_all, tables_all)
    enter, begin, act, items, drain = gather_steps(
        shards,
        (bounce.at[0], up_ref, down_ref),
        (gathered_ref, up_all_ref, down_all_ref),
        smalls,
        small_targets,
        send_sem,
        recv_sem,
    )
    loads = [
        pltpu.make_async_copy(qkv_weight_ref, bounce.at[0, 0:split], copy_sem.at[0]),
        pltpu.make_async_copy(out_weight_ref, bounce.at[0, split:], copy_sem.at[1]),
        pltpu.make_async_copy(up_ref, bounce.at[1], copy_sem.at[2]),
        pltpu.make_async_copy(down_ref, bounce.at[2], copy_sem.at[3]),
    ]
    stores = [
        pltpu.make_async_copy(bounce.at[index], target.at[place], copy_sem.at[4 + index])
        for index, target in enumerate((gathered_ref, up_all_ref, down_all_ref))
    ] + [
        pltpu.make_async_copy(source, target.at[place], copy_sem.at[7 + index])
        for index, (source, target) in enumerate(zip(smalls, small_targets))
    ]
    weight_copies = [
        pltpu.make_async_copy(
            gathered_ref.at[:, pl.ds(kind * own, own)], weights.at[kind], copy_sem.at[10 + kind]
        )
        for kind in range(4)
    ]
    start, groups = gather_order(items, shards - 1)

    @pl.when(page == 0)
    def _():
        for copy in loads:
            copy.start()
        vectors = (
            gain_one_ref,
            shift_one_ref,
            out_bias_ref,
            gain_two_ref,
            shift_two_ref,
            down_bias_ref,
            up_bias_ref,
            up_bias_ref,
        )
        for index, vector in enumerate(vectors):
            for part in range(model // 128):
                rows[index : index + 1, part * 128 : (part + 1) * 128] = vector[part : part + 1, :]
        rows_ref[...] = rows[...]
        enter()
        for copy in loads[0:2]:
            copy.wait()
        begin()
        for copy in loads[2:4]:
            copy.wait()
        for copy in stores:
            copy.start()
        for stage, item in start:
            act(stage, item)
        for copy in stores:
            copy.wait()
        for copy in weight_copies:
            copy.start()
        drain(True)
        for shard in range(shards):
            span = slice(shard * own, (shard + 1) * own)
            for kind in range(2):
                wide = jnp.broadcast_to(bias_all[shard, kind : kind + 1, :], (128, own))
                bias_columns[kind, span, :] = wide.T
        m = lax.broadcasted_iota(jnp.int32, (bins, 2 * bins), 1)
        signed = jnp.where(m >= bins, 2 * bins - m, -m)
        level = lax.broadcasted_iota(jnp.int32, (bins, 2 * bins), 0)
        pick = jnp.where(jnp.clip(signed, -(bins // 2), bins // 2 - 1) + bins // 2 == level, 1.0, 0.0).astype(bf16)
        lane = lax.broadcasted_iota(jnp.int32, (bins, 2 * bins), 1)
        for shard in range(shards):
            for one in range(own_heads):
                at = (shard * own_heads + one) * 2 * bins
                for kind in range(2):
                    table = (tables_all[shard, one, kind : kind + 1, :] * LOG2E).astype(bf16)
                    line = nn(jnp.broadcast_to(table, (bins, bins)), pick)
                    rolled = pltpu.roll(line, kind * bins, 1, stride=1, stride_axis=0)
                    inside = lane >= bins if kind else lane < bins
                    toeplitz[at + kind * bins : at + (kind + 1) * bins, :] = jnp.where(inside, rolled, 0.0).astype(bf16)
        for copy in weight_copies:
            copy.wait()

    points = 5

    def run_group(group):
        for stage, item in group:
            act(stage, item)

    def point(index):
        for at, group in enumerate(groups):
            where = (at + 1) * points * pages // len(groups) - 1
            if where % points == index:
                pl.when(page == where // points)(functools.partial(run_group, group))

    tokens = x_ref[...].astype(f32)
    xhat, _ = norm_parts(tokens)
    low = (xhat * rows[0:1, :] + rows[1:2, :]).astype(bf16)
    for kind in range(3):
        product = nt(weights[kind].reshape(model, model), low)
        if kind == 0:
            product = (product + bias_columns[0, :, 0:1]) * (LOG2E * HEAD_DIM**-0.5)
        if kind == 2:
            product = product + bias_columns[1, :, 0:1]
        qkv_ref[0, kind] = product.astype(bf16)
    hot = one_hot_columns(box_x_ref, box_y_ref, bins)
    spread[...] = nn(toeplitz[...], hot).astype(bf16)
    lane = lax.broadcasted_iota(jnp.int32, (1, width), 1)
    open_key = (lane < counts_ref[page]) & (keep_ref[0] == 1)
    mask_row = jnp.where(open_key, 0.0, masked_score)
    first = lax.broadcasted_iota(jnp.int32, (HEAD_DIM, width), 0) == 0
    key_pad = jnp.where(first, mask_row, 0.0).astype(bf16)
    query_pad = jnp.where(first, 1.0, 0.0).astype(bf16)
    ones = jnp.ones((16, width), bf16)
    eye = lax.broadcasted_iota(jnp.int32, (BLOCK, BLOCK), 0) == lax.broadcasted_iota(jnp.int32, (BLOCK, BLOCK), 1)

    def score(index, slot):
        span = slice(index * HEAD_DIM, (index + 1) * HEAD_DIM)
        query = qkv_ref[0, 0, span]
        key = qkv_ref[0, 1, span]
        bias = spread[index * 2 * bins : (index + 1) * 2 * bins, :]
        left = jnp.concatenate([key, key_pad, hot], axis=0)
        right = jnp.concatenate([query, query_pad, bias], axis=0)
        scores[slot] = tn(left, right)
        return jnp.sum(query.astype(f32) * key.astype(f32), axis=0, keepdims=True) + jnp.sum(
            bias.astype(f32) * hot.astype(f32), axis=0, keepdims=True
        )

    def soften(index, slot, own_score):
        for at in range(width // BLOCK):
            span = slice(at * BLOCK, (at + 1) * BLOCK)
            scores[slot, span, span] = jnp.where(eye, own_score[:, span], scores[slot, span, span])
        top = jnp.max(scores[slot], axis=0, keepdims=True)
        probs_ref[0, index] = jnp.exp2(scores[slot] - top).astype(bf16)

    def mix(index):
        span = slice(index * HEAD_DIM, (index + 1) * HEAD_DIM)
        mixed = nn(jnp.concatenate([qkv_ref[0, 2, span], ones], axis=0), probs_ref[0, index])
        inverse = 1.0 / mixed[HEAD_DIM : HEAD_DIM + 1]
        inverse_ref[0, index] = inverse
        context_ref[0, span] = (mixed[0:HEAD_DIM] * inverse).astype(bf16)

    point(0)
    owns = [score(0, 0)]
    for at in range(heads):
        if at + 1 < heads:
            owns.append(score(at + 1, (at + 1) % 2))
        soften(at, at % 2, owns[at])
        if at > 0:
            mix(at - 1)
        if at % 3 == 2 and at + 1 < heads:
            point(1 + at // 3)
    mix(heads - 1)
    point(4)
    attended = tn(context_ref[0], weights[3].reshape(model, model))
    hidden_ref[...] = tokens + attended + rows[2:3, :]

    @pl.when(page == pages - 1)
    def _():
        drain(False)


def mlp_kernel(
    counts_ref,
    place_ref,
    hidden_ref,
    cotangent_ref,
    rows_ref,
    bias_ref,
    up_ref,
    down_ref,
    out_ref,
    grad_hidden_ref,
    grad_up_ref,
    grad_down_ref,
    sums_ref,
    up_total,
    down_total,
    low_ref,
    gl_ref,
    down_acc,
    gn_acc,
    act_ref,
    gu_ref,
    upper_ref,
    grad_ref,
):
    page = pl.program_id(0)
    shards = up_ref.shape[0]
    place = place_ref[0]

    @pl.when(page == 0)
    def _():
        up_total[...] = jnp.zeros_like(up_total)
        down_total[...] = jnp.zeros_like(down_total)
        sums_ref[...] = jnp.zeros_like(sums_ref)

    count = counts_ref[page]

    def body(width):
        valid = lax.broadcasted_iota(jnp.int32, (width, 1), 0) < count
        hidden = hidden_ref[0:width, :]
        xhat, inverse = norm_parts(hidden)
        low = (xhat * rows_ref[3:4, :] + rows_ref[4:5, :]).astype(bf16)
        grad_result = jnp.where(valid, cotangent_ref[0:width, :].astype(f32), 0.0)
        grad_low = grad_result.astype(bf16)

        low_ref[0:width, :] = low
        gl_ref[0:width, :] = grad_low
        down_acc[0:width, :] = jnp.zeros((width, hidden.shape[1]), f32)
        gn_acc[0:width, :] = jnp.zeros((width, hidden.shape[1]), f32)

        def lead(at, slot):
            upper_ref[slot, 0:width, :] = nn(low_ref[0:width, :], up_ref[at]) + bias_ref[at, 6:7, :]
            grad_ref[slot, 0:width, :] = nt(gl_ref[0:width, :], down_ref[at])

        def bend(at, slot):
            upper = upper_ref[slot, 0:width, :]
            half = 0.5 * (1.0 + lax.erf(upper * 0.7071067811865476))
            density = jnp.exp(-0.5 * upper * upper) * 0.3989422804014327
            act_ref[at, 0:width, :] = (upper * half).astype(bf16)
            slope = half + upper * density
            gu_ref[at, 0:width, :] = (grad_ref[slot, 0:width, :] * slope).astype(bf16)

        def mix(at):
            down_acc[0:width, :] += nn(act_ref[at, 0:width, :], down_ref[at])
            gn_acc[0:width, :] += nt(gu_ref[at, 0:width, :], up_ref[at])

        lead(0, 0)
        for at in range(shards):
            if at + 1 < shards:
                lead(at + 1, (at + 1) % 2)
            bend(at, at % 2)
            if at > 0:
                mix(at - 1)
        mix(shards - 1)
        down_proj = down_acc[0:width, :]
        grad_normed = gn_acc[0:width, :]
        up_total[...] += tn(low_ref[0:width, :], gu_ref[place, 0:width, :])
        down_total[...] += tn(act_ref[place, 0:width, :], gl_ref[0:width, :])
        sums_ref[4:5, :] += jnp.sum(gu_ref[place, 0:width, :].astype(f32), axis=0, keepdims=True)
        result = jnp.where(valid, hidden + down_proj + rows_ref[5:6, :], 0.0)
        out_ref[0:width, :] = result.astype(bf16)
        grad_hidden = grad_result + norm_grad(grad_normed, xhat, inverse, rows_ref[3:4, :])
        grad_hidden_ref[0:width, :] = grad_hidden
        sums_ref[0:1, :] += jnp.sum(grad_normed * xhat, axis=0, keepdims=True)
        sums_ref[1:2, :] += jnp.sum(grad_normed, axis=0, keepdims=True)
        sums_ref[2:3, :] += jnp.sum(grad_hidden, axis=0, keepdims=True)
        sums_ref[3:4, :] += jnp.sum(grad_result, axis=0, keepdims=True)
        if width < PAGE:
            out_ref[width:PAGE, :] = jnp.zeros((PAGE - width, hidden.shape[1]), bf16)
            grad_hidden_ref[width:PAGE, :] = jnp.zeros((PAGE - width, hidden.shape[1]), f32)

    by_halves(count, body)

    @pl.when(page == pl.num_programs(0) - 1)
    def _():
        grad_up_ref[...] = up_total[...].astype(bf16)
        grad_down_ref[...] = down_total[...].astype(bf16)


def reduce_steps(bits, parts, sums, smalls, scratch):
    arrays = len(parts)
    got_core, got_one, got_two, got_more, kept_core, kept_one, send_sem, recv_sem = scratch[0:8]
    place = lax.axis_index("tensor")
    lane = lax.axis_index("dp")
    core, side_x, side_y, to_core, to_x, to_y = neighbours(lane)
    steps = [to_core, to_x, to_y]
    for bit in range(3, bits):
        size = 2**bit
        steps.append(size - 2 * size * ((lane // size) % 2))
    rows = parts[0].shape[0]
    quarter, eighth, sixteenth = rows // 4, rows // 8, rows // 16
    order = ((side_x, side_y, to_x, to_y), (side_y, side_x, to_y, to_x))
    sides = range(2)

    def device(step):
        return {"dp": lane + step, "tensor": place}

    def remote(stage, array, side, source, target, step):
        return pltpu.make_async_remote_copy(
            src_ref=source,
            dst_ref=target,
            send_sem=send_sem.at[stage, array, side],
            recv_sem=recv_sem.at[stage, array, side],
            device_id=device(step),
            device_id_type=pl.DeviceIdType.MESH,
        )

    def span(side, of_core, one=None, two=None):
        start = side * (rows // 2) + of_core * quarter
        if one is None:
            return pl.ds(pl.multiple_of(start, 16), quarter)
        start = start + one * eighth
        if two is None:
            return pl.ds(pl.multiple_of(start, 16), eighth)
        return pl.ds(pl.multiple_of(start + two * sixteenth, 16), sixteenth)

    def part_of(index, size):
        return pl.ds(pl.multiple_of(index * size, 16), size)

    def core_copy(array, side):
        return remote(0, array, side, parts[array].at[span(side, 1 - core)], got_core.at[array, side], to_core)

    def one_copy(array, side):
        one, two, to_one, to_two = order[side]
        source = kept_core.at[array, side, part_of(1 - one, eighth)]
        return remote(1, array, side, source, got_one.at[array, side], to_one)

    def two_copy(array, side):
        one, two, to_one, to_two = order[side]
        source = kept_one.at[array, side, part_of(1 - two, sixteenth)]
        return remote(2, array, side, source, got_two.at[array, side], to_two)

    def more_copy(array, side, bit):
        source = got_more.at[bit - 3, array, side]
        return remote(bit + 3, array, side, source, got_more.at[bits - 3 + bit - 3, array, side], steps[bit])

    def back_copy(stage, array, side, inward):
        one, two, to_one, to_two = order[side]
        if stage == 3:
            region, step = span(side, core, one, 1 - two if inward else two), to_two
        elif stage == 4:
            region, step = span(side, core, 1 - one if inward else one), to_one
        else:
            region, step = span(side, 1 - core if inward else core), to_core
        ref = sums[array].at[region]
        return remote(stage, array, side, ref, ref, step)

    def enter():
        greet([(lane + step, place) for step in steps])

    def begin():
        for array in range(arrays):
            for side in sides:
                core_copy(array, side).start()

    def add_core(array):
        for side in sides:
            keep = span(side, core)
            core_copy(array, side).wait_recv()
            kept_core[array, side] = (
                parts[array][keep, :].astype(f32) + got_core[array, side].astype(f32)
            ).astype(bf16)
            one_copy(array, side).start()

    def add_one(array):
        for side in sides:
            one, two, to_one, to_two = order[side]
            one_copy(array, side).wait_recv()
            kept_one[array, side] = (
                kept_core[array, side, part_of(one, eighth), :].astype(f32) + got_one[array, side].astype(f32)
            ).astype(bf16)
            two_copy(array, side).start()

    def add_two(array):
        for side in sides:
            one, two, to_one, to_two = order[side]
            two_copy(array, side).wait_recv()
            total = (
                kept_one[array, side, part_of(two, sixteenth), :].astype(f32) + got_two[array, side].astype(f32)
            ).astype(bf16)
            for bit in range(3, bits):
                got_more[bit - 3, array, side] = total
                more_copy(array, side, bit).start()
                more_copy(array, side, bit).wait()
                total = (total.astype(f32) + got_more[bits - 3 + bit - 3, array, side].astype(f32)).astype(bf16)
            sums[array][span(side, core, one, two), :] = total
            back_copy(3, array, side, False).start()

    def back(stage, array):
        for side in sides:
            back_copy(stage, array, side, True).wait_recv()
            if stage < 5:
                back_copy(stage + 1, array, side, False).start()

    def small_copy(index, bit):
        got, small_send, small_recv = scratch[8:11]
        source = smalls[index] if bit == 0 else got.at[index, bits + bit - 1]
        return pltpu.make_async_remote_copy(
            src_ref=source,
            dst_ref=got.at[index, bit],
            send_sem=small_send.at[index, bit],
            recv_sem=small_recv.at[index, bit],
            device_id=device(steps[bit]),
            device_id_type=pl.DeviceIdType.MESH,
        )

    def small_begin():
        for index in range(len(smalls)):
            small_copy(index, 0).start()

    def small_step(bit):
        got = scratch[8]
        for index in range(len(smalls)):
            small_copy(index, bit).wait()
            before = smalls[index][...] if bit == 0 else got[index, bits + bit - 1]
            got[index, bits + bit] = before + got[index, bit]
            if bit + 1 < bits:
                small_copy(index, bit + 1).start()

    def drain():
        for array in range(arrays):
            for side in sides:
                core_copy(array, side).wait_send()
                one_copy(array, side).wait_send()
                two_copy(array, side).wait_send()
                for stage in (3, 4, 5):
                    back_copy(stage, array, side, False).wait_send()

    ticks = (
        [functools.partial(add_core, array) for array in range(arrays)]
        + [functools.partial(add_one, array) for array in range(arrays)]
        + [functools.partial(add_two, array) for array in range(arrays)]
        + [functools.partial(back, stage, array) for stage in (3, 4, 5) for array in range(arrays)]
    )
    return enter, begin, ticks, drain, small_begin, small_step


def reduce_scratch(arrays, rows, model, bits):
    more = max(2 * (bits - 3), 1)
    return [
        pltpu.VMEM((arrays, 2, rows // 4, model), bf16),
        pltpu.VMEM((arrays, 2, rows // 8, model), bf16),
        pltpu.VMEM((arrays, 2, rows // 16, model), bf16),
        pltpu.VMEM((more, arrays, 2, rows // 16, model), bf16),
        pltpu.VMEM((arrays, 2, rows // 4, model), bf16),
        pltpu.VMEM((arrays, 2, rows // 8, model), bf16),
        pltpu.SemaphoreType.DMA((bits + 3, arrays, 2)),
        pltpu.SemaphoreType.DMA((bits + 3, arrays, 2)),
    ]


def backward_kernel(
    shards,
    bits,
    pages_here,
    x_ref,
    box_x_ref,
    box_y_ref,
    rows_ref,
    grad_hidden_ref,
    qkv_ref,
    probs_ref,
    inverse_ref,
    context_ref,
    gathered_ref,
    part_up_ref,
    part_down_ref,
    grad_input_ref,
    grad_pack_ref,
    sums_ref,
    grad_up_ref,
    grad_down_ref,
    weights,
    copy_sem,
    grad_qkv,
    grad_context,
    grad_probs,
    small_scores,
    pack_total,
    bias_total,
    levels_total,
    summed,
    *scratch,
):
    page = pl.program_id(0)
    pages = pl.num_programs(0)
    steps_here = pages_here
    place = lax.axis_index("tensor")
    width, model = x_ref.shape
    heads = model // HEAD_DIM
    own = model // shards
    own_heads = heads // shards
    bins = 64
    enter, begin, ticks, drain, _, _ = reduce_steps(
        bits, (part_up_ref, part_down_ref), (summed.at[0], summed.at[1]), (), scratch
    )
    weight_copies = [
        pltpu.make_async_copy(gathered_ref.at[:, pl.ds(kind * own, own)], weights.at[kind], copy_sem.at[kind])
        for kind in range(4)
    ]
    stores = [
        pltpu.make_async_copy(summed.at[index], target, copy_sem.at[4 + index])
        for index, target in enumerate((grad_up_ref, grad_down_ref))
    ]

    @pl.when(page == 0)
    def _():
        for copy in weight_copies:
            copy.start()
        enter()
        begin()
        pack_total[...] = jnp.zeros_like(pack_total)
        bias_total[...] = jnp.zeros_like(bias_total)
        levels_total[...] = jnp.zeros_like(levels_total)
        sums_ref[...] = jnp.zeros_like(sums_ref)
        for copy in weight_copies:
            copy.wait()

    points = 5

    def point(index):
        for at, act in enumerate(ticks):
            where = (at + 1) * points * steps_here // (len(ticks) + 1) - 1
            if where % points == index:
                pl.when(page == where // points)(act)

    grad_hidden = grad_hidden_ref[...]
    grad_low = grad_hidden.astype(bf16)
    grad_context[...] = nt(weights[3].reshape(model, model), grad_low)
    hot = one_hot_columns(box_x_ref, box_y_ref, bins)
    back_hot = one_hot_columns(box_x_ref, box_y_ref, bins, True)

    def order(at):
        return lax.rem(place * own_heads + at, heads)

    def rows_of(at):
        return pl.ds(pl.multiple_of(order(at) * HEAD_DIM, HEAD_DIM), HEAD_DIM)

    def lead(at):
        rows = rows_of(at)
        grad_mixed = (grad_context[rows] * inverse_ref[0, order(at)]).astype(bf16)
        grad_probs[at % 2] = tn(qkv_ref[0, 2, rows], grad_mixed)
        delta = jnp.sum(
            grad_mixed.astype(f32) * context_ref[0, rows].astype(f32), axis=0, keepdims=True
        )
        return grad_mixed, delta

    def soften(at, delta):
        probs = probs_ref[0, order(at)].astype(f32)
        small_scores[at % 2] = (probs * (grad_probs[at % 2] - delta)).astype(bf16)

    def mix(at, grad_mixed):
        rows = rows_of(at)
        query = qkv_ref[0, 0, rows]
        key = qkv_ref[0, 1, rows]
        grad_scores = small_scores[at % 2]
        grad_value = nt(grad_mixed, probs_ref[0, order(at)])
        grad_key = nt(query, grad_scores) * LN2
        both = nn(jnp.concatenate([key, hot], axis=0) if at < own_heads else key, grad_scores)
        grad_qkv[0, rows] = (both[0:HEAD_DIM] * HEAD_DIM**-0.5).astype(bf16)
        grad_qkv[1, rows] = grad_key.astype(bf16)
        grad_qkv[2, rows] = grad_value.astype(bf16)
        if at < own_heads:
            levels_total[at] += nt(both[HEAD_DIM:].astype(bf16), back_hot)

    point(0)
    kept = [lead(0)]
    for at in range(heads):
        if at + 1 < heads:
            kept.append(lead(at + 1))
        soften(at, kept[at][1])
        if at > 0:
            mix(at - 1, kept[at - 1][0])
        if at % 3 == 2 and at + 1 < heads:
            point(1 + at // 3)
    mix(heads - 1, kept[-1][0])
    point(4)
    tokens = x_ref[...].astype(f32)
    xhat, inverse = norm_parts(tokens)
    low = (xhat * rows_ref[0:1, :] + rows_ref[1:2, :]).astype(bf16)
    mine = pl.ds(pl.multiple_of(place * own, own), own)
    stacked = jnp.concatenate([grad_qkv[kind, mine] for kind in range(3)], axis=0)
    pack_total[0 : 3 * own, :] += nn(stacked, low)
    pack_total[3 * own :, :] += nn(context_ref[0, mine], grad_low)
    wide = stacked.astype(f32)
    folded = wide[:, 0:BLOCK]
    for at in range(1, width // BLOCK):
        folded = folded + wide[:, at * BLOCK : (at + 1) * BLOCK]
    bias_total[...] += folded
    grad_normed = tn(grad_qkv[0], weights[0].reshape(model, model))
    for kind in (1, 2):
        grad_normed = grad_normed + tn(grad_qkv[kind], weights[kind].reshape(model, model))
    grad_total = grad_hidden + norm_grad(grad_normed, xhat, inverse, rows_ref[0:1, :])
    grad_input_ref[...] = grad_total.astype(bf16)
    sums_ref[0:1, :] += jnp.sum(grad_normed * xhat, axis=0, keepdims=True)
    sums_ref[1:2, :] += jnp.sum(grad_normed, axis=0, keepdims=True)

    @pl.when(page == pages - 1)
    def _():
        grad_pack_ref[...] = pack_total[...].astype(bf16)
        row = jnp.sum(bias_total[...].T, axis=0, keepdims=True)
        sums_ref[2:3, 0:own] = row[:, 0:own]
        sums_ref[3:4, 0:own] = row[:, 2 * own : 3 * own]
        lane = lax.broadcasted_iota(jnp.int32, (bins, 2 * bins), 1)
        for one in range(own_heads):
            for kind in range(2):
                block = levels_total[one, kind * bins : (kind + 1) * bins, :]
                inside = lane >= bins if kind else lane < bins
                rolled = pltpu.roll(jnp.where(inside, block, 0.0), kind * bins, 1, stride=1, stride_axis=0)
                at = (kind * own_heads + one) * 2 * bins
                sums_ref[4:5, at : at + 2 * bins] = jnp.sum(rolled, axis=0, keepdims=True)
        for copy in stores:
            copy.start()
        drain()
        for copy in stores:
            copy.wait()


def reduce_kernel(bits, part_ref, small_one_ref, small_two_ref, sum_ref, sum_one_ref, sum_two_ref, *scratch):
    enter, begin, ticks, drain, small_begin, small_step = reduce_steps(
        bits, (part_ref,), (sum_ref,), (small_one_ref, small_two_ref), scratch
    )
    enter()
    begin()
    small_begin()
    for at, act in enumerate(ticks):
        act()
        if at < 3:
            small_step(at)
    for bit in range(3, bits):
        small_step(bit)
    drain()
    sum_one_ref[...] = scratch[8][0, 2 * bits - 1]
    sum_two_ref[...] = scratch[8][1, 2 * bits - 1]


def finish_kernel(pack_ref, up_ref, down_ref, one_ref, two_ref, qkv, qv_bias, out, up, down, tables, rows):
    own = out.shape[0]
    bins = tables.shape[-1]
    for kind in range(3):
        qkv[kind] = pack_ref[kind * own : (kind + 1) * own, :].astype(f32)
    out[...] = pack_ref[3 * own :, :].astype(f32)
    up[...] = up_ref[...].astype(f32)
    down[...] = down_ref[...].astype(f32)
    qv_bias[...] = one_ref[2:4, 0:own]
    rows[0:2, :] = one_ref[0:2, :]
    rows[2:7, :] = two_ref[0:5, :]
    rows[7:8, :] = one_ref[7:8, :]
    m = lax.broadcasted_iota(jnp.int32, (2 * bins, bins), 0)
    level = lax.broadcasted_iota(jnp.int32, (2 * bins, bins), 1)
    pick = jnp.where(jnp.clip(m - (bins - 1), -(bins // 2), bins // 2 - 1) + bins // 2 == level, 1.0, 0.0)
    own_heads = tables.shape[0]
    for one in range(own_heads):
        for kind in range(2):
            at = (kind * own_heads + one) * 2 * bins
            line = jnp.broadcast_to(one_ref[4:5, at : at + 2 * bins], (8, 2 * bins))
            folded = lax.dot_general(
                line, pick, (((1,), (0,)), ((), ())), precision=lax.Precision.HIGHEST, preferred_element_type=f32
            )
            tables[one, kind : kind + 1, :] = folded[0:1]


ANYWHERE = pl.BlockSpec(memory_space=pl.ANY)
IN_VMEM = pl.BlockSpec(memory_space=pltpu.VMEM)


def whole(shape):
    return pl.BlockSpec(shape, lambda *_: (0,) * len(shape), pipeline_mode=pl.Buffered(1))


def page_rows(model):
    return pl.BlockSpec((PAGE, model), lambda p, *_: (p, 0))


def page_block(*shape):
    return pl.BlockSpec((1,) + shape, lambda p, *_: (p,) + (0,) * len(shape))


def params(collective_id=None):
    if collective_id is None:
        return pltpu.CompilerParams(vmem_limit_bytes=VMEM_LIMIT)
    return pltpu.CompilerParams(
        vmem_limit_bytes=VMEM_LIMIT, collective_id=collective_id, has_side_effects=True
    )


def attention_forward(shards, counts, inputs, keep, box_x, box_y, vectors, bias, tables, qkv_weight, out_weight, up, down):
    rows_here, model = inputs.shape
    pages = rows_here // PAGE
    own = model // shards
    bins = tables.shape[-1]
    heads = model // HEAD_DIM
    gathered = jax.ShapeDtypeStruct((shards,) + up.shape, bf16)
    return pl.pallas_call(
        functools.partial(forward_kernel, shards),
        out_shape=(
            jax.ShapeDtypeStruct((pages, 3, model, PAGE), bf16),
            jax.ShapeDtypeStruct((pages, heads, PAGE, PAGE), bf16),
            jax.ShapeDtypeStruct((pages, heads, 1, PAGE), f32),
            jax.ShapeDtypeStruct((pages, model, PAGE), bf16),
            jax.ShapeDtypeStruct((rows_here, model), f32),
            gathered,
            gathered,
            gathered,
            jax.ShapeDtypeStruct((8, model), f32),
            jax.ShapeDtypeStruct((shards, 8, model), f32),
        ),
        grid_spec=pltpu.PrefetchScalarGridSpec(
            num_scalar_prefetch=1,
            grid=(pages,),
            in_specs=[page_rows(model)]
            + [page_block(1, PAGE)] * 3
            + [whole(vector.shape) for vector in vectors]
            + [whole(bias.shape), whole(tables.shape)]
            + [ANYWHERE] * 4,
            out_specs=(
                page_block(3, model, PAGE),
                page_block(heads, PAGE, PAGE),
                page_block(heads, 1, PAGE),
                page_block(model, PAGE),
                page_rows(model),
                ANYWHERE,
                ANYWHERE,
                ANYWHERE,
                whole((8, model)),
                ANYWHERE,
            ),
            scratch_shapes=[
                pltpu.VMEM((8, model), f32),
                pltpu.VMEM((4, shards, own, model), bf16),
                pltpu.SemaphoreType.DMA((14,)),
                pltpu.VMEM((3,) + up.shape, bf16),
                pltpu.VMEM((shards,) + bias.shape, f32),
                pltpu.VMEM((shards,) + tables.shape, f32),
            ]
            + gather_semaphores(3, shards)
            + [
                pltpu.VMEM((2, model, 128), f32),
                pltpu.VMEM((heads * 2 * bins, 2 * bins), bf16),
                pltpu.VMEM((heads * 2 * bins, PAGE), bf16),
                pltpu.VMEM((2, PAGE, PAGE), f32),
            ],
        ),
        compiler_params=params(1),
        name="attention_forward",
    )(counts, inputs, keep, box_x, box_y, *vectors, bias, tables, qkv_weight, out_weight, up, down)


def feed_forward(counts, place, hidden, cotangent, rows, rows_all, up_all, down_all):
    rows_here, model = hidden.shape
    pages = rows_here // PAGE
    shards, _, hidden_units = up_all.shape
    return pl.pallas_call(
        mlp_kernel,
        out_shape=(
            jax.ShapeDtypeStruct((rows_here, model), bf16),
            jax.ShapeDtypeStruct((rows_here, model), f32),
            jax.ShapeDtypeStruct((model, hidden_units), bf16),
            jax.ShapeDtypeStruct((hidden_units, model), bf16),
            jax.ShapeDtypeStruct((8, model), f32),
        ),
        grid_spec=pltpu.PrefetchScalarGridSpec(
            num_scalar_prefetch=2,
            grid=(pages,),
            in_specs=[
                page_rows(model),
                page_rows(model),
                whole(rows.shape),
                whole(rows_all.shape),
                whole((shards, model, hidden_units)),
                whole((shards, hidden_units, model)),
            ],
            out_specs=(
                page_rows(model),
                page_rows(model),
                whole((model, hidden_units)),
                whole((hidden_units, model)),
                whole((8, model)),
            ),
            scratch_shapes=[
                pltpu.VMEM((model, hidden_units), f32),
                pltpu.VMEM((hidden_units, model), f32),
                pltpu.VMEM((PAGE, model), bf16),
                pltpu.VMEM((PAGE, model), bf16),
                pltpu.VMEM((PAGE, model), f32),
                pltpu.VMEM((PAGE, model), f32),
                pltpu.VMEM((shards, PAGE, hidden_units), bf16),
                pltpu.VMEM((shards, PAGE, hidden_units), bf16),
                pltpu.VMEM((2, PAGE, hidden_units), f32),
                pltpu.VMEM((2, PAGE, hidden_units), f32),
            ],
        ),
        compiler_params=params(),
        name="feed_forward",
    )(counts, place, hidden, cotangent, rows, rows_all, up_all, down_all)


def attention_backward(
    shards,
    devices,
    inputs,
    box_x,
    box_y,
    rows,
    grad_hidden,
    qkv,
    probs,
    inverse,
    context,
    gathered,
    part_up,
    part_down,
):
    rows_here, model = inputs.shape
    pages, heads = probs.shape[:2]
    own = model // shards
    bins = 64
    bits = devices.bit_length() - 1
    return pl.pallas_call(
        functools.partial(backward_kernel, shards, bits, pages),
        out_shape=(
            jax.ShapeDtypeStruct((rows_here, model), bf16),
            jax.ShapeDtypeStruct((4 * own, model), bf16),
            jax.ShapeDtypeStruct((8, model), f32),
            jax.ShapeDtypeStruct(part_up.shape, bf16),
            jax.ShapeDtypeStruct(part_down.shape, bf16),
        ),
        grid_spec=pltpu.PrefetchScalarGridSpec(
            num_scalar_prefetch=0,
            grid=(pages,),
            in_specs=[page_rows(model)]
            + [page_block(1, PAGE)] * 2
            + [whole(rows.shape)]
            + [
                page_rows(model),
                page_block(3, model, PAGE),
                page_block(heads, PAGE, PAGE),
                page_block(heads, 1, PAGE),
                page_block(model, PAGE),
                ANYWHERE,
                whole(part_up.shape),
                whole(part_down.shape),
            ],
            out_specs=(
                page_rows(model),
                whole((4 * own, model)),
                whole((8, model)),
                ANYWHERE,
                ANYWHERE,
            ),
            scratch_shapes=[
                pltpu.VMEM((4, shards, own, model), bf16),
                pltpu.SemaphoreType.DMA((6,)),
                pltpu.VMEM((3, model, PAGE), bf16),
                pltpu.VMEM((model, PAGE), f32),
                pltpu.VMEM((2, PAGE, PAGE), f32),
                pltpu.VMEM((2, PAGE, PAGE), bf16),
                pltpu.VMEM((4 * own, model), f32),
                pltpu.VMEM((3 * own, BLOCK), f32),
                pltpu.VMEM((own // HEAD_DIM, 2 * bins, 2 * bins), f32),
                pltpu.VMEM((2,) + part_up.shape, bf16),
            ]
            + reduce_scratch(2, part_up.shape[0], model, bits),
        ),
        compiler_params=params(2),
        name="attention_backward",
    )(
        inputs,
        box_x,
        box_y,
        rows,
        grad_hidden,
        qkv,
        probs,
        inverse,
        context,
        gathered,
        part_up,
        part_down,
    )


def reduce_grads(devices, part, small_one, small_two):
    rows, model = part.shape
    bits = devices.bit_length() - 1
    return pl.pallas_call(
        functools.partial(reduce_kernel, bits),
        out_shape=(jax.ShapeDtypeStruct(part.shape, bf16),)
        + tuple(jax.ShapeDtypeStruct(small.shape, f32) for small in (small_one, small_two)),
        in_specs=[IN_VMEM] * 3,
        out_specs=(IN_VMEM,) * 3,
        scratch_shapes=reduce_scratch(1, rows, model, bits)
        + [
            pltpu.VMEM((2, 2 * bits) + small_one.shape, f32),
            pltpu.SemaphoreType.DMA((2, bits)),
            pltpu.SemaphoreType.DMA((2, bits)),
        ],
        compiler_params=params(3),
        name="reduce_grads",
    )(part, small_one, small_two)


def finish_grads(pack, up, down, small_one, small_two, bins):
    own, model = pack.shape[0] // 4, pack.shape[1]
    return pl.pallas_call(
        finish_kernel,
        out_shape=(
            jax.ShapeDtypeStruct((3, own, model), f32),
            jax.ShapeDtypeStruct((2, own), f32),
            jax.ShapeDtypeStruct((own, model), f32),
            jax.ShapeDtypeStruct(up.shape, f32),
            jax.ShapeDtypeStruct(down.shape, f32),
            jax.ShapeDtypeStruct((own // HEAD_DIM, 2, bins), f32),
            jax.ShapeDtypeStruct(small_one.shape, f32),
        ),
        in_specs=[IN_VMEM] * 5,
        out_specs=(IN_VMEM,) * 7,
        compiler_params=params(),
        name="finish_grads",
    )(pack, up, down, small_one, small_two)


def on_device(
    inputs,
    cotangent,
    counts,
    keep_mask,
    box_x,
    box_y,
    gain_one,
    shift_one,
    w_qkv,
    b_qv,
    w_out,
    b_out,
    gain_two,
    shift_two,
    w_up,
    b_up,
    w_down,
    b_down,
    rel_tables,
    *,
    devices,
):
    rows_here, model = inputs.shape
    pages = rows_here // PAGE
    own_heads, bins = rel_tables.shape[1:]
    own = own_heads * HEAD_DIM
    shards = model // own
    place = lax.axis_index("tensor").astype(jnp.int32).reshape(1)
    paged = lambda array: array.reshape(pages, 1, PAGE)
    keep_mask, box_x, box_y = paged(keep_mask), paged(box_x), paged(box_y)
    vectors = [
        vector.reshape(-1, 128) for vector in (gain_one, shift_one, b_out, gain_two, shift_two, b_down, b_up)
    ]

    qkv, probs, inverse, context, hidden, gathered, up_all, down_all, rows, rows_all = attention_forward(
        shards,
        counts,
        inputs,
        keep_mask,
        box_x,
        box_y,
        vectors,
        b_qv,
        rel_tables.transpose(1, 0, 2),
        w_qkv.transpose(0, 2, 1).reshape(3 * own, model),
        w_out,
        w_up,
        w_down,
    )
    out, grad_hidden, part_up, part_down, small_two = feed_forward(
        counts, place, hidden, cotangent, rows, rows_all, up_all, down_all
    )
    grad_input, part_pack, small_one, grad_up, grad_down = attention_backward(
        shards,
        devices,
        inputs,
        box_x,
        box_y,
        rows,
        grad_hidden,
        qkv,
        probs,
        inverse,
        context,
        gathered,
        part_up,
        part_down,
    )
    grad_pack, small_one, small_two = reduce_grads(devices, part_pack, small_one, small_two)
    grad_qkv, grad_b_qv, grad_w_out, grad_w_up, grad_w_down, grad_tables, sums = finish_grads(
        grad_pack, grad_up, grad_down, small_one, small_two, bins
    )
    return (
        out,
        grad_input,
        grad_qkv.transpose(0, 2, 1),
        grad_b_qv,
        grad_w_out,
        sums[4],
        sums[0],
        sums[1],
        sums[2],
        sums[3],
        grad_w_up,
        sums[6],
        grad_w_down,
        sums[5],
        grad_tables.transpose(1, 0, 2),
    )


def solution(mesh):
    placed = (
        P("dp", None),
        P("dp", None),
        P("dp"),
        P("dp"),
        P("dp"),
        P("dp"),
        P(),
        P(),
        P(None, None, "tensor"),
        P(None, "tensor"),
        P("tensor", None),
        P(),
        P(),
        P(),
        P(None, "tensor"),
        P("tensor"),
        P("tensor", None),
        P(),
        P(None, "tensor", None),
    )
    return jax.shard_map(
        functools.partial(on_device, devices=mesh.shape["dp"]),
        mesh=mesh,
        in_specs=placed,
        out_specs=(
            P("dp", None),
            P("dp", None),
            P(None, None, "tensor"),
            P(None, "tensor"),
            P("tensor", None),
            P(),
            P(),
            P(),
            P(),
            P(),
            P(None, "tensor"),
            P("tensor"),
            P("tensor", None),
            P(),
            P(None, "tensor", None),
        ),
        check_vma=False,
    )
```
